32 devices in a mesh: rep: 2 (over x), space: 16 (over z, y, core).
Axes of the slice: x: 2, y: 2, z: 4, core: 2. Of those that a mesh axis runs over, the one named last changes fastest.
Arguments:
- positions: float32 [15, 16, 32, 128], P(None, None, ('rep', 'space')), parts along dimension 2, may hold values from -1.5 to 1.5
- momenta: float32 [15, 16, 32, 128], P(None, None, ('rep', 'space')), parts along dimension 2, may hold values from -5 to 5
- masses: float32 [15], replicated, may hold values from 1 to 4
- step_size: float32 [1], replicated, may hold values from 0.25 to 0.5
- cycle_frequency: float32 [1], replicated, may hold values from 0.5 to 1
- layer_one: bfloat16 [256, 405], replicated, may hold values from -0.625 to 0.625
- bias_one: float32 [256], replicated, may hold values from -3 to 3
- layer_two: bfloat16 [256, 256], replicated, may hold values from -0.375 to 0.375
- bias_two: float32 [256], replicated, may hold values from -3 to 3
- readout: float32 [256], replicated, may hold values from -1.5 to 1.5
- wavevectors: int32 [3, 4096], replicated, may hold values from -8 to 7
Outputs:
- positions_final: float32 [15, 16, 32, 128], P(None, None, ('rep', 'space')), parts along dimension 2
- momenta_final: float32 [15, 16, 32, 128], P(None, None, ('rep', 'space')), parts along dimension 2
- spectrum: float32 [8192, 480], P(('rep', 'space')), parts along dimension 0
The draws below stay inside these ranges and needn't reach their ends.
There are 2 independent parts, one for each index of `rep`. The reference program is written for one: setup_inputs(seed, part) draws one part's arguments, and reference() takes and returns one part's arrays. A program takes and returns all parts, laid end to end along the dimension named above; an argument that names none is the same for every part. Nothing has to cross between parts.
All inputs are finite; a program needn't handle non-finite values.
Results may differ from the reference program's by a relative error of at most 0.0044.
Values may be sent and summed in bfloat16 or wider, within the bound.
No kernel may reach another device: no remote copies, remote signals or barrier semaphores. Data moves between devices by JAX's collectives and lax.ppermute only.
A program may use at most 64 MiB of HBM per device.

```python
import math
import jax
import jax.numpy as jnp
from jax import lax

COORDS = 15
BEADS = 16
HIDDEN_SIZE = 256
KVEC = 4096
NY = 8
NZ = 16
STEPS = 1
FEATURES = 405
NX = 16


def with_ends(drawn, rng, least, largest):
    place = [jax.random.randint(jax.random.fold_in(rng, axis), (), 0, length) for axis, length in enumerate(drawn.shape)]
    main_axis = drawn.shape.index(max(drawn.shape))
    next_to = place[:main_axis] + [(place[main_axis] + 1) % drawn.shape[main_axis]] + place[main_axis + 1:]
    return drawn.at[tuple(place)].set(least).at[tuple(next_to)].set(largest)


def levels(key, dims, split, least, largest):
    gain, own = 1.0, jax.random.fold_in(key, 6)
    for axis_at, blocks in split:
        steps = jnp.exp(jax.random.uniform(jax.random.fold_in(own, axis_at), (blocks,), jnp.float32, least / len(split), largest / len(split)))
        gain = gain * jnp.repeat(steps, dims[axis_at] // blocks).reshape([-1 if axis == axis_at else 1 for axis in range(len(dims))])
    return gain


def scatter_about(key, extent, width, most, cuts=(), kind=jnp.bfloat16):
    factor_of = levels(key, extent, cuts, -0.22, 0.18) if cuts else 1.0
    values = jax.random.normal(key, extent, jnp.float32) * width * factor_of
    return jnp.minimum(jnp.maximum(values, -most), most).astype(kind)


def setup_inputs(seed: int = 0, part: int = 0) -> dict:
    streams_of = jax.random.split(jax.random.key(seed), 12)
    part_keys = jax.random.split(jax.random.fold_in(streams_of[11], part), 12)
    return {
        "positions": scatter_about(part_keys[0], (COORDS, BEADS, NX, NY * NZ), 0.3, 1.5, ((2, 16),), jnp.float32),
        "momenta": scatter_about(part_keys[1], (COORDS, BEADS, NX, NY * NZ), 1.0, 5.0, ((2, 16),), jnp.float32),
        "masses": jnp.clip(jnp.exp(jax.random.uniform(streams_of[2], (COORDS,), jnp.float32, math.log(1.0), math.log(4.0))), 1.0, 4.0),
        "step_size": jnp.clip(jax.random.uniform(streams_of[3], (1,), jnp.float32, 0.25, 0.5), 0.25, 0.5),
        "cycle_frequency": jnp.clip(jax.random.uniform(streams_of[4], (1,), jnp.float32, 0.5, 1.0), 0.5, 1.0),
        "layer_one": scatter_about(streams_of[5], (HIDDEN_SIZE, FEATURES), (FEATURES // 4) ** -0.5, 0.625),
        "bias_one": scatter_about(streams_of[6], (HIDDEN_SIZE,), 0.5, 3.0, (), jnp.float32),
        "layer_two": scatter_about(streams_of[7], (HIDDEN_SIZE, HIDDEN_SIZE), HIDDEN_SIZE ** -0.5, 0.375),
        "bias_two": scatter_about(streams_of[8], (HIDDEN_SIZE,), 0.5, 3.0, (), jnp.float32),
        "readout": scatter_about(streams_of[9], (HIDDEN_SIZE,), 0.25, 1.5, (), jnp.float32),
        "wavevectors": with_ends(jax.random.randint(streams_of[10], (3, KVEC), -8, 8), jax.random.fold_in(streams_of[10], 1), -8, 7).astype(jnp.int32),
    }


TWO_PI = 6.283185307179586
OFFSETS = [(along_x, along_y, along_z) for along_x in (-1, 0, 1) for along_y in (-1, 0, 1) for along_z in (-1, 0, 1)]

def shift_cells(values, step_y, step_z, depth_z):
    length = values.shape[-1]
    if step_y != 0:
        values = jnp.roll(values, -step_y * depth_z, axis=-1)
    inner = lax.broadcasted_iota(jnp.int32, (length,), 0) % depth_z
    if step_z == 1:
        values = jnp.where(inner == depth_z - 1, jnp.roll(values, depth_z - 1, axis=-1), jnp.roll(values, -1, axis=-1))
    elif step_z == -1:
        values = jnp.where(inner == 0, jnp.roll(values, 1 - depth_z, axis=-1), jnp.roll(values, 1, axis=-1))
    return values

def network(features, layer_one, bias_one, layer_two, bias_two, readout):
    contract_rows = (((0,), (0,)), ((), ()))
    hidden_one = jnp.tanh(jnp.dot(layer_one, features, preferred_element_type=jnp.float32) + bias_one[:, None]).astype(jnp.bfloat16)
    hidden_two = jnp.tanh(jnp.dot(layer_two, hidden_one, preferred_element_type=jnp.float32) + bias_two[:, None])
    back_two = (readout[:, None] * (1.0 - hidden_two * hidden_two)).astype(jnp.bfloat16)
    widened = hidden_one.astype(jnp.float32)
    back_one = lax.dot_general(layer_two, back_two, contract_rows, preferred_element_type=jnp.float32)
    back_one = (back_one * (1.0 - widened * widened)).astype(jnp.bfloat16)
    return lax.dot_general(layer_one, back_one, contract_rows, preferred_element_type=jnp.float32)

def mode_matrix():
    column_j = jnp.arange(BEADS, dtype=jnp.float32)[:, None]
    column_k = jnp.arange(BEADS, dtype=jnp.float32)[None, :]
    angles = TWO_PI * column_j * column_k / BEADS
    halfway = BEADS // 2
    boundary = jnp.cos(angles) / math.sqrt(BEADS)
    cosines = jnp.cos(angles) * math.sqrt(2.0 / BEADS)
    sines = jnp.sin(angles) * math.sqrt(2.0 / BEADS)
    inside = jnp.where(column_k < halfway, cosines, sines)
    return jnp.where((column_k == 0) | (column_k == halfway), boundary, inside)

def cycle_update(positions, momenta, masses, step_size, cycle_frequency):
    highest = lax.Precision.HIGHEST
    matrix = mode_matrix()
    mode_positions = jnp.einsum('jk,cjxs->ckxs', matrix, positions, precision=highest)
    mode_momenta = jnp.einsum('jk,cjxs->ckxs', matrix, momenta, precision=highest)
    order = jnp.arange(BEADS, dtype=jnp.float32)
    frequency = 2.0 * cycle_frequency * jnp.sin(0.5 * TWO_PI * order / BEADS)
    phase = frequency * step_size
    safe_phase = jnp.where(order == 0, 1.0, phase)
    ratio = jnp.where(order == 0, 1.0, jnp.sin(phase) / safe_phase)
    weight_mass = masses[:, None, None, None]
    cosine = jnp.cos(phase)[None, :, None, None]
    drift = (step_size * ratio)[None, :, None, None] / weight_mass
    spring = weight_mass * (frequency * jnp.sin(phase))[None, :, None, None]
    moved = cosine * mode_positions + drift * mode_momenta
    pushed = cosine * mode_momenta - spring * mode_positions
    new_positions = jnp.einsum('jk,ckxs->cjxs', matrix, moved, precision=highest)
    new_momenta = jnp.einsum('jk,ckxs->cjxs', matrix, pushed, precision=highest)
    return (new_positions, new_momenta)

def bead_forces(bead_positions, weights):
    rounded = bead_positions.astype(jnp.bfloat16)
    blocks = [shift_cells(jnp.roll(rounded, -along_x, axis=1), along_y, along_z, NZ) for along_x, along_y, along_z in OFFSETS]
    features = jnp.stack(blocks).reshape(27 * COORDS, -1)
    sensitivity = network(features, weights[0], weights[1], weights[2], weights[3], weights[4])
    sensitivity = sensitivity.reshape(27, COORDS, NX, NY * NZ)
    summed = jnp.zeros((COORDS, NX, NY * NZ), jnp.float32)
    for offset_number, (along_x, along_y, along_z) in enumerate(OFFSETS):
        moved_back = shift_cells(sensitivity[offset_number], -along_y, -along_z, NZ)
        summed = summed + jnp.roll(moved_back, along_x, axis=1)
    return -summed

def all_forces(positions, weights):
    per_bead = jnp.moveaxis(positions, 1, 0)
    result = lax.map(lambda bead: bead_forces(bead, weights), per_bead)
    return jnp.moveaxis(result, 0, 1)

def phase_angles(vectors, flat_cells, extent_x):
    plane_cells = NY * NZ
    cell_x = flat_cells // plane_cells
    remain = flat_cells % plane_cells
    cell_y = remain // NZ
    cell_z = remain % NZ
    whole = extent_x * NY * NZ
    numerator = vectors[0][:, None] * (cell_x * (NY * NZ))[None, :]
    numerator = numerator + vectors[1][:, None] * (cell_y * (extent_x * NZ))[None, :]
    numerator = numerator + vectors[2][:, None] * (cell_z * (extent_x * NY))[None, :]
    return TWO_PI * jnp.mod(numerator, whole).astype(jnp.float32) / whole

def projection_term(vectors, flat_cells, velocity, extent_x):
    angles = phase_angles(vectors, flat_cells, extent_x)
    contract_cells = (((1,), (1,)), ((), ()))
    cosine = jnp.cos(angles).astype(jnp.bfloat16)
    sine = jnp.sin(angles).astype(jnp.bfloat16)
    scale = 1.0 / math.sqrt(extent_x * NY * NZ)
    cos_part = lax.dot_general(cosine, velocity, contract_cells, preferred_element_type=jnp.float32)
    sin_part = lax.dot_general(sine, velocity, contract_cells, preferred_element_type=jnp.float32)
    return jnp.concatenate([cos_part, sin_part], axis=1) * scale

def reference(positions, momenta, masses, step_size, cycle_frequency, layer_one, bias_one, layer_two, bias_two, readout, wavevectors):
    weights = (layer_one, bias_one, layer_two, bias_two, readout)
    forces = all_forces(positions, weights)
    for repeat in range(STEPS):
        momenta = momenta + 0.5 * step_size * forces
        positions, momenta = cycle_update(positions, momenta, masses, step_size, cycle_frequency)
        forces = all_forces(positions, weights)
        momenta = momenta + 0.5 * step_size * forces
    mode_momenta = jnp.einsum('jk,cjxs->ckxs', mode_matrix(), momenta, precision=lax.Precision.HIGHEST)
    velocity = (mode_momenta / masses[:, None, None, None]).astype(jnp.bfloat16).reshape(COORDS * BEADS, -1)
    flat_cells = jnp.arange(NX * NY * NZ, dtype=jnp.int32)
    grouped = jnp.transpose(wavevectors.reshape(3, KVEC // 128, 128), (1, 0, 2))
    blocks = lax.map(lambda group: projection_term(group, flat_cells, velocity, NX), grouped)
    spectrum = blocks.reshape(KVEC, 2 * BEADS * COORDS)
    return (positions, momenta, spectrum)
```

```python
import functools
import math

import jax
import jax.numpy as jnp
import numpy as np
from jax import lax
from jax.experimental import pallas as pl
from jax.experimental.pallas import tpu as pltpu
from jax.sharding import PartitionSpec as P

NY = 8
NZ = 16
CELLS = NY * NZ
PAD = 16
SHIFTS = [(b, d) for b in (-1, 0, 1) for d in (-1, 0, 1)]
HIGHEST = lax.Precision.HIGHEST
TWO_PI = 6.283185307179586
VMEM = pl.BlockSpec(memory_space=pltpu.VMEM)


def roll(values, amount):
    amount = amount % CELLS
    return values if amount == 0 else pltpu.roll(values, amount, 1)


def shift_y(values, step):
    return roll(values, -step * NZ)


def shift_z(values, step, inner):
    if step == 0:
        return values
    edge = NZ - 1 if step == 1 else 0
    return jnp.where(inner == edge, roll(values, step * (NZ - 1)), roll(values, -step))


def z_index(rows):
    return lax.broadcasted_iota(jnp.int32, (rows, CELLS), 1) % NZ


def prepare_kernel(coords, beads, q_ref, out_ref):
    empty = jnp.zeros((PAD - coords, CELLS), jnp.float32)
    for j in range(beads):
        rows = q_ref[pl.ds(j, coords, stride=beads), :]
        out_ref[j * PAD : (j + 1) * PAD, :] = jnp.concatenate([rows, empty]).astype(jnp.bfloat16)


def force_kernel(
    beads, group, outer2_ref, outer_ref, own_ref, inner_ref, forward_ref, backward_ref,
    two_ref, two_t_ref, vectors_ref, kept_ref, sent_ref, features
):
    block = 9 * PAD
    inner_z = z_index(beads * PAD)
    for place, ref in enumerate((outer2_ref, outer_ref, own_ref, inner_ref)):
        plane = ref[...].astype(jnp.float32)
        along = {d: shift_z(plane, d, inner_z) for d in (-1, 0, 1)}
        for o, (b, d) in enumerate(SHIFTS):
            moved = shift_y(along[d], b).astype(jnp.bfloat16)
            top = place * block + o * PAD
            for j in range(beads):
                features[top : top + PAD, j * CELLS : (j + 1) * CELLS] = moved[j * PAD : (j + 1) * PAD]
    bias_one = vectors_ref[:, 0:1]
    bias_two = vectors_ref[:, 1:2]
    readout = vectors_ref[:, 2:3]
    dot = functools.partial(jnp.dot, preferred_element_type=jnp.float32)
    inner_z = z_index(PAD)

    def back_one(top, columns):
        hidden = dot(forward_ref[...], features[top : top + 3 * block, columns])
        hidden = jnp.tanh(hidden + bias_one).astype(jnp.bfloat16)
        second = jnp.tanh(dot(two_ref[...], hidden) + bias_two)
        back = (readout * (1.0 - second * second)).astype(jnp.bfloat16)
        widened = hidden.astype(jnp.float32)
        return (dot(two_t_ref[...], back) * (1.0 - widened * widened)).astype(jnp.bfloat16)

    def gathered(sums, at):
        total = None
        for d in (-1, 0, 1):
            part = None
            for b in (-1, 0, 1):
                o = (b + 1) * 3 + d + 1
                moved = shift_y(sums[o * PAD : (o + 1) * PAD, at * CELLS : (at + 1) * CELLS], -b)
                part = moved if part is None else part + moved
            part = shift_z(part, -d, inner_z)
            total = part if total is None else total + part
        return total

    for first in range(0, beads, group):
        columns = slice(first * CELLS, (first + group) * CELLS)
        back_outer = back_one(0, columns)
        back_own = back_one(block, columns)
        kept = dot(backward_ref[block : 2 * block], back_own) + dot(backward_ref[2 * block :], back_outer)
        sent = dot(backward_ref[2 * block :], back_own)
        for at in range(group):
            rows = slice((first + at) * PAD, (first + at + 1) * PAD)
            kept_ref[rows, :] = gathered(kept, at)
            sent_ref[rows, :] = gathered(sent, at)


def update_kernel(
    half_ref, q_ref, p_ref, kept_ref, came_ref, modes_ref, modes_t_ref, padded_ref, padded_t_ref,
    table_ref, q_out, rounded_out, pushed_out
):
    dot = functools.partial(jnp.dot, precision=HIGHEST, preferred_element_type=jnp.float32)
    mode_q = dot(modes_t_ref[...], q_ref[...])
    mode_p = dot(modes_t_ref[...], p_ref[...])
    mode_p = mode_p - half_ref[0] * dot(padded_t_ref[...], kept_ref[...] + came_ref[...])
    cosine, drift, spring = (table_ref[:, i : i + 1] for i in range(3))
    moved = cosine * mode_q + drift * mode_p
    pushed_out[...] = cosine * mode_p - spring * mode_q
    q_out[...] = dot(modes_ref[...], moved)
    rounded_out[...] = dot(padded_ref[...], moved).astype(jnp.bfloat16)


def finish_kernel(
    half_ref, pushed_ref, kept_ref, came_ref, modes_ref, padded_t_ref, table_ref, p_out, velocity_out
):
    dot = functools.partial(jnp.dot, precision=HIGHEST, preferred_element_type=jnp.float32)
    mode_p = pushed_ref[...] - half_ref[0] * dot(padded_t_ref[...], kept_ref[...] + came_ref[...])
    velocity_out[...] = (mode_p / table_ref[:, 3:4]).astype(jnp.bfloat16)
    p_out[...] = dot(modes_ref[...], mode_p)


def project_kernel(scale, velocity_ref, planes_ref, cells_ref, out_ref):
    count, fields, _ = velocity_ref.shape
    over_lanes = (((1,), (1,)), ((), ()))
    cos_cell, sin_cell = cells_ref[0], cells_ref[1]
    cos_sum = sin_sum = 0.0
    for i in range(count):
        cos_plane = planes_ref[0, :, i : i + 1]
        sin_plane = planes_ref[1, :, i : i + 1]
        cosine = (cos_plane * cos_cell - sin_plane * sin_cell).astype(jnp.bfloat16)
        sine = (sin_plane * cos_cell + cos_plane * sin_cell).astype(jnp.bfloat16)
        block = velocity_ref[i]
        cos_sum += lax.dot_general(cosine, block, over_lanes, preferred_element_type=jnp.float32)
        sin_sum += lax.dot_general(sine, block, over_lanes, preferred_element_type=jnp.float32)
    out_ref[:, :fields] = cos_sum * scale
    out_ref[:, fields:] = sin_sum * scale


def mode_matrices(coords, beads):
    j = np.arange(beads)[:, None]
    k = np.arange(beads)[None, :]
    angles = 2.0 * np.pi * ((j * k) % beads) / beads
    edge = np.cos(angles) / math.sqrt(beads)
    inside = np.where(k < beads // 2, np.cos(angles), np.sin(angles)) * math.sqrt(2.0 / beads)
    matrix = np.where((k == 0) | (k == beads // 2), edge, inside)
    modes = np.einsum("ab,jk->ajbk", np.eye(coords), matrix).reshape(coords * beads, coords * beads)
    padded = np.einsum("ab,jk->jabk", np.eye(PAD, coords), matrix).reshape(beads * PAD, coords * beads)
    return modes.astype(np.float32), padded.astype(np.float32)


def trig_tables(vectors, planes_at, extent_x):
    whole = extent_x * CELLS
    cell = lax.broadcasted_iota(jnp.int32, (1, CELLS), 1)
    along = vectors[1][:, None] * (cell // NZ * (extent_x * NZ))
    along = along + vectors[2][:, None] * (cell % NZ * (extent_x * NY))
    across = vectors[0][:, None] * (planes_at[None, :] * CELLS)

    def pair(numerator):
        angle = TWO_PI * jnp.mod(numerator, whole).astype(jnp.float32) / whole
        return jnp.stack([jnp.cos(angle), jnp.sin(angle)])

    return pair(across), pair(along)


def update_table(masses, step_size, cycle_frequency, beads):
    order = jnp.arange(beads, dtype=jnp.float32)
    frequency = 2.0 * cycle_frequency * jnp.sin(0.5 * TWO_PI * order / beads)
    phase = frequency * step_size
    ratio = jnp.where(order == 0, 1.0, jnp.sin(phase) / jnp.where(order == 0, 1.0, phase))
    mass = masses[:, None]
    columns = [
        jnp.broadcast_to(jnp.cos(phase)[None, :], (masses.shape[0], beads)),
        (step_size * ratio)[None, :] / mass,
        mass * (frequency * jnp.sin(phase))[None, :],
        jnp.broadcast_to(mass, (masses.shape[0], beads)),
    ]
    return jnp.stack(columns, axis=-1).reshape(masses.shape[0] * beads, len(columns))


def swap(value, distance):
    return lax.ppermute(value, "space", [(i, i ^ distance) for i in range(lax.axis_size("space"))])


def neighbour_planes(plane):
    count = lax.axis_size("space")
    step = [1 if i % 2 else -1 for i in range(count)]
    outer = lax.ppermute(plane, "space", [(i, (i + step[i]) % count) for i in range(count)])
    outer2 = lax.ppermute(plane, "space", [(i, (i - 2 * step[i]) % count) for i in range(count)])
    return outer2, outer, plane, swap(plane, 1)


def gather_planes(velocity):
    count = lax.axis_size("space")
    held, at = velocity[None], np.zeros((1,), np.int32)
    distance = count // 2
    while distance:
        held = jnp.concatenate([held, swap(held, distance)])
        at = np.concatenate([at, at ^ distance])
        distance //= 2
    return held, lax.axis_index("space") ^ jnp.asarray(at)


def on_device(
    positions, momenta, masses, step_size, cycle_frequency,
    layer_one, bias_one, layer_two, bias_two, readout, wavevectors
):
    coords, beads, planes, cells = positions.shape
    devices = lax.axis_size("space")
    assert planes == 1 and cells == CELLS and devices & (devices - 1) == 0 and devices > 1
    rows = coords * beads
    f32, bf16 = jnp.float32, jnp.bfloat16
    shape = jax.ShapeDtypeStruct
    q = positions.reshape(rows, CELLS)
    p = momenta.reshape(rows, CELLS)
    rounded = pl.pallas_call(
        functools.partial(prepare_kernel, coords, beads),
        out_shape=shape((beads * PAD, CELLS), bf16), in_specs=[VMEM], out_specs=VMEM,
    )(q)

    odd = lax.axis_index("space") % 2
    hidden = layer_one.shape[0]
    by_offset = layer_one.T.reshape(3, 9, coords, hidden)
    by_offset = jnp.pad(by_offset, ((0, 0), (0, 0), (0, PAD - coords), (0, 0)))
    by_offset = jnp.where(odd == 1, by_offset[::-1], by_offset)
    backward = by_offset.reshape(27 * PAD, hidden)
    vectors = jnp.stack([bias_one, bias_two, readout], axis=1)
    weights = (backward.T, backward, layer_two, layer_two.T, vectors)

    def forces(plane):
        both = shape((beads * PAD, CELLS), f32)
        kept, sent = pl.pallas_call(
            functools.partial(force_kernel, beads, 4),
            out_shape=(both, both), in_specs=[VMEM] * 9, out_specs=(VMEM, VMEM),
            scratch_shapes=[pltpu.VMEM((36 * PAD, beads * CELLS), bf16)],
        )(*neighbour_planes(plane), *weights)
        return kept, swap(sent, 1)

    modes, padded = mode_matrices(coords, beads)
    table = update_table(masses, step_size, cycle_frequency, beads)
    half = 0.5 * step_size
    scalar = pl.BlockSpec(memory_space=pltpu.SMEM)
    q_new, rounded, pushed = pl.pallas_call(
        update_kernel,
        out_shape=(shape((rows, CELLS), f32), shape((beads * PAD, CELLS), bf16), shape((rows, CELLS), f32)),
        in_specs=[scalar] + [VMEM] * 9, out_specs=(VMEM, VMEM, VMEM),
    )(half, q, p, *forces(rounded), modes, modes.T, padded, padded.T, table)
    p_new, velocity = pl.pallas_call(
        finish_kernel,
        out_shape=(shape((rows, CELLS), f32), shape((rows, CELLS), bf16)),
        in_specs=[scalar] + [VMEM] * 6, out_specs=(VMEM, VMEM),
    )(half, pushed, *forces(rounded), modes, padded.T, table)

    share = wavevectors.shape[1] // devices
    own_vectors = lax.dynamic_slice_in_dim(wavevectors, lax.axis_index("space") * share, share, 1)
    fragment, planes_at = gather_planes(velocity)
    across, along = trig_tables(own_vectors, planes_at, devices)
    spectrum = pl.pallas_call(
        functools.partial(project_kernel, 1.0 / math.sqrt(devices * CELLS)),
        out_shape=shape((share, 2 * rows), f32), in_specs=[VMEM] * 3, out_specs=VMEM,
    )(fragment, across, along)
    return q_new.reshape(positions.shape), p_new.reshape(momenta.shape), spectrum


def solution(mesh):
    field = P(None, None, ("rep", "space"), None)
    return jax.shard_map(
        on_device,
        mesh=mesh,
        in_specs=(field, field) + (P(),) * 9,
        out_specs=(field, field, P(("rep", "space"), None)),
        check_vma=False,
    )
```

```python
import functools
import math

import jax
import jax.numpy as jnp
import numpy as np
from jax import lax
from jax.experimental import pallas as pl
from jax.experimental.pallas import tpu as pltpu
from jax.sharding import PartitionSpec as P

NY = 8
NZ = 16
CELLS = NY * NZ
PAD = 16
SHIFTS = [(b, d) for b in (-1, 0, 1) for d in (-1, 0, 1)]
HIGHEST = lax.Precision.HIGHEST
TWO_PI = 6.283185307179586
VMEM = pl.BlockSpec(memory_space=pltpu.VMEM)


call = functools.partial(pl.pallas_call, compiler_params=pltpu.CompilerParams(vmem_limit_bytes=16 << 20))


def roll(values, amount):
    amount = amount % CELLS
    return values if amount == 0 else pltpu.roll(values, amount, 1)


def shift_y(values, step):
    return roll(values, -step * NZ)


def shift_z(values, step, inner):
    if step == 0:
        return values
    edge = NZ - 1 if step == 1 else 0
    return jnp.where(inner == edge, roll(values, step * (NZ - 1)), roll(values, -step))


def z_index(rows):
    return lax.broadcasted_iota(jnp.int32, (rows, CELLS), 1) % NZ


def setup_kernel(coords, odd_ref, one_ref, two_ref, vectors_ref, forward_ref, backward_ref, two_t_ref, columns_ref, rows):
    hidden = one_ref.shape[1]
    rows[: one_ref.shape[0], :] = one_ref[...].astype(jnp.float32)
    rows[one_ref.shape[0] :, :] = jnp.zeros((rows.shape[0] - one_ref.shape[0], hidden), jnp.float32)
    real = lax.broadcasted_iota(jnp.int32, (PAD, hidden), 0) < coords
    for along_x in range(3):
        for o in range(9):
            even, odd = ((a * 9 + o) * coords for a in (along_x, 2 - along_x))
            taken = rows[even : even + PAD, :]
            if odd != even:
                taken = jnp.where(odd_ref[0] == 1, rows[odd : odd + PAD, :], taken)
            top = (along_x * 9 + o) * PAD
            backward_ref[top : top + PAD, :] = jnp.where(real, taken, 0.0).astype(jnp.bfloat16)
    forward_ref[...] = backward_ref[...].astype(jnp.float32).T.astype(jnp.bfloat16)
    two_t_ref[...] = two_ref[...].astype(jnp.float32).T.astype(jnp.bfloat16)
    columns_ref[...] = vectors_ref[...].T


def force_kernel(
    coords, beads, group, outer2_ref, outer_ref, own_ref, inner_ref, forward_ref, backward_ref,
    two_ref, two_t_ref, vectors_ref, kept_ref, sent_ref, features, stage
):
    block = 9 * PAD
    inner_z = z_index(beads * PAD)
    empty = jnp.zeros((PAD - coords, CELLS), jnp.float32)
    for place, ref in enumerate((outer2_ref, outer_ref, own_ref, inner_ref)):
        stage[...] = ref[...].astype(jnp.float32)
        pieces = []
        for j in range(beads):
            pieces += [stage[pl.ds(j, coords, stride=beads), :], empty]
        plane = jnp.concatenate(pieces)
        along = {d: shift_z(plane, d, inner_z) for d in (-1, 0, 1)}
        for o, (b, d) in enumerate(SHIFTS):
            moved = shift_y(along[d], b).astype(jnp.bfloat16)
            top = place * block + o * PAD
            for j in range(beads):
                features[top : top + PAD, j * CELLS : (j + 1) * CELLS] = moved[j * PAD : (j + 1) * PAD]
    bias_one = vectors_ref[:, 0:1]
    bias_two = vectors_ref[:, 1:2]
    readout = vectors_ref[:, 2:3]
    dot = functools.partial(jnp.dot, preferred_element_type=jnp.float32)
    inner_z = z_index(PAD)

    def back_one(top, columns):
        hidden = dot(forward_ref[...], features[top : top + 3 * block, columns])
        hidden = jnp.tanh(hidden + bias_one).astype(jnp.bfloat16)
        second = jnp.tanh(dot(two_ref[...], hidden) + bias_two)
        back = (readout * (1.0 - second * second)).astype(jnp.bfloat16)
        widened = hidden.astype(jnp.float32)
        return (dot(two_t_ref[...], back) * (1.0 - widened * widened)).astype(jnp.bfloat16)

    def gathered(sums, at):
        total = None
        for d in (-1, 0, 1):
            part = None
            for b in (-1, 0, 1):
                o = (b + 1) * 3 + d + 1
                moved = shift_y(sums[o * PAD : (o + 1) * PAD, at * CELLS : (at + 1) * CELLS], -b)
                part = moved if part is None else part + moved
            part = shift_z(part, -d, inner_z)
            total = part if total is None else total + part
        return total

    for first in range(0, beads, group):
        columns = slice(first * CELLS, (first + group) * CELLS)
        back_outer = back_one(0, columns)
        back_own = back_one(block, columns)
        kept = dot(backward_ref[block : 2 * block], back_own) + dot(backward_ref[2 * block :], back_outer)
        sent = dot(backward_ref[2 * block :], back_own)
        for at in range(group):
            rows = pl.ds(first + at, coords, stride=beads)
            kept_ref[rows, :] = gathered(kept, at)[:coords]
            sent_ref[rows, :] = gathered(sent, at)[:coords]


def update_kernel(
    half_ref, q_ref, p_ref, kept_ref, came_ref, modes_ref, modes_t_ref, table_ref,
    q_out, rounded_out, p_out, pushed_out
):
    dot = functools.partial(jnp.dot, precision=HIGHEST, preferred_element_type=jnp.float32)
    kicked = p_ref[...] - half_ref[0] * (kept_ref[...] + came_ref[...])
    mode = dot(modes_t_ref[...], jnp.concatenate([q_ref[...], kicked], axis=1))
    mode_q, mode_p = mode[:, :CELLS], mode[:, CELLS:]
    cosine, drift, spring = (table_ref[:, i : i + 1] for i in range(3))
    moved = cosine * mode_q + drift * mode_p
    pushed = cosine * mode_p - spring * mode_q
    pushed_out[...] = pushed
    result = dot(modes_ref[...], jnp.concatenate([moved, pushed], axis=1))
    q_out[...] = result[:, :CELLS]
    rounded_out[...] = result[:, :CELLS].astype(jnp.bfloat16)
    p_out[...] = result[:, CELLS:]


def finish_kernel(half_ref, p_ref, pushed_ref, kept_ref, came_ref, modes_t_ref, table_ref, p_out, velocity_out):
    kick = half_ref[0] * (kept_ref[...] + came_ref[...])
    p_out[...] = p_ref[...] - kick
    mode_p = pushed_ref[...] - jnp.dot(modes_t_ref[...], kick, precision=HIGHEST, preferred_element_type=jnp.float32)
    velocity_out[...] = (mode_p / table_ref[:, 3:4]).astype(jnp.bfloat16)


def project_kernel(scale, velocity_ref, planes_ref, cells_ref, out_ref):
    count, fields, _ = velocity_ref.shape
    dot = functools.partial(jnp.dot, preferred_element_type=jnp.float32)
    cos_cell, sin_cell = cells_ref[0], cells_ref[1]

    def trig(i):
        cos_plane, sin_plane = planes_ref[0, i : i + 1, :], planes_ref[1, i : i + 1, :]
        cosine = cos_plane * cos_cell - sin_plane * sin_cell
        sine = sin_plane * cos_cell + cos_plane * sin_cell
        return cosine.astype(jnp.bfloat16), sine.astype(jnp.bfloat16)

    cos_sum = sin_sum = 0.0
    for i in range(0, count, 2):
        (cos_0, sin_0), (cos_1, sin_1) = trig(i), trig(i + 1)
        block = jnp.concatenate([velocity_ref[i], velocity_ref[i + 1]], axis=1)
        cos_sum += dot(block, jnp.concatenate([cos_0, cos_1]))
        sin_sum += dot(block, jnp.concatenate([sin_0, sin_1]))
    out_ref[:fields, :] = cos_sum * scale
    out_ref[fields:, :] = sin_sum * scale


def mode_matrices(coords, beads):
    j = np.arange(beads)[:, None]
    k = np.arange(beads)[None, :]
    angles = 2.0 * np.pi * ((j * k) % beads) / beads
    edge = np.cos(angles) / math.sqrt(beads)
    inside = np.where(k < beads // 2, np.cos(angles), np.sin(angles)) * math.sqrt(2.0 / beads)
    matrix = np.where((k == 0) | (k == beads // 2), edge, inside)
    modes = np.einsum("ab,jk->ajbk", np.eye(coords), matrix).reshape(coords * beads, coords * beads)
    return modes.astype(np.float32)


def trig_tables(vectors, planes_at, extent_x):
    whole = extent_x * CELLS
    cell = lax.broadcasted_iota(jnp.int32, (CELLS, 1), 0)
    along = vectors[1][None, :] * (cell // NZ * (extent_x * NZ))
    along = along + vectors[2][None, :] * (cell % NZ * (extent_x * NY))
    across = vectors[0][None, :] * (planes_at[:, None] * CELLS)

    def pair(numerator):
        angle = TWO_PI * jnp.mod(numerator, whole).astype(jnp.float32) / whole
        return jnp.stack([jnp.cos(angle), jnp.sin(angle)])

    return pair(across), pair(along)


def update_table(masses, step_size, cycle_frequency, beads):
    order = jnp.arange(beads, dtype=jnp.float32)
    frequency = 2.0 * cycle_frequency * jnp.sin(0.5 * TWO_PI * order / beads)
    phase = frequency * step_size
    ratio = jnp.where(order == 0, 1.0, jnp.sin(phase) / jnp.where(order == 0, 1.0, phase))
    mass = masses[:, None]
    columns = [
        jnp.broadcast_to(jnp.cos(phase)[None, :], (masses.shape[0], beads)),
        (step_size * ratio)[None, :] / mass,
        mass * (frequency * jnp.sin(phase))[None, :],
        jnp.broadcast_to(mass, (masses.shape[0], beads)),
    ]
    return jnp.stack(columns, axis=-1).reshape(masses.shape[0] * beads, len(columns))


def swap(value, distance):
    return lax.ppermute(value, "space", [(i, i ^ distance) for i in range(lax.axis_size("space"))])


def neighbour_planes(plane):
    count = lax.axis_size("space")
    step = [1 if i % 2 else -1 for i in range(count)]
    outer = lax.ppermute(plane, "space", [(i, (i + step[i]) % count) for i in range(count)])
    outer2 = lax.ppermute(plane, "space", [(i, (i - 2 * step[i]) % count) for i in range(count)])
    return outer2, outer, plane, swap(plane, 1)


def gather_planes(velocity):
    count = lax.axis_size("space")
    held, at = velocity[None], np.zeros((1,), np.int32)
    distance = count // 2
    while distance:
        held = jnp.concatenate([held, swap(held, distance)])
        at = np.concatenate([at, at ^ distance])
        distance //= 2
    return held, lax.axis_index("space") ^ jnp.asarray(at)


def on_device(
    positions, momenta, masses, step_size, cycle_frequency,
    layer_one, bias_one, layer_two, bias_two, readout, wavevectors
):
    coords, beads, planes, cells = positions.shape
    devices = lax.axis_size("space")
    assert planes == 1 and cells == CELLS and devices & (devices - 1) == 0 and devices > 1
    rows = coords * beads
    f32, bf16 = jnp.float32, jnp.bfloat16
    shape = jax.ShapeDtypeStruct
    q = positions.reshape(rows, CELLS)
    p = momenta.reshape(rows, CELLS)
    scalar = pl.BlockSpec(memory_space=pltpu.SMEM)
    rounded = q.astype(bf16)

    odd = (lax.axis_index("space") % 2).reshape(1)
    hidden = layer_one.shape[0]
    width = 27 * PAD
    vectors = jnp.stack([bias_one, bias_two, readout] + [readout] * 5)
    forward, backward, two_t, columns = call(
        functools.partial(setup_kernel, coords),
        out_shape=(
            shape((hidden, width), bf16), shape((width, hidden), bf16),
            shape((hidden, hidden), bf16), shape((hidden, 8), f32),
        ),
        in_specs=[scalar] + [VMEM] * 3, out_specs=(VMEM,) * 4,
        scratch_shapes=[pltpu.VMEM((width, hidden), f32)],
    )(odd, layer_one.T, layer_two, vectors)
    weights = (forward, backward, layer_two, two_t, columns)

    field = shape((rows, CELLS), f32)

    def forces(plane):
        kept, sent = call(
            functools.partial(force_kernel, coords, beads, 4),
            out_shape=(field, field), in_specs=[VMEM] * 9, out_specs=(VMEM, VMEM),
            scratch_shapes=[pltpu.VMEM((36 * PAD, beads * CELLS), bf16), pltpu.VMEM((rows, CELLS), f32)],
        )(*neighbour_planes(plane), *weights)
        return kept, swap(sent, 1)

    modes = mode_matrices(coords, beads)
    table = update_table(masses, step_size, cycle_frequency, beads)
    half = 0.5 * step_size
    narrow = shape((rows, CELLS), bf16)
    q_new, rounded, p_mid, pushed = call(
        update_kernel,
        out_shape=(field, narrow, field, field), in_specs=[scalar] + [VMEM] * 7, out_specs=(VMEM,) * 4,
    )(half, q, p, *forces(rounded), modes, modes.T, table)
    p_new, velocity = call(
        finish_kernel,
        out_shape=(field, narrow), in_specs=[scalar] + [VMEM] * 6, out_specs=(VMEM, VMEM),
    )(half, p_mid, pushed, *forces(rounded), modes.T, table)

    share = wavevectors.shape[1] // devices
    own_vectors = lax.dynamic_slice_in_dim(wavevectors, lax.axis_index("space") * share, share, 1)
    fragment, planes_at = gather_planes(velocity)
    across, along = trig_tables(own_vectors, planes_at, devices)
    spectrum = call(
        functools.partial(project_kernel, 1.0 / math.sqrt(devices * CELLS)),
        out_shape=shape((2 * rows, share), f32), in_specs=[VMEM] * 3, out_specs=VMEM,
    )(fragment, across, along)
    return q_new.reshape(positions.shape), p_new.reshape(momenta.shape), spectrum.T


def solution(mesh):
    field = P(None, None, ("rep", "space"), None)
    return jax.shard_map(
        on_device,
        mesh=mesh,
        in_specs=(field, field) + (P(),) * 9,
        out_specs=(field, field, P(("rep", "space"), None)),
        check_vma=False,
    )
```

```python
import functools
import math

import jax
import jax.numpy as jnp
import numpy as np
from jax import lax
from jax.experimental import pallas as pl
from jax.experimental.pallas import tpu as pltpu
from jax.sharding import PartitionSpec as P


NY = 8
NZ = 16
CELLS = NY * NZ
PAD = 16
BLOCK = 9 * PAD
DEPTH = 256
GROUP = 4
SHIFTS = [(b, d) for b in (-1, 0, 1) for d in (-1, 0, 1)]
HIGHEST = lax.Precision.HIGHEST
TWO_PI = 6.283185307179586
VMEM = pl.BlockSpec(memory_space=pltpu.VMEM)
SMEM = pl.BlockSpec(memory_space=pltpu.SMEM)
HBM = pl.BlockSpec(memory_space=pltpu.MemorySpace.HBM)
shape = jax.ShapeDtypeStruct
f32, bf16 = jnp.float32, jnp.bfloat16

call = functools.partial(pl.pallas_call, compiler_params=pltpu.CompilerParams(vmem_limit_bytes=16 << 20))
dot = functools.partial(jnp.dot, preferred_element_type=jnp.float32)
exact_dot = functools.partial(jnp.dot, precision=HIGHEST, preferred_element_type=jnp.float32)


def in_hbm(value):
    return pltpu.with_memory_space_constraint(value, pltpu.MemorySpace.HBM)


def roll(values, amount):
    amount = amount % CELLS
    return values if amount == 0 else pltpu.roll(values, amount, 1)


def shift_y(values, step):
    return roll(values, -step * NZ)


def shift_z(values, step, inner):
    if step == 0:
        return values
    edge = NZ - 1 if step == 1 else 0
    return jnp.where(inner == edge, roll(values, step * (NZ - 1)), roll(values, -step))


def z_index(rows):
    return lax.broadcasted_iota(jnp.int32, (rows, CELLS), 1) % NZ


def load_kernel(*refs):
    count = (len(refs) - 2) // 2
    sources, rounded_ref, targets, semaphores = refs[:count], refs[count], refs[count + 1 : -1], refs[-1]
    copies = [pltpu.make_async_copy(a, b, semaphores.at[i]) for i, (a, b) in enumerate(zip(sources, targets))]
    for copy in copies:
        copy.start()
    copies[0].wait()
    rounded_ref[...] = targets[0][...].astype(bf16)
    for copy in copies[1:]:
        copy.wait()


def setup_kernel(
    coords, beads, masses_hbm, step_hbm, cycle_hbm, one_ref, bias_one_ref, two_ref, bias_two_ref, readout_ref,
    q_ref, p_ref, modes_ref, modes_t_ref, forward_ref, outer_forward_ref, backward_ref, two_t_ref, wide_ref,
    q_base_ref, q_map_ref, p_base_ref, pushed_ref, cosine_ref, finish_ref, half_ref,
    rows, masses_ref, step_ref, cycle_ref, semaphores
):
    copies = [
        pltpu.make_async_copy(masses_hbm, masses_ref, semaphores.at[0]),
        pltpu.make_async_copy(step_hbm, step_ref, semaphores.at[1]),
        pltpu.make_async_copy(cycle_hbm, cycle_ref, semaphores.at[2]),
    ]
    for copy in copies:
        copy.start()
    is_odd = lax.axis_index("space") % 2 == 1
    hidden = one_ref.shape[1]
    rows[: one_ref.shape[0], :] = one_ref[...].astype(f32)
    rows[one_ref.shape[0] :, :] = jnp.zeros((rows.shape[0] - one_ref.shape[0], hidden), f32)
    at = lax.broadcasted_iota(jnp.int32, (PAD, hidden), 0)
    real = at < coords
    rest = bias_one_ref[...]
    turned = []
    for along_x in range(3):
        for o in range(9):
            even, odd = ((a * 9 + o) * coords for a in (along_x, 2 - along_x))
            taken = rows[even : even + PAD, :]
            if odd != even:
                taken = jnp.where(is_odd, rows[odd : odd + PAD, :], taken)
            taken = jnp.where(real, taken, 0.0)
            top = (along_x * 9 + o) * PAD
            backward_ref[top : top + PAD, :] = taken.astype(bf16)
            if along_x == 0 and o < 3:
                term = rest.astype(bf16).astype(f32)
                rest = rest - term
                taken = jnp.where(real, taken, jnp.broadcast_to(term, taken.shape))
                taken = jnp.where(at <= coords, taken, 0.0)
            turned.append(taken)
    forward = jnp.concatenate(turned).T.astype(bf16)
    forward_ref[...] = forward
    outer_forward_ref[...] = jnp.concatenate([forward[:, BLOCK:], forward[:, :BLOCK]], axis=1)
    two_t_ref[...] = two_ref[...].astype(f32).T.astype(bf16)
    columns = jnp.concatenate([bias_two_ref[...], readout_ref[...], jnp.zeros((6, hidden), f32)]).T
    for i in range(2):
        wide_ref[i] = jnp.broadcast_to(columns[:, i : i + 1], (hidden, CELLS))

    for copy in copies:
        copy.wait()
    total = coords * beads
    order = (lax.broadcasted_iota(jnp.int32, (total, CELLS), 0) % beads).astype(f32)
    mass = jnp.concatenate([jnp.full((beads, CELLS), masses_ref[c], f32) for c in range(coords)])
    step = step_ref[0]
    half = 0.5 * step
    frequency = 2.0 * cycle_ref[0] * jnp.sin(order * (0.5 * TWO_PI / beads))
    phase = frequency * step
    cosine, sine = jnp.cos(phase), jnp.sin(phase)
    drift = step * jnp.where(order == 0, 1.0, sine / jnp.where(order == 0, 1.0, phase)) / mass
    spring = mass * frequency * sine
    mode = exact_dot(modes_t_ref[...], jnp.concatenate([q_ref[...], p_ref[...]], axis=1))
    mode_q, mode_p = mode[:, :CELLS], mode[:, CELLS:]
    moved = cosine * mode_q + drift * mode_p
    pushed = cosine * mode_p - spring * mode_q
    base = exact_dot(modes_ref[...], jnp.concatenate([moved, pushed], axis=1))
    q_base_ref[...] = base[:, :CELLS]
    p_base_ref[...] = base[:, CELLS:]
    pushed_ref[...] = pushed
    cosine_ref[...] = cosine
    q_map_ref[...] = exact_dot(modes_ref[...], (half * drift[:, :1]) * modes_t_ref[...])
    finish_ref[...] = jnp.concatenate([half / mass, 1.0 / mass], axis=1)
    half_ref[...] = jnp.full(half_ref.shape, half, f32)


def put_features(coords, beads, plane_ref, stage, features, top):
    stage[...] = plane_ref[...].astype(f32)
    filler = jnp.ones((PAD - coords, CELLS), f32)
    pieces = []
    for j in range(beads):
        pieces += [stage[pl.ds(j, coords, stride=beads), :], filler]
    plane = jnp.concatenate(pieces)
    inner_z = z_index(beads * PAD)
    along = {d: shift_z(plane, d, inner_z) for d in (-1, 0, 1)}
    for o, (b, d) in enumerate(SHIFTS):
        moved = shift_y(along[d], b).astype(bf16)
        first = top + o * PAD
        for j in range(beads):
            features[first : first + PAD, j * CELLS : (j + 1) * CELLS] = moved[j * PAD : (j + 1) * PAD]


def back_one(first, two_ref, two_t_ref, wide_ref):
    bias, readout = (jnp.concatenate([wide_ref[i]] * GROUP, axis=1) for i in range(2))
    hidden = jnp.tanh(first).astype(bf16)
    second = jnp.tanh(dot(two_ref[...], hidden) + bias)
    back = (readout * (1.0 - second * second)).astype(bf16)
    widened = hidden.astype(f32)
    return (dot(two_t_ref[...], back) * (1.0 - widened * widened)).astype(bf16)


def shifted_sum(sums, at):
    inner_z = z_index(PAD)
    total = None
    for d in (-1, 0, 1):
        part = None
        for b in (-1, 0, 1):
            o = (b + 1) * 3 + d + 1
            moved = shift_y(sums[o * PAD : (o + 1) * PAD, at * CELLS : (at + 1) * CELLS], -b)
            part = moved if part is None else part + moved
        part = shift_z(part, -d, inner_z)
        total = part if total is None else total + part
    return total


def own_kernel(
    coords, beads, tied, outer_ref, own_ref, inner_ref, forward_ref, backward_ref, two_ref, two_t_ref, wide_ref, *refs
):
    sent_ref, kept_ref, features, stage = refs[tied:]
    for place, ref in enumerate((outer_ref, own_ref, inner_ref)):
        put_features(coords, beads, ref, stage, features, place * BLOCK)
    for first in range(0, beads, GROUP):
        columns = slice(first * CELLS, (first + GROUP) * CELLS)
        back = back_one(dot(forward_ref[...], features[:, columns]), two_ref, two_t_ref, wide_ref)
        sums = dot(backward_ref[BLOCK:], back)
        for at in range(GROUP):
            rows = pl.ds(first + at, coords, stride=beads)
            kept_ref[rows, :] = shifted_sum(sums[:BLOCK], at)[:coords]
            sent_ref[rows, :] = shifted_sum(sums[BLOCK:], at)[:coords]


def outer_kernel(
    coords, beads, outer2_ref, features_ref, kept_in_ref, forward_ref, backward_ref, two_ref, two_t_ref, wide_ref,
    kept_ref, features, stage
):
    extra = 2 * BLOCK - DEPTH
    put_features(coords, beads, outer2_ref, stage, features, extra)
    features[:extra, :] = features_ref[DEPTH : 2 * BLOCK, :]
    for first in range(0, beads, GROUP):
        columns = slice(first * CELLS, (first + GROUP) * CELLS)
        pre = dot(forward_ref[:, :DEPTH], features_ref[:DEPTH, columns])
        pre = pre + dot(forward_ref[:, DEPTH:], features[:, columns])
        sums = dot(backward_ref[2 * BLOCK :], back_one(pre, two_ref, two_t_ref, wide_ref))
        for at in range(GROUP):
            rows = pl.ds(first + at, coords, stride=beads)
            kept_ref[rows, :] = kept_in_ref[rows, :] + shifted_sum(sums, at)[:coords]


def move_kernel(q_base_ref, q_map_ref, kept_ref, came_ref, q_out, rounded_out, sum_out):
    sums = kept_ref[...] + came_ref[...]
    sum_out[...] = sums
    q = q_base_ref[...] - exact_dot(q_map_ref[...], sums)
    q_out[...] = q
    rounded_out[...] = q.astype(bf16)


def push_kernel(
    share, planes_at, half_ref, sum_ref, p_base_ref, pushed_ref, cosine_ref, finish_ref, modes_ref, modes_t_ref,
    vectors_ref, p_out, velocity_out, velocity_map_out, planes_out, cells_out
):
    kick = cosine_ref[...] * exact_dot(modes_t_ref[...], half_ref[0:1, :] * sum_ref[...])
    p_out[...] = p_base_ref[...] - exact_dot(modes_ref[...], kick)
    velocity_out[...] = (pushed_ref[...] - kick) * finish_ref[:, CELLS:]
    velocity_map_out[...] = finish_ref[:, :1] * modes_t_ref[...]
    extent_x = len(planes_at)
    whole = extent_x * CELLS
    here = lax.axis_index("space")
    if vectors_ref.shape[1] == share:
        vectors = vectors_ref[...]
    else:
        vectors = vectors_ref[:, pl.ds(pl.multiple_of(here * share, CELLS), share)]
    cell = lax.broadcasted_iota(jnp.int32, (CELLS, share), 0)
    along = vectors[1:2] * ((cell // NZ) * (extent_x * NZ)) + vectors[2:3] * ((cell % NZ) * (extent_x * NY))
    across = jnp.concatenate([vectors[0:1] * ((here ^ at) * CELLS) for at in planes_at])
    for numerator, out in ((across, planes_out), (along, cells_out)):
        angle = TWO_PI * (numerator & (whole - 1)).astype(f32) / whole
        out[0] = jnp.cos(angle)
        out[1] = jnp.sin(angle)


def finish_kernel(half_ref, velocity_ref, map_ref, kept_ref, came_ref, velocity_out, kick_out):
    sums = kept_ref[...] + came_ref[...]
    velocity_out[...] = (velocity_ref[...] - exact_dot(map_ref[...], sums)).astype(bf16)
    kick_out[...] = half_ref[0:1, :] * sums


def project_kernel(scale, velocity_ref, planes_ref, cells_ref, out_ref):
    count, fields, _ = velocity_ref.shape
    cos_cell, sin_cell = cells_ref[0], cells_ref[1]

    def trig(i):
        cos_plane, sin_plane = planes_ref[0, i : i + 1, :], planes_ref[1, i : i + 1, :]
        cosine = cos_plane * cos_cell - sin_plane * sin_cell
        sine = sin_plane * cos_cell + cos_plane * sin_cell
        return cosine.astype(bf16), sine.astype(bf16)

    cos_sum = sin_sum = 0.0
    for i in range(0, count, 2):
        (cos_0, sin_0), (cos_1, sin_1) = trig(i), trig(i + 1)
        block = jnp.concatenate([velocity_ref[i], velocity_ref[i + 1]], axis=1)
        cos_sum += dot(block, jnp.concatenate([cos_0, cos_1]))
        sin_sum += dot(block, jnp.concatenate([sin_0, sin_1]))
    out_ref[:fields, :] = cos_sum * scale
    out_ref[fields:, :] = sin_sum * scale


def mode_matrix(coords, beads):
    j = np.arange(beads)[:, None]
    k = np.arange(beads)[None, :]
    angles = 2.0 * np.pi * ((j * k) % beads) / beads
    edge = np.cos(angles) / math.sqrt(beads)
    inside = np.where(k < beads // 2, np.cos(angles), np.sin(angles)) * math.sqrt(2.0 / beads)
    matrix = np.where((k == 0) | (k == beads // 2), edge, inside)
    modes = np.einsum("ab,jk->ajbk", np.eye(coords), matrix).reshape(coords * beads, coords * beads)
    return modes.astype(np.float32)


def swap(value, distance):
    return lax.ppermute(value, "space", [(i, i ^ distance) for i in range(lax.axis_size("space"))])


def neighbour_planes(plane):
    count = lax.axis_size("space")
    step = [1 if i % 2 else -1 for i in range(count)]
    outer = lax.ppermute(plane, "space", [(i, (i + step[i]) % count) for i in range(count)])
    inner = swap(plane, 1)
    outer2 = lax.ppermute(plane, "space", [(i, (i - 2 * step[i]) % count) for i in range(count)])
    return outer2, outer, inner


def gather_order(count):
    order, distance = [0], count // 2
    while distance:
        if distance == 4:
            order, distance = [i ^ d for d in (0, 2, 4, 6) for i in order], 1
        else:
            order, distance = [i ^ d for d in (0, distance) for i in order], distance // 2
    return order


def gather_planes(velocity):
    held, distance = velocity[None], lax.axis_size("space") // 2
    while distance:
        if distance == 4:
            near, far = swap(held, 2), swap(held, 4)
            held, distance = jnp.concatenate([held, near, far, swap(near, 4)]), 1
        else:
            held, distance = jnp.concatenate([held, swap(held, distance)]), distance // 2
    return held


def on_device(
    positions, momenta, masses, step_size, cycle_frequency,
    layer_one, bias_one, layer_two, bias_two, readout, wavevectors
):
    coords, beads, planes, cells = positions.shape
    devices = lax.axis_size("space")
    assert planes == 1 and cells == CELLS and devices & (devices - 1) == 0 and devices > 1
    total = coords * beads
    hidden = layer_one.shape[0]
    width = 27 * PAD
    field, narrow = shape((total, CELLS), f32), shape((total, CELLS), bf16)
    square = shape((total, total), f32)

    modes = mode_matrix(coords, beads)
    share = wavevectors.shape[1] // devices
    if share % CELLS:
        wavevectors = lax.dynamic_slice_in_dim(wavevectors, lax.axis_index("space") * share, share, 1)
    inputs = (
        positions.reshape(total, CELLS), momenta.reshape(total, CELLS),
        layer_one.T, bias_one.reshape(1, hidden), layer_two, bias_two.reshape(1, hidden), readout.reshape(1, hidden),
        jnp.asarray(modes), jnp.asarray(modes.T), wavevectors,
    )
    rounded, q, p, one_t, bias_one, two, bias_two, readout, modes, modes_t, wavevectors = call(
        load_kernel,
        out_shape=(narrow,) + tuple(shape(x.shape, x.dtype) for x in inputs),
        in_specs=[HBM] * len(inputs), out_specs=(VMEM,) * (len(inputs) + 1),
        scratch_shapes=[pltpu.SemaphoreType.DMA((len(inputs),))],
    )(*map(in_hbm, inputs))

    (
        forward, outer_forward, backward, two_t, wide, q_base, q_map, p_base, pushed, cosine, finish, half
    ) = call(
        functools.partial(setup_kernel, coords, beads),
        out_shape=(
            shape((hidden, width), bf16), shape((hidden, width), bf16), shape((width, hidden), bf16),
            shape((hidden, hidden), bf16), shape((2, hidden, CELLS), f32),
            field, square, field, field, field, shape((total, 2 * CELLS), f32), shape((8, CELLS), f32),
        ),
        in_specs=[HBM] * 3 + [VMEM] * 9, out_specs=(VMEM,) * 12,
        scratch_shapes=[
            pltpu.VMEM((width, hidden), f32), pltpu.SMEM((coords,), f32), pltpu.SMEM((1,), f32),
            pltpu.SMEM((1,), f32), pltpu.SemaphoreType.DMA((3,)),
        ],
    )(
        in_hbm(masses), step_size, cycle_frequency, one_t, bias_one, two, bias_two, readout, q, p, modes, modes_t
    )
    layers = (backward, two, two_t, wide)
    stage = pltpu.VMEM((total, CELLS), f32)

    def forces(plane, *tied):
        outer2, outer, inner = neighbour_planes(plane)
        sent, kept, features = call(
            functools.partial(own_kernel, coords, beads, len(tied)),
            out_shape=(field, field, shape((width, beads * CELLS), bf16)),
            in_specs=[VMEM] * (8 + len(tied)), out_specs=(VMEM,) * 3, scratch_shapes=[stage],
        )(outer, plane, inner, forward, *layers, *tied)
        came = swap(sent, 1)
        kept = call(
            functools.partial(outer_kernel, coords, beads),
            out_shape=field, in_specs=[VMEM] * 8, out_specs=VMEM,
            scratch_shapes=[pltpu.VMEM((width - DEPTH, beads * CELLS), bf16), stage],
        )(outer2, features, kept, outer_forward, *layers)
        return kept, came

    q_new, rounded, sums = call(
        move_kernel, out_shape=(field, narrow, field), in_specs=[VMEM] * 4, out_specs=(VMEM,) * 3,
    )(q_base, q_map, *forces(rounded))
    order = gather_order(devices)
    p_mid, velocity_base, velocity_map, across, along = call(
        functools.partial(push_kernel, share, order),
        out_shape=(field, field, square, shape((2, devices, share), f32), shape((2, CELLS, share), f32)),
        in_specs=[VMEM] * 9, out_specs=(VMEM,) * 5,
    )(half, sums, p_base, pushed, cosine, finish, modes, modes_t, wavevectors)
    velocity, kick = call(
        finish_kernel, out_shape=(narrow, field), in_specs=[VMEM] * 5, out_specs=(VMEM,) * 2,
    )(half, velocity_base, velocity_map, *forces(rounded))
    p_new = p_mid - kick
    spectrum = call(
        functools.partial(project_kernel, 1.0 / math.sqrt(devices * CELLS)),
        out_shape=shape((2 * total, share), f32), in_specs=[VMEM] * 3, out_specs=VMEM,
    )(gather_planes(velocity), across, along)
    return q_new.reshape(positions.shape), p_new.reshape(momenta.shape), spectrum.T


def solution(mesh):
    field = P(None, None, ("rep", "space"), None)

    return jax.shard_map(
        on_device,
        mesh=mesh,
        in_specs=(field, field) + (P(),) * 9,
        out_specs=(field, field, P(("rep", "space"), None)),
        check_vma=False,
    )
```

```python
import functools
import math

import jax
import jax.numpy as jnp
import numpy as np
from jax import lax
from jax.experimental import pallas as pl
from jax.experimental.pallas import tpu as pltpu
from jax.sharding import PartitionSpec as P


NY = 8
NZ = 16
CELLS = NY * NZ
PAD = 16
BLOCK = 9 * PAD
DEPTH = 256
SIZES = (8,8,)
SKEW = 1
SHIFTS = [(b, d) for b in (-1, 0, 1) for d in (-1, 0, 1)]
HIGHEST = lax.Precision.HIGHEST
TWO_PI = 6.283185307179586
VMEM = pl.BlockSpec(memory_space=pltpu.VMEM)
SMEM = pl.BlockSpec(memory_space=pltpu.SMEM)
HBM = pl.BlockSpec(memory_space=pltpu.MemorySpace.HBM)
shape = jax.ShapeDtypeStruct
f32, bf16 = jnp.float32, jnp.bfloat16

call = functools.partial(pl.pallas_call, compiler_params=pltpu.CompilerParams(vmem_limit_bytes=16 << 20))
dot = functools.partial(jnp.dot, preferred_element_type=jnp.float32)
exact_dot = functools.partial(jnp.dot, precision=HIGHEST, preferred_element_type=jnp.float32)


def in_hbm(value):
    return pltpu.with_memory_space_constraint(value, pltpu.MemorySpace.HBM)


def roll(values, amount):
    amount = amount % CELLS
    return values if amount == 0 else pltpu.roll(values, amount, 1)


def shift_y(values, step):
    return roll(values, -step * NZ)


def shift_z(values, step, inner):
    if step == 0:
        return values
    edge = NZ - 1 if step == 1 else 0
    return jnp.where(inner == edge, roll(values, step * (NZ - 1)), roll(values, -step))


def z_index(rows):
    return lax.broadcasted_iota(jnp.int32, (rows, CELLS), 1) % NZ


def round_kernel(q_hbm, rounded_ref, q_ref, semaphore):
    copy = pltpu.make_async_copy(q_hbm, q_ref, semaphore)
    copy.start()
    copy.wait()
    rounded_ref[...] = q_ref[...].astype(bf16)


def setup_kernel(
    coords, beads, masses_hbm, step_hbm, cycle_hbm, one_hbm, bias_one_hbm, bias_two_hbm, readout_hbm, p_hbm,
    two_hbm, modes_hbm, modes_t_hbm, vectors_hbm, q_ref,
    forward_ref, outer_forward_ref, backward_ref, two_t_ref, wide_ref,
    q_base_ref, q_map_ref, p_base_ref, pushed_ref, cosine_ref, finish_ref, half_ref,
    two_ref, modes_ref, modes_t_ref, vectors_ref,
    rows, masses_ref, step_ref, cycle_ref, one_ref, bias_one_ref, bias_two_ref, readout_ref, p_ref, semaphores
):
    moves = (
        (one_hbm, one_ref), (bias_one_hbm, bias_one_ref), (bias_two_hbm, bias_two_ref), (readout_hbm, readout_ref),
        (two_hbm, two_ref), (masses_hbm, masses_ref), (step_hbm, step_ref), (cycle_hbm, cycle_ref),
        (p_hbm, p_ref), (modes_hbm, modes_ref), (modes_t_hbm, modes_t_ref), (vectors_hbm, vectors_ref),
    )
    copies = [pltpu.make_async_copy(a, b, semaphores.at[i]) for i, (a, b) in enumerate(moves)]
    for copy in copies:
        copy.start()
    for copy in copies[:5]:
        copy.wait()
    is_odd = lax.axis_index("space") % 2 == 1
    hidden = one_ref.shape[1]
    rows[: one_ref.shape[0], :] = one_ref[...].astype(f32)
    rows[one_ref.shape[0] :, :] = jnp.zeros((rows.shape[0] - one_ref.shape[0], hidden), f32)
    at = lax.broadcasted_iota(jnp.int32, (PAD, hidden), 0)
    real = at < coords
    rest = bias_one_ref[...]
    turned = []
    for along_x in range(3):
        for o in range(9):
            even, odd = ((a * 9 + o) * coords for a in (along_x, 2 - along_x))
            taken = rows[even : even + PAD, :]
            if odd != even:
                taken = jnp.where(is_odd, rows[odd : odd + PAD, :], taken)
            taken = jnp.where(real, taken, 0.0)
            top = (along_x * 9 + o) * PAD
            backward_ref[top : top + PAD, :] = taken.astype(bf16)
            if along_x == 0 and o < 3:
                term = rest.astype(bf16).astype(f32)
                rest = rest - term
                taken = jnp.where(real, taken, jnp.broadcast_to(term, taken.shape))
                taken = jnp.where(at <= coords, taken, 0.0)
            turned.append(taken)
    forward = jnp.concatenate(turned).T.astype(bf16)
    forward_ref[...] = forward
    outer_forward_ref[...] = jnp.concatenate([forward[:, BLOCK:], forward[:, :BLOCK]], axis=1)
    two_t_ref[...] = two_ref[...].astype(f32).T.astype(bf16)
    columns = jnp.concatenate([bias_two_ref[...], readout_ref[...], jnp.zeros((6, hidden), f32)]).T
    for i in range(2):
        wide_ref[i] = jnp.broadcast_to(columns[:, i : i + 1], (hidden, CELLS))

    for copy in copies[5:]:
        copy.wait()
    order = lax.broadcasted_iota(jnp.int32, (beads, CELLS), 0).astype(f32)
    mass = jnp.concatenate([jnp.full((beads, CELLS), masses_ref[c], f32) for c in range(coords)])
    step = step_ref[0]
    half = 0.5 * step
    frequency = 2.0 * cycle_ref[0] * jnp.sin(order * (0.5 * TWO_PI / beads))
    phase = frequency * step
    sine = jnp.sin(phase)
    ratio = jnp.where(order == 0, 1.0, sine / jnp.where(order == 0, 1.0, phase))
    cosine, drift, spring = (
        jnp.concatenate([term] * coords) for term in (jnp.cos(phase), step * ratio, frequency * sine)
    )
    drift, spring = drift / mass, mass * spring
    mode = exact_dot(modes_t_ref[...], jnp.concatenate([q_ref[...], p_ref[...]], axis=1))
    mode_q, mode_p = mode[:, :CELLS], mode[:, CELLS:]
    moved = cosine * mode_q + drift * mode_p
    pushed = cosine * mode_p - spring * mode_q
    base = exact_dot(modes_ref[...], jnp.concatenate([moved, pushed], axis=1))
    q_base_ref[...] = base[:, :CELLS]
    p_base_ref[...] = base[:, CELLS:]
    pushed_ref[...] = pushed
    cosine_ref[...] = cosine
    q_map_ref[...] = exact_dot(modes_ref[...], (half * drift[:, :1]) * modes_t_ref[...])
    finish_ref[...] = jnp.concatenate([half / mass, 1.0 / mass], axis=1)
    half_ref[...] = jnp.full(half_ref.shape, half, f32)


def put_features(coords, beads, chosen, stage, features, top):
    filler = jnp.ones((PAD - coords, CELLS), f32)
    inner_z = z_index(PAD)
    for j in chosen:
        plane = jnp.concatenate([stage[pl.ds(j, coords, stride=beads), :], filler]).astype(bf16)
        along = {d: shift_z(plane, d, inner_z) for d in (-1, 0, 1)}
        for o, (b, d) in enumerate(SHIFTS):
            first = top + o * PAD
            features[first : first + PAD, j * CELLS : (j + 1) * CELLS] = shift_y(along[d], b)


def groups_of(beads):
    sizes = SIZES if sum(SIZES) == beads else (beads,)
    starts = np.cumsum((0,) + sizes)
    return [range(int(first), int(first) + size) for first, size in zip(starts, sizes)]


def columns_of(chosen):
    return slice(chosen[0] * CELLS, (chosen[-1] + 1) * CELLS)


def run_skewed(groups, stages):
    state = [() for _ in groups]
    order = sorted((SKEW * g + s, -s, g) for g in range(len(groups)) for s in range(len(stages)))
    for _, s, g in order:
        state[g] = stages[-s](groups[g], *state[g])


def back_stages(two_ref, two_t_ref, wide_ref):
    def second(chosen, first):
        bias, readout = (jnp.concatenate([wide_ref[i]] * len(chosen), axis=1) for i in range(2))
        hidden = jnp.tanh(first).astype(bf16)
        second = jnp.tanh(dot(two_ref[...], hidden) + bias)
        return hidden, (readout * (1.0 - second * second)).astype(bf16)

    def third(chosen, hidden, back):
        widened = hidden.astype(f32)
        return ((dot(two_t_ref[...], back) * (1.0 - widened * widened)).astype(bf16),)

    return second, third


def shifted_sum(sums, at):
    inner_z = z_index(PAD)
    total = None
    for d in (-1, 0, 1):
        part = None
        for b in (-1, 0, 1):
            o = (b + 1) * 3 + d + 1
            moved = shift_y(sums[o * PAD : (o + 1) * PAD, at * CELLS : (at + 1) * CELLS], -b)
            part = moved if part is None else part + moved
        part = shift_z(part, -d, inner_z)
        total = part if total is None else total + part
    return total


def own_kernel(
    coords, beads, tied, outer_ref, own_ref, inner_ref, forward_ref, backward_ref, two_ref, two_t_ref, wide_ref, *refs
):
    sent_ref, kept_ref, features, stage = refs[tied:]
    for place, ref in enumerate((outer_ref, own_ref, inner_ref)):
        stage[place] = ref[...].astype(f32)

    def put(chosen):
        for place in range(3):
            put_features(coords, beads, chosen, stage.at[place], features, place * BLOCK)
        return ()

    def first(chosen):
        return (dot(forward_ref[...], features[:, columns_of(chosen)]),)

    def last(chosen, back):
        return (dot(backward_ref[BLOCK:], back),)

    def store(chosen, sums):
        for at, j in enumerate(chosen):
            rows = pl.ds(j, coords, stride=beads)
            kept_ref[rows, :] = shifted_sum(sums[:BLOCK], at)[:coords]
            sent_ref[rows, :] = shifted_sum(sums[BLOCK:], at)[:coords]

    run_skewed(groups_of(beads), (put, first, *back_stages(two_ref, two_t_ref, wide_ref), last, store))


def outer_kernel(
    coords, beads, outer2_ref, features_ref, kept_in_ref, forward_ref, backward_ref, two_ref, two_t_ref, wide_ref,
    kept_ref, features, stage
):
    extra = 2 * BLOCK - DEPTH
    stage[...] = outer2_ref[...].astype(f32)

    def put(chosen):
        put_features(coords, beads, chosen, stage, features, extra)
        features[:extra, columns_of(chosen)] = features_ref[DEPTH : 2 * BLOCK, columns_of(chosen)]
        return ()

    def first(chosen):
        near = dot(forward_ref[:, :DEPTH], features_ref[:DEPTH, columns_of(chosen)])
        return (near + dot(forward_ref[:, DEPTH:], features[:, columns_of(chosen)]),)

    def last(chosen, back):
        return (dot(backward_ref[2 * BLOCK :], back),)

    def store(chosen, sums):
        for at, j in enumerate(chosen):
            rows = pl.ds(j, coords, stride=beads)
            kept_ref[rows, :] = kept_in_ref[rows, :] + shifted_sum(sums, at)[:coords]

    run_skewed(groups_of(beads), (put, first, *back_stages(two_ref, two_t_ref, wide_ref), last, store))


def move_kernel(q_base_ref, q_map_ref, kept_ref, came_ref, q_out, rounded_out, sum_out):
    sums = kept_ref[...] + came_ref[...]
    sum_out[...] = sums
    q = q_base_ref[...] - exact_dot(q_map_ref[...], sums)
    q_out[...] = q
    rounded_out[...] = q.astype(bf16)


def push_kernel(
    share, planes_at, half_ref, sum_ref, p_base_ref, pushed_ref, cosine_ref, finish_ref, modes_ref, modes_t_ref,
    vectors_ref, p_out, velocity_out, velocity_map_out, planes_out, cells_out
):
    kick = cosine_ref[...] * exact_dot(modes_t_ref[...], half_ref[0:1, :] * sum_ref[...])
    p_out[...] = p_base_ref[...] - exact_dot(modes_ref[...], kick)
    velocity_out[...] = (pushed_ref[...] - kick) * finish_ref[:, CELLS:]
    velocity_map_out[...] = finish_ref[:, :1] * modes_t_ref[...]
    extent_x = len(planes_at)
    whole = extent_x * CELLS
    here = lax.axis_index("space")
    if vectors_ref.shape[1] == share:
        vectors = vectors_ref[...]
    else:
        vectors = vectors_ref[:, pl.ds(pl.multiple_of(here * share, CELLS), share)]
    cell = lax.broadcasted_iota(jnp.int32, (CELLS, share), 0)
    along = vectors[1:2] * ((cell // NZ) * (extent_x * NZ)) + vectors[2:3] * ((cell % NZ) * (extent_x * NY))
    across = jnp.concatenate([vectors[0:1] * ((here ^ at) * CELLS) for at in planes_at])
    for numerator, out in ((across, planes_out), (along, cells_out)):
        angle = TWO_PI * (numerator & (whole - 1)).astype(f32) / whole
        out[0] = jnp.cos(angle)
        out[1] = jnp.sin(angle)


def finish_kernel(half_ref, velocity_ref, map_ref, kept_ref, came_ref, velocity_out, kick_out):
    sums = kept_ref[...] + came_ref[...]
    velocity_out[...] = (velocity_ref[...] - exact_dot(map_ref[...], sums)).astype(bf16)
    kick_out[...] = half_ref[0:1, :] * sums


def project_kernel(scale, velocity_ref, planes_ref, cells_ref, out_ref):
    count, fields, _ = velocity_ref.shape
    cos_cell, sin_cell = cells_ref[0], cells_ref[1]

    def trig(i):
        cos_plane, sin_plane = planes_ref[0, i : i + 1, :], planes_ref[1, i : i + 1, :]
        cosine = cos_plane * cos_cell - sin_plane * sin_cell
        sine = sin_plane * cos_cell + cos_plane * sin_cell
        return cosine.astype(bf16), sine.astype(bf16)

    cos_sum = sin_sum = 0.0
    for i in range(0, count, 2):
        (cos_0, sin_0), (cos_1, sin_1) = trig(i), trig(i + 1)
        block = jnp.concatenate([velocity_ref[i], velocity_ref[i + 1]], axis=1)
        cos_sum += dot(block, jnp.concatenate([cos_0, cos_1]))
        sin_sum += dot(block, jnp.concatenate([sin_0, sin_1]))
    out_ref[:fields, :] = cos_sum * scale
    out_ref[fields:, :] = sin_sum * scale


def mode_matrix(coords, beads):
    j = np.arange(beads)[:, None]
    k = np.arange(beads)[None, :]
    angles = 2.0 * np.pi * ((j * k) % beads) / beads
    edge = np.cos(angles) / math.sqrt(beads)
    inside = np.where(k < beads // 2, np.cos(angles), np.sin(angles)) * math.sqrt(2.0 / beads)
    matrix = np.where((k == 0) | (k == beads // 2), edge, inside)
    modes = np.einsum("ab,jk->ajbk", np.eye(coords), matrix).reshape(coords * beads, coords * beads)
    return modes.astype(np.float32)


def swap(value, distance):
    return lax.ppermute(value, "space", [(i, i ^ distance) for i in range(lax.axis_size("space"))])


def neighbour_planes(plane):
    count = lax.axis_size("space")
    step = [1 if i % 2 else -1 for i in range(count)]
    outer = lax.ppermute(plane, "space", [(i, (i + step[i]) % count) for i in range(count)])
    inner = swap(plane, 1)
    outer2 = lax.ppermute(plane, "space", [(i, (i - 2 * step[i]) % count) for i in range(count)])
    return outer2, outer, inner


def gather_order(count):
    order, distance = [0], count // 2
    while distance:
        if distance == 4:
            order, distance = [i ^ d for d in (0, 2, 4, 6) for i in order], 1
        else:
            order, distance = [i ^ d for d in (0, distance) for i in order], distance // 2
    return order


def gather_planes(velocity):
    held, distance = velocity[None], lax.axis_size("space") // 2
    while distance:
        if distance == 4:
            near, far = swap(held, 2), swap(held, 4)
            held, distance = jnp.concatenate([held, near, far, swap(near, 4)]), 1
        else:
            held, distance = jnp.concatenate([held, swap(held, distance)]), distance // 2
    return held


def on_device(
    positions, momenta, masses, step_size, cycle_frequency,
    layer_one, bias_one, layer_two, bias_two, readout, wavevectors
):
    coords, beads, planes, cells = positions.shape
    devices = lax.axis_size("space")
    assert planes == 1 and cells == CELLS and devices & (devices - 1) == 0 and devices > 1
    total = coords * beads
    hidden = layer_one.shape[0]
    width = 27 * PAD
    field, narrow = shape((total, CELLS), f32), shape((total, CELLS), bf16)
    square = shape((total, total), f32)

    modes = mode_matrix(coords, beads)
    share = wavevectors.shape[1] // devices
    if share % CELLS:
        wavevectors = lax.dynamic_slice_in_dim(wavevectors, lax.axis_index("space") * share, share, 1)
    rounded, q = call(
        round_kernel, out_shape=(narrow, field), in_specs=[HBM], out_specs=(VMEM,) * 2,
        scratch_shapes=[pltpu.SemaphoreType.DMA],
    )(in_hbm(positions.reshape(total, CELLS)))

    row = pltpu.VMEM((1, hidden), f32)
    inputs = (
        layer_one.T, bias_one.reshape(1, hidden), bias_two.reshape(1, hidden), readout.reshape(1, hidden),
        momenta.reshape(total, CELLS), layer_two, jnp.asarray(modes), jnp.asarray(modes.T), wavevectors,
    )
    (
        forward, outer_forward, backward, two_t, wide, q_base, q_map, p_base, pushed, cosine, finish, half,
        two, modes, modes_t, wavevectors
    ) = call(
        functools.partial(setup_kernel, coords, beads),
        out_shape=(
            shape((hidden, width), bf16), shape((hidden, width), bf16), shape((width, hidden), bf16),
            shape((hidden, hidden), bf16), shape((2, hidden, CELLS), f32),
            field, square, field, field, field, shape((total, 2 * CELLS), f32), shape((8, CELLS), f32),
        ) + tuple(shape(x.shape, x.dtype) for x in inputs[5:]),
        in_specs=[HBM] * 12 + [VMEM], out_specs=(VMEM,) * 16,
        scratch_shapes=[
            pltpu.VMEM((width, hidden), f32), pltpu.SMEM((coords,), f32), pltpu.SMEM((1,), f32),
            pltpu.SMEM((1,), f32), pltpu.VMEM(inputs[0].shape, bf16), row, row, row,
            pltpu.VMEM((total, CELLS), f32), pltpu.SemaphoreType.DMA((12,)),
        ],
    )(in_hbm(masses), step_size, cycle_frequency, *map(in_hbm, inputs), q)
    layers = (backward, two, two_t, wide)
    stage = pltpu.VMEM((total, CELLS), f32)

    def forces(plane, *tied):
        outer2, outer, inner = neighbour_planes(plane)
        sent, kept, features = call(
            functools.partial(own_kernel, coords, beads, len(tied)),
            out_shape=(field, field, shape((width, beads * CELLS), bf16)),
            in_specs=[VMEM] * (8 + len(tied)), out_specs=(VMEM,) * 3, scratch_shapes=[pltpu.VMEM((3, total, CELLS), f32)],
        )(outer, plane, inner, forward, *layers, *tied)
        came = swap(sent, 1)
        kept = call(
            functools.partial(outer_kernel, coords, beads),
            out_shape=field, in_specs=[VMEM] * 8, out_specs=VMEM,
            scratch_shapes=[pltpu.VMEM((width - DEPTH, beads * CELLS), bf16), stage],
        )(outer2, features, kept, outer_forward, *layers)
        return kept, came

    q_new, rounded, sums = call(
        move_kernel, out_shape=(field, narrow, field), in_specs=[VMEM] * 4, out_specs=(VMEM,) * 3,
    )(q_base, q_map, *forces(rounded))
    order = gather_order(devices)
    p_mid, velocity_base, velocity_map, across, along = call(
        functools.partial(push_kernel, share, order),
        out_shape=(field, field, square, shape((2, devices, share), f32), shape((2, CELLS, share), f32)),
        in_specs=[VMEM] * 9, out_specs=(VMEM,) * 5,
    )(half, sums, p_base, pushed, cosine, finish, modes, modes_t, wavevectors)
    velocity, kick = call(
        finish_kernel, out_shape=(narrow, field), in_specs=[VMEM] * 5, out_specs=(VMEM,) * 2,
    )(half, velocity_base, velocity_map, *forces(rounded))
    p_new = p_mid - kick
    spectrum = call(
        functools.partial(project_kernel, 1.0 / math.sqrt(devices * CELLS)),
        out_shape=shape((2 * total, share), f32), in_specs=[VMEM] * 3, out_specs=VMEM,
    )(gather_planes(velocity), across, along)
    return q_new.reshape(positions.shape), p_new.reshape(momenta.shape), spectrum.T


def solution(mesh):
    field = P(None, None, ("rep", "space"), None)

    return jax.shard_map(
        on_device,
        mesh=mesh,
        in_specs=(field, field) + (P(),) * 9,
        out_specs=(field, field, P(("rep", "space"), None)),
        check_vma=False,
    )
```

```python
import functools
import math

import jax
import jax.numpy as jnp
import numpy as np
from jax import lax
from jax.experimental import pallas as pl
from jax.experimental.pallas import tpu as pltpu
from jax.sharding import PartitionSpec as P


NY = 8
NZ = 16
CELLS = NY * NZ
PAD = 16
BLOCK = 9 * PAD
DEPTH = 256
SIZES = (8,8,)
SKEW = 1
SHIFTS = [(b, d) for b in (-1, 0, 1) for d in (-1, 0, 1)]
TWO_PI = 6.283185307179586
VMEM = pl.BlockSpec(memory_space=pltpu.VMEM)
SMEM = pl.BlockSpec(memory_space=pltpu.SMEM)
HBM = pl.BlockSpec(memory_space=pltpu.MemorySpace.HBM)
shape = jax.ShapeDtypeStruct
f32, bf16 = jnp.float32, jnp.bfloat16

call = functools.partial(pl.pallas_call, compiler_params=pltpu.CompilerParams(vmem_limit_bytes=16 << 20))
dot = functools.partial(jnp.dot, preferred_element_type=jnp.float32)


def split(values):
    high = values.astype(bf16)
    return high, (values - high.astype(f32)).astype(bf16)


def left_terms(values):
    high, low = split(values)
    return jnp.concatenate([high, high, low], axis=1)


def close_dot(left, values):
    high, low = split(values)
    return dot(left, jnp.concatenate([high, low, high]))


def in_hbm(value):
    return pltpu.with_memory_space_constraint(value, pltpu.MemorySpace.HBM)


def roll(values, amount):
    amount = amount % CELLS
    return values if amount == 0 else pltpu.roll(values, amount, 1)


def shift_y(values, step):
    return roll(values, -step * NZ)


def shift_z(values, step, inner):
    if step == 0:
        return values
    edge = NZ - 1 if step == 1 else 0
    return jnp.where(inner == edge, roll(values, step * (NZ - 1)), roll(values, -step))


def z_index(rows):
    return lax.broadcasted_iota(jnp.int32, (rows, CELLS), 1) % NZ


def round_kernel(*refs):
    count = (len(refs) - 2) // 2
    sources, rounded_ref, targets, semaphores = refs[:count], refs[count], refs[count + 1 : -1], refs[-1]
    copies = [pltpu.make_async_copy(a, b, semaphores.at[i]) for i, (a, b) in enumerate(zip(sources, targets))]
    for copy in copies:
        copy.start()
    copies[0].wait()
    rounded_ref[...] = targets[0][...].astype(bf16)
    for copy in copies[1:]:
        copy.wait()


def setup_kernel(
    coords, beads, masses_hbm, step_hbm, cycle_hbm, p_hbm, modes_hbm, modes_t_hbm, vectors_hbm,
    q_ref, one_ref, bias_one_ref, bias_two_ref, readout_ref, two_ref,
    forward_ref, outer_forward_ref, backward_ref, two_t_ref, wide_ref,
    q_base_ref, q_map_ref, p_base_ref, pushed_ref, cosine_ref, finish_ref, half_ref,
    modes_ref, modes_t_ref, vectors_ref, rows, masses_ref, step_ref, cycle_ref, p_ref, semaphores
):
    moves = (
        (masses_hbm, masses_ref), (step_hbm, step_ref), (cycle_hbm, cycle_ref), (p_hbm, p_ref),
        (modes_hbm, modes_ref), (modes_t_hbm, modes_t_ref), (vectors_hbm, vectors_ref),
    )
    copies = [pltpu.make_async_copy(a, b, semaphores.at[i]) for i, (a, b) in enumerate(moves)]
    for copy in copies:
        copy.start()
    is_odd = lax.axis_index("space") % 2 == 1
    hidden = one_ref.shape[1]
    rows[: one_ref.shape[0], :] = one_ref[...].astype(f32)
    rows[one_ref.shape[0] :, :] = jnp.zeros((rows.shape[0] - one_ref.shape[0], hidden), f32)
    at = lax.broadcasted_iota(jnp.int32, (PAD, hidden), 0)
    real = at < coords
    rest = bias_one_ref[...]
    turned = []
    for along_x in range(3):
        for o in range(9):
            even, odd = ((a * 9 + o) * coords for a in (along_x, 2 - along_x))
            taken = rows[even : even + PAD, :]
            if odd != even:
                taken = jnp.where(is_odd, rows[odd : odd + PAD, :], taken)
            taken = jnp.where(real, taken, 0.0)
            top = (along_x * 9 + o) * PAD
            backward_ref[top : top + PAD, :] = taken.astype(bf16)
            if along_x == 0 and o < 3:
                term = rest.astype(bf16).astype(f32)
                rest = rest - term
                taken = jnp.where(real, taken, jnp.broadcast_to(term, taken.shape))
                taken = jnp.where(at <= coords, taken, 0.0)
            turned.append(taken)
    forward = jnp.concatenate(turned).T.astype(bf16)
    forward_ref[...] = forward
    outer_forward_ref[...] = jnp.concatenate([forward[:, BLOCK:], forward[:, :BLOCK]], axis=1)
    two_t_ref[...] = two_ref[...].astype(f32).T.astype(bf16)
    columns = jnp.concatenate([bias_two_ref[...], readout_ref[...], jnp.zeros((6, hidden), f32)]).T
    for i in range(2):
        wide_ref[i] = jnp.broadcast_to(columns[:, i : i + 1], (hidden, CELLS))

    for copy in copies:
        copy.wait()
    total = coords * beads
    order = lax.broadcasted_iota(jnp.int32, (beads, CELLS), 0).astype(f32)
    mass = jnp.concatenate([jnp.full((beads, CELLS), masses_ref[c], f32) for c in range(coords)])
    step = step_ref[0]
    half = 0.5 * step
    frequency = 2.0 * cycle_ref[0] * jnp.sin(order * (0.5 * TWO_PI / beads))
    phase = frequency * step
    sine = jnp.sin(phase)
    ratio = jnp.where(order == 0, 1.0, sine / jnp.where(order == 0, 1.0, phase))
    cosine, drift, spring = (
        jnp.concatenate([term] * coords) for term in (jnp.cos(phase), step * ratio, frequency * sine)
    )
    drift, spring = drift / mass, mass * spring
    mode = close_dot(modes_t_ref[...], jnp.concatenate([q_ref[...], p_ref[...]], axis=1))
    mode_q, mode_p = mode[:, :CELLS], mode[:, CELLS:]
    moved = cosine * mode_q + drift * mode_p
    pushed = cosine * mode_p - spring * mode_q
    base = close_dot(modes_ref[...], jnp.concatenate([moved, pushed], axis=1))
    q_base_ref[...] = base[:, :CELLS]
    p_base_ref[...] = base[:, CELLS:]
    pushed_ref[...] = pushed
    cosine_ref[...] = cosine
    modes_t = modes_t_ref[:, :total].astype(f32) + modes_t_ref[:, 2 * total :].astype(f32)
    q_map_ref[...] = left_terms(close_dot(modes_ref[...], (half * drift[:, :1]) * modes_t))
    finish_ref[...] = jnp.concatenate([half / mass, 1.0 / mass], axis=1)
    half_ref[...] = jnp.full(half_ref.shape, half, f32)


def put_features(coords, beads, chosen, stage, features, top):
    filler = jnp.ones((PAD - coords, CELLS), f32)
    inner_z = z_index(PAD)
    for j in chosen:
        plane = jnp.concatenate([stage[pl.ds(j, coords, stride=beads), :], filler]).astype(bf16)
        along = {d: shift_z(plane, d, inner_z) for d in (-1, 0, 1)}
        for o, (b, d) in enumerate(SHIFTS):
            first = top + o * PAD
            features[first : first + PAD, j * CELLS : (j + 1) * CELLS] = shift_y(along[d], b)


def groups_of(beads):
    sizes = SIZES if sum(SIZES) == beads else (beads,)
    starts = np.cumsum((0,) + sizes)
    return [range(int(first), int(first) + size) for first, size in zip(starts, sizes)]


def columns_of(chosen):
    return slice(chosen[0] * CELLS, (chosen[-1] + 1) * CELLS)


def run_skewed(groups, stages):
    state = [() for _ in groups]
    order = sorted((SKEW * g + s, -s, g) for g in range(len(groups)) for s in range(len(stages)))
    for _, s, g in order:
        state[g] = stages[-s](groups[g], *state[g])


def back_stages(two_ref, two_t_ref, wide_ref):
    def second(chosen, first):
        bias, readout = (jnp.concatenate([wide_ref[i]] * len(chosen), axis=1) for i in range(2))
        hidden = jnp.tanh(first).astype(bf16)
        second = jnp.tanh(dot(two_ref[...], hidden) + bias)
        return hidden, (readout * (1.0 - second * second)).astype(bf16)

    def third(chosen, hidden, back):
        widened = hidden.astype(f32)
        return ((dot(two_t_ref[...], back) * (1.0 - widened * widened)).astype(bf16),)

    return second, third


def shifted_sum(sums, at):
    inner_z = z_index(PAD)
    total = None
    for d in (-1, 0, 1):
        part = None
        for b in (-1, 0, 1):
            o = (b + 1) * 3 + d + 1
            moved = shift_y(sums[o * PAD : (o + 1) * PAD, at * CELLS : (at + 1) * CELLS], -b)
            part = moved if part is None else part + moved
        part = shift_z(part, -d, inner_z)
        total = part if total is None else total + part
    return total


def own_kernel(
    coords, beads, tied, outer_ref, own_ref, inner_ref, forward_ref, backward_ref, two_ref, two_t_ref, wide_ref, *refs
):
    sent_ref, kept_ref, features, stage = refs[tied:]
    for place, ref in enumerate((outer_ref, own_ref, inner_ref)):
        stage[place] = ref[...].astype(f32)

    def put(chosen):
        for place in range(3):
            put_features(coords, beads, chosen, stage.at[place], features, place * BLOCK)
        return ()

    def first(chosen):
        return (dot(forward_ref[...], features[:, columns_of(chosen)]),)

    def last(chosen, back):
        return (dot(backward_ref[BLOCK:], back),)

    def store(chosen, sums):
        for at, j in enumerate(chosen):
            rows = pl.ds(j, coords, stride=beads)
            kept_ref[rows, :] = shifted_sum(sums[:BLOCK], at)[:coords]
            sent_ref[rows, :] = shifted_sum(sums[BLOCK:], at)[:coords]

    run_skewed(groups_of(beads), (put, first, *back_stages(two_ref, two_t_ref, wide_ref), last, store))


def outer_kernel(
    coords, beads, outer2_ref, features_ref, kept_in_ref, forward_ref, backward_ref, two_ref, two_t_ref, wide_ref,
    kept_ref, features, stage
):
    extra = 2 * BLOCK - DEPTH
    stage[...] = outer2_ref[...].astype(f32)

    def put(chosen):
        put_features(coords, beads, chosen, stage, features, extra)
        features[:extra, columns_of(chosen)] = features_ref[DEPTH : 2 * BLOCK, columns_of(chosen)]
        return ()

    def first(chosen):
        near = dot(forward_ref[:, :DEPTH], features_ref[:DEPTH, columns_of(chosen)])
        return (near + dot(forward_ref[:, DEPTH:], features[:, columns_of(chosen)]),)

    def last(chosen, back):
        return (dot(backward_ref[2 * BLOCK :], back),)

    def store(chosen, sums):
        for at, j in enumerate(chosen):
            rows = pl.ds(j, coords, stride=beads)
            kept_ref[rows, :] = kept_in_ref[rows, :] + shifted_sum(sums, at)[:coords]

    run_skewed(groups_of(beads), (put, first, *back_stages(two_ref, two_t_ref, wide_ref), last, store))


def move_kernel(q_base_ref, q_map_ref, kept_ref, came_ref, q_out, rounded_out, sum_out):
    sums = kept_ref[...] + came_ref[...]
    q = q_base_ref[...] - close_dot(q_map_ref[...], sums)
    rounded_out[...] = q.astype(bf16)
    q_out[...] = q
    sum_out[...] = sums


def push_kernel(
    share, planes_at, half_ref, q_ref, sum_ref, p_base_ref, pushed_ref, cosine_ref, finish_ref, modes_ref,
    modes_t_ref, vectors_ref, q_out, p_out, velocity_out, velocity_map_out, planes_out, cells_out
):
    total = modes_ref.shape[0]
    q_out[...] = q_ref[...]
    kick = cosine_ref[...] * close_dot(modes_t_ref[...], half_ref[0:1, :] * sum_ref[...])
    p_out[...] = p_base_ref[...] - close_dot(modes_ref[...], kick)
    velocity_out[...] = (pushed_ref[...] - kick) * finish_ref[:, CELLS:]
    modes_t = modes_t_ref[:, :total].astype(f32) + modes_t_ref[:, 2 * total :].astype(f32)
    velocity_map_out[...] = left_terms(finish_ref[:, :1] * modes_t)
    extent_x = len(planes_at)
    whole = extent_x * CELLS
    here = lax.axis_index("space")
    if vectors_ref.shape[1] == share:
        vectors = vectors_ref[...]
    else:
        vectors = vectors_ref[:, pl.ds(pl.multiple_of(here * share, CELLS), share)]
    cell = lax.broadcasted_iota(jnp.int32, (CELLS, share), 0)
    along = vectors[1:2] * ((cell // NZ) * (extent_x * NZ)) + vectors[2:3] * ((cell % NZ) * (extent_x * NY))
    across = jnp.concatenate([vectors[0:1] * ((here ^ at) * CELLS) for at in planes_at])
    for numerator, out in ((across, planes_out), (along, cells_out)):
        angle = TWO_PI * (numerator & (whole - 1)).astype(f32) / whole
        out[0] = jnp.cos(angle)
        out[1] = jnp.sin(angle)


def finish_kernel(half_ref, velocity_ref, map_ref, kept_ref, came_ref, velocity_out, kick_out):
    sums = kept_ref[...] + came_ref[...]
    velocity_out[...] = (velocity_ref[...] - close_dot(map_ref[...], sums)).astype(bf16)
    kick_out[...] = half_ref[0:1, :] * sums


def projected(velocity_ref, planes_ref, cells_ref, first, part):
    cos_cell, sin_cell = cells_ref[0], cells_ref[1]

    def trig(i):
        cos_plane, sin_plane = (planes_ref[t, first + i : first + i + 1, :] for t in range(2))
        if part == 0:
            return (cos_plane * cos_cell - sin_plane * sin_cell).astype(bf16)
        return (sin_plane * cos_cell + cos_plane * sin_cell).astype(bf16)

    total = 0.0
    for i in range(0, velocity_ref.shape[0] - 1, 2):
        block = jnp.concatenate([velocity_ref[i], velocity_ref[i + 1]], axis=1)
        total += dot(block, jnp.concatenate([trig(i), trig(i + 1)]))
    if velocity_ref.shape[0] % 2:
        total += dot(velocity_ref[velocity_ref.shape[0] - 1], trig(velocity_ref.shape[0] - 1))
    return total


def near_project_kernel(velocity_ref, planes_ref, cells_ref, out_ref):
    fields = velocity_ref.shape[1]
    for part in range(2):
        out_ref[part * fields : (part + 1) * fields, :] = projected(velocity_ref, planes_ref, cells_ref, 0, part)


def project_kernel(scale, near_ref, velocity_ref, planes_ref, cells_ref, out_hbm, result, semaphores):
    count, fields, _ = velocity_ref.shape
    copies = []
    for part in range(2):
        rows = slice(part * fields, (part + 1) * fields)
        result[rows, :] = (near_ref[rows, :] + projected(velocity_ref, planes_ref, cells_ref, count, part)) * scale
        copies.append(pltpu.make_async_copy(result.at[rows, :], out_hbm.at[rows, :], semaphores.at[part]))
        copies[-1].start()
    for copy in copies:
        copy.wait()


def mode_matrix(coords, beads):
    j = np.arange(beads)[:, None]
    k = np.arange(beads)[None, :]
    angles = 2.0 * np.pi * ((j * k) % beads) / beads
    edge = np.cos(angles) / math.sqrt(beads)
    inside = np.where(k < beads // 2, np.cos(angles), np.sin(angles)) * math.sqrt(2.0 / beads)
    matrix = np.where((k == 0) | (k == beads // 2), edge, inside)
    modes = np.einsum("ab,jk->ajbk", np.eye(coords), matrix).reshape(coords * beads, coords * beads)
    return modes.astype(np.float32)


def constant_terms(matrix):
    high = matrix.astype(jnp.bfloat16)
    low = (matrix - high.astype(np.float32)).astype(jnp.bfloat16)
    return jnp.asarray(np.concatenate([high, high, low], axis=1))


def swap(value, distance):
    return lax.ppermute(value, "space", [(i, i ^ distance) for i in range(lax.axis_size("space"))])


def neighbour_planes(plane):
    count = lax.axis_size("space")
    step = [1 if i % 2 else -1 for i in range(count)]
    outer = lax.ppermute(plane, "space", [(i, (i + step[i]) % count) for i in range(count)])
    inner = swap(plane, 1)
    outer2 = lax.ppermute(plane, "space", [(i, (i - 2 * step[i]) % count) for i in range(count)])
    return outer2, outer, inner


def gather_order(count):
    order, distance = [0], count // 2
    while distance:
        if distance == 4:
            order, distance = [i ^ d for d in (0, 2, 4, 6) for i in order], 1
        else:
            order, distance = [i ^ d for d in (0, distance) for i in order], distance // 2
    return order


def gather_planes(velocity):
    held, distance = velocity[None], lax.axis_size("space") // 2
    while distance > 1:
        if distance == 4:
            near, far = swap(held, 2), swap(held, 4)
            held, distance = jnp.concatenate([held, near, far, swap(near, 4)]), 1
        else:
            held, distance = jnp.concatenate([held, swap(held, distance)]), distance // 2
    return held, swap(held, 1)


def on_device(
    positions, momenta, masses, step_size, cycle_frequency,
    layer_one, bias_one, layer_two, bias_two, readout, wavevectors
):
    coords, beads, planes, cells = positions.shape
    devices = lax.axis_size("space")
    assert planes == 1 and cells == CELLS and devices & (devices - 1) == 0 and devices > 1
    total = coords * beads
    hidden = layer_one.shape[0]
    width = 27 * PAD
    field, narrow = shape((total, CELLS), f32), shape((total, CELLS), bf16)
    square = shape((total, 3 * total), bf16)

    modes = mode_matrix(coords, beads)
    share = wavevectors.shape[1] // devices
    if share % CELLS:
        wavevectors = lax.dynamic_slice_in_dim(wavevectors, lax.axis_index("space") * share, share, 1)
    inputs = (
        positions.reshape(total, CELLS), layer_one.T, bias_one.reshape(1, hidden), bias_two.reshape(1, hidden),
        readout.reshape(1, hidden), layer_two,
    )
    rounded, *brought = call(
        round_kernel, out_shape=(narrow,) + tuple(shape(x.shape, x.dtype) for x in inputs),
        in_specs=[HBM] * 6, out_specs=(VMEM,) * 7, scratch_shapes=[pltpu.SemaphoreType.DMA((6,))],
    )(*map(in_hbm, inputs))
    two = brought[-1]

    inputs = (momenta.reshape(total, CELLS), constant_terms(modes), constant_terms(modes.T), wavevectors)
    (
        forward, outer_forward, backward, two_t, wide, q_base, q_map, p_base, pushed, cosine, finish, half,
        modes, modes_t, wavevectors
    ) = call(
        functools.partial(setup_kernel, coords, beads),
        out_shape=(
            shape((hidden, width), bf16), shape((hidden, width), bf16), shape((width, hidden), bf16),
            shape((hidden, hidden), bf16), shape((2, hidden, CELLS), f32),
            field, square, field, field, field, shape((total, 2 * CELLS), f32), shape((8, CELLS), f32),
        ) + tuple(shape(x.shape, x.dtype) for x in inputs[1:]),
        in_specs=[HBM] * 7 + [VMEM] * 6, out_specs=(VMEM,) * 15,
        scratch_shapes=[
            pltpu.VMEM((width, hidden), f32), pltpu.SMEM((coords,), f32), pltpu.SMEM((1,), f32),
            pltpu.SMEM((1,), f32), pltpu.VMEM((total, CELLS), f32), pltpu.SemaphoreType.DMA((7,)),
        ],
    )(in_hbm(masses), step_size, cycle_frequency, *map(in_hbm, inputs), *brought)
    layers = (backward, two, two_t, wide)
    stage = pltpu.VMEM((total, CELLS), f32)

    def forces(plane, *tied):
        outer2, outer, inner = neighbour_planes(plane)
        sent, kept, features = call(
            functools.partial(own_kernel, coords, beads, len(tied)),
            out_shape=(field, field, shape((width, beads * CELLS), bf16)),
            in_specs=[VMEM] * (8 + len(tied)), out_specs=(VMEM,) * 3, scratch_shapes=[pltpu.VMEM((3, total, CELLS), f32)],
        )(outer, plane, inner, forward, *layers, *tied)
        came = swap(sent, 1)
        kept = call(
            functools.partial(outer_kernel, coords, beads),
            out_shape=field, in_specs=[VMEM] * 8, out_specs=VMEM,
            scratch_shapes=[pltpu.VMEM((width - DEPTH, beads * CELLS), bf16), stage],
        )(outer2, features, kept, outer_forward, *layers)
        return kept, came

    q_moved, rounded, sums = call(
        move_kernel, out_shape=(field, narrow, field), in_specs=[VMEM] * 4, out_specs=(VMEM,) * 3,
    )(q_base, q_map, *forces(rounded))
    order = gather_order(devices)
    q_new, p_mid, velocity_base, velocity_map, across, along = call(
        functools.partial(push_kernel, share, order),
        out_shape=(
            field, field, field, square, shape((2, devices, share), f32), shape((2, CELLS, share), f32),
        ),
        in_specs=[VMEM] * 10, out_specs=(VMEM,) * 6,
    )(half, q_moved, sums, p_base, pushed, cosine, finish, modes, modes_t, wavevectors)
    velocity, kick = call(
        finish_kernel, out_shape=(narrow, field), in_specs=[VMEM] * 5, out_specs=(VMEM,) * 2,
    )(half, velocity_base, velocity_map, *forces(rounded))
    p_new = p_mid - kick
    held, last = gather_planes(velocity)
    spectrum = shape((2 * total, share), f32)
    near = call(near_project_kernel, out_shape=spectrum, in_specs=[VMEM] * 3, out_specs=VMEM)(held, across, along)
    spectrum = call(
        functools.partial(project_kernel, 1.0 / math.sqrt(devices * CELLS)),
        out_shape=spectrum, in_specs=[VMEM] * 4, out_specs=HBM,
        scratch_shapes=[pltpu.VMEM((2 * total, share), f32), pltpu.SemaphoreType.DMA((2,))],
    )(near, last, across, along)
    return q_new.reshape(positions.shape), p_new.reshape(momenta.shape), spectrum.T


def solution(mesh):
    field = P(None, None, ("rep", "space"), None)

    return jax.shard_map(
        on_device,
        mesh=mesh,
        in_specs=(field, field) + (P(),) * 9,
        out_specs=(field, field, P(("rep", "space"), None)),
        check_vma=False,
    )
```

```python
import functools
import math

import jax
import jax.numpy as jnp
import numpy as np
from jax import lax
from jax.experimental import pallas as pl
from jax.experimental.pallas import tpu as pltpu
from jax.sharding import PartitionSpec as P


NY = 8
NZ = 16
CELLS = NY * NZ
PAD = 16
BLOCK = 9 * PAD
DEPTH = 256
SIZES = (8,8,)
SKEW = 1
SHIFTS = [(b, d) for b in (-1, 0, 1) for d in (-1, 0, 1)]
TWO_PI = 6.283185307179586
VMEM = pl.BlockSpec(memory_space=pltpu.VMEM)
SMEM = pl.BlockSpec(memory_space=pltpu.SMEM)
HBM = pl.BlockSpec(memory_space=pltpu.MemorySpace.HBM)
shape = jax.ShapeDtypeStruct
f32, bf16 = jnp.float32, jnp.bfloat16

call = functools.partial(pl.pallas_call, compiler_params=pltpu.CompilerParams(vmem_limit_bytes=16 << 20))
dot = functools.partial(jnp.dot, preferred_element_type=jnp.float32)


def split(values):
    high = values.astype(bf16)
    return high, (values - high.astype(f32)).astype(bf16)


def left_terms(values):
    high, low = split(values)
    return jnp.concatenate([high, high, low], axis=1)


def close_dot(left, values):
    high, low = split(values)
    rest = jnp.zeros((left.shape[1] // 3 - values.shape[0], values.shape[1]), bf16)
    return dot(left, jnp.concatenate([high, rest, low, rest, high, rest]))


def in_hbm(value):
    return pltpu.with_memory_space_constraint(value, pltpu.MemorySpace.HBM)


def roll(values, amount):
    amount = amount % CELLS
    return values if amount == 0 else pltpu.roll(values, amount, 1)


def shift_y(values, step):
    return roll(values, -step * NZ)


def shift_z(values, step, inner):
    if step == 0:
        return values
    edge = NZ - 1 if step == 1 else 0
    return jnp.where(inner == edge, roll(values, step * (NZ - 1)), roll(values, -step))


def z_index(rows):
    return lax.broadcasted_iota(jnp.int32, (rows, CELLS), 1) % NZ


def round_kernel(*refs):
    count = (len(refs) - 2) // 2
    sources, rounded_ref, targets, semaphores = refs[:count], refs[count], refs[count + 1 : -1], refs[-1]
    copies = [pltpu.make_async_copy(a, b, semaphores.at[i]) for i, (a, b) in enumerate(zip(sources, targets))]
    for copy in copies:
        copy.start()
    copies[0].wait()
    rounded_ref[...] = targets[0][...].astype(bf16)
    for copy in copies[1:]:
        copy.wait()


def setup_kernel(
    coords, beads, masses_hbm, step_hbm, cycle_hbm, p_hbm, blocks_hbm, vectors_hbm,
    q_ref, one_ref, bias_one_ref, bias_two_ref, readout_ref, two_ref,
    forward_ref, outer_forward_ref, backward_ref, two_t_ref, wide_ref,
    q_base_ref, q_map_ref, p_base_ref, pushed_ref, cosine_ref, finish_ref, half_ref,
    modes_ref, modes_t_ref, vectors_ref, rows, masses_ref, step_ref, cycle_ref, p_ref, blocks_ref, semaphores
):
    moves = (
        (blocks_hbm, blocks_ref), (p_hbm, p_ref), (masses_hbm, masses_ref), (step_hbm, step_ref),
        (cycle_hbm, cycle_ref), (vectors_hbm, vectors_ref),
    )
    copies = [pltpu.make_async_copy(a, b, semaphores.at[i]) for i, (a, b) in enumerate(moves)]
    for copy in copies:
        copy.start()
    is_odd = lax.axis_index("space") % 2 == 1
    hidden = one_ref.shape[1]
    rows[: one_ref.shape[0], :] = one_ref[...].astype(f32)
    rows[one_ref.shape[0] :, :] = jnp.zeros((rows.shape[0] - one_ref.shape[0], hidden), f32)
    at = lax.broadcasted_iota(jnp.int32, (PAD, hidden), 0)
    real = at < coords
    rest = bias_one_ref[...]
    turned = []
    for along_x in range(3):
        for o in range(9):
            even, odd = ((a * 9 + o) * coords for a in (along_x, 2 - along_x))
            taken = rows[even : even + PAD, :]
            if odd != even:
                taken = jnp.where(is_odd, rows[odd : odd + PAD, :], taken)
            taken = jnp.where(real, taken, 0.0)
            top = (along_x * 9 + o) * PAD
            backward_ref[top : top + PAD, :] = taken.astype(bf16)
            if along_x == 0 and o < 3:
                term = rest.astype(bf16).astype(f32)
                rest = rest - term
                taken = jnp.where(real, taken, jnp.broadcast_to(term, taken.shape))
                taken = jnp.where(at <= coords, taken, 0.0)
            turned.append(taken)
    forward = jnp.concatenate(turned).T.astype(bf16)
    forward_ref[...] = forward
    outer_forward_ref[...] = jnp.concatenate([forward[:, BLOCK:], forward[:, :BLOCK]], axis=1)
    two_t_ref[...] = two_ref[...].astype(f32).T.astype(bf16)
    columns = jnp.concatenate([bias_two_ref[...], readout_ref[...], jnp.zeros((6, hidden), f32)]).T
    for i in range(2):
        wide_ref[i] = jnp.broadcast_to(columns[:, i : i + 1], (hidden, CELLS))

    for copy in copies[:-1]:
        copy.wait()
    depth = blocks_ref.shape[1]
    column = lax.broadcasted_iota(jnp.int32, (beads, depth), 1) // beads
    for matrix_ref, first in ((modes_ref, 0), (modes_t_ref, 2 * beads)):
        high, low = blocks_ref[first : first + beads, :], blocks_ref[first + beads : first + 2 * beads, :]
        for c in range(coords):
            rows_at = slice(c * beads, (c + 1) * beads)
            mine = jnp.where(column == c, high, 0.0).astype(bf16)
            rest = jnp.where(column == c, low, 0.0).astype(bf16)
            matrix_ref[rows_at, :] = jnp.concatenate([mine, mine, rest], axis=1)
    order = lax.broadcasted_iota(jnp.int32, (beads, CELLS), 0).astype(f32)
    mass = jnp.concatenate([jnp.full((beads, CELLS), masses_ref[c], f32) for c in range(coords)])
    step = step_ref[0]
    half = 0.5 * step
    frequency = 2.0 * cycle_ref[0] * jnp.sin(order * (0.5 * TWO_PI / beads))
    phase = frequency * step
    sine = jnp.sin(phase)
    ratio = jnp.where(order == 0, 1.0, sine / jnp.where(order == 0, 1.0, phase))
    cosine, drift, spring = (
        jnp.concatenate([term] * coords) for term in (jnp.cos(phase), step * ratio, frequency * sine)
    )
    drift, spring = drift / mass, mass * spring
    mode = close_dot(modes_t_ref[...], jnp.concatenate([q_ref[...], p_ref[...]], axis=1))
    mode_q, mode_p = mode[:, :CELLS], mode[:, CELLS:]
    moved = cosine * mode_q + drift * mode_p
    pushed = cosine * mode_p - spring * mode_q
    base = close_dot(modes_ref[...], jnp.concatenate([moved, pushed], axis=1))
    q_base_ref[...] = base[:, :CELLS]
    p_base_ref[...] = base[:, CELLS:]
    pushed_ref[...] = pushed
    cosine_ref[...] = cosine
    modes_t = modes_t_ref[:, :depth].astype(f32) + modes_t_ref[:, 2 * depth :].astype(f32)
    q_map_ref[...] = left_terms(close_dot(modes_ref[...], (half * drift[:, :1]) * modes_t))
    finish_ref[...] = jnp.concatenate([half / mass, 1.0 / mass], axis=1)
    half_ref[...] = jnp.full(half_ref.shape, half, f32)
    copies[-1].wait()


def put_features(coords, beads, chosen, stage, features, top):
    filler = jnp.ones((PAD - coords, CELLS), f32)
    inner_z = z_index(PAD)
    for j in chosen:
        plane = jnp.concatenate([stage[pl.ds(j, coords, stride=beads), :], filler]).astype(bf16)
        along = {d: shift_z(plane, d, inner_z) for d in (-1, 0, 1)}
        for o, (b, d) in enumerate(SHIFTS):
            first = top + o * PAD
            features[first : first + PAD, j * CELLS : (j + 1) * CELLS] = shift_y(along[d], b)


def groups_of(beads):
    sizes = SIZES if sum(SIZES) == beads else (beads,)
    starts = np.cumsum((0,) + sizes)
    return [range(int(first), int(first) + size) for first, size in zip(starts, sizes)]


def columns_of(chosen):
    return slice(chosen[0] * CELLS, (chosen[-1] + 1) * CELLS)


def run_skewed(groups, stages):
    state = [() for _ in groups]
    order = sorted((SKEW * g + s, -s, g) for g in range(len(groups)) for s in range(len(stages)))
    for _, s, g in order:
        state[g] = stages[-s](groups[g], *state[g])


def back_stages(two_ref, two_t_ref, wide_ref):
    def second(chosen, first):
        bias, readout = (jnp.concatenate([wide_ref[i]] * len(chosen), axis=1) for i in range(2))
        hidden = jnp.tanh(first).astype(bf16)
        second = jnp.tanh(dot(two_ref[...], hidden) + bias)
        return hidden, (readout * (1.0 - second * second)).astype(bf16)

    def third(chosen, hidden, back):
        widened = hidden.astype(f32)
        return ((dot(two_t_ref[...], back) * (1.0 - widened * widened)).astype(bf16),)

    return second, third


def shifted_sum(sums, at):
    inner_z = z_index(PAD)
    total = None
    for d in (-1, 0, 1):
        part = None
        for b in (-1, 0, 1):
            o = (b + 1) * 3 + d + 1
            moved = shift_y(sums[o * PAD : (o + 1) * PAD, at * CELLS : (at + 1) * CELLS], -b)
            part = moved if part is None else part + moved
        part = shift_z(part, -d, inner_z)
        total = part if total is None else total + part
    return total


def own_kernel(
    coords, beads, tied, outer_ref, own_ref, inner_ref, forward_ref, backward_ref, two_ref, two_t_ref, wide_ref, *refs
):
    sent_ref, sums_ref, features, stage = refs[tied:]
    for place, ref in enumerate((outer_ref, own_ref, inner_ref)):
        stage[place] = ref[...].astype(f32)

    def put(chosen):
        for place in range(3):
            put_features(coords, beads, chosen, stage.at[place], features, place * BLOCK)
        return ()

    def first(chosen):
        return (dot(forward_ref[...], features[:, columns_of(chosen)]),)

    def last(chosen, back):
        sums = dot(backward_ref[BLOCK:], back)
        sums_ref[:, columns_of(chosen)] = sums[:BLOCK]
        return (sums,)

    def store(chosen, sums):
        for at, j in enumerate(chosen):
            rows = pl.ds(j, coords, stride=beads)
            sent_ref[rows, :] = shifted_sum(sums[BLOCK:], at)[:coords]

    run_skewed(groups_of(beads), (put, first, *back_stages(two_ref, two_t_ref, wide_ref), last, store))


def outer_kernel(
    coords, beads, outer2_ref, features_ref, sums_ref, forward_ref, backward_ref, two_ref, two_t_ref, wide_ref,
    kept_ref, features, stage
):
    extra = 2 * BLOCK - DEPTH
    stage[...] = outer2_ref[...].astype(f32)

    def put(chosen):
        put_features(coords, beads, chosen, stage, features, extra)
        features[:extra, columns_of(chosen)] = features_ref[DEPTH : 2 * BLOCK, columns_of(chosen)]
        return ()

    def first(chosen):
        near = dot(forward_ref[:, :DEPTH], features_ref[:DEPTH, columns_of(chosen)])
        return (near + dot(forward_ref[:, DEPTH:], features[:, columns_of(chosen)]),)

    def last(chosen, back):
        return (dot(backward_ref[2 * BLOCK :], back) + sums_ref[:, columns_of(chosen)],)

    def store(chosen, sums):
        for at, j in enumerate(chosen):
            rows = pl.ds(j, coords, stride=beads)
            kept_ref[rows, :] = shifted_sum(sums, at)[:coords]

    run_skewed(groups_of(beads), (put, first, *back_stages(two_ref, two_t_ref, wide_ref), last, store))


def move_kernel(q_base_ref, q_map_ref, kept_ref, came_ref, q_out, rounded_out, sum_out):
    sums = kept_ref[...] + came_ref[...]
    q = q_base_ref[...] - close_dot(q_map_ref[...], sums)
    rounded_out[...] = q.astype(bf16)
    q_out[...] = q
    sum_out[...] = sums


def push_kernel(
    share, planes_at, half_ref, q_ref, sum_ref, p_base_ref, pushed_ref, cosine_ref, finish_ref, modes_ref,
    modes_t_ref, vectors_ref, q_out, p_out, velocity_out, velocity_map_out, planes_out, cells_out
):
    depth = modes_ref.shape[1] // 3
    q_out[...] = q_ref[...]
    kick = cosine_ref[...] * close_dot(modes_t_ref[...], half_ref[0:1, :] * sum_ref[...])
    p_out[...] = p_base_ref[...] - close_dot(modes_ref[...], kick)
    velocity_out[...] = (pushed_ref[...] - kick) * finish_ref[:, CELLS:]
    modes_t = modes_t_ref[:, :depth].astype(f32) + modes_t_ref[:, 2 * depth :].astype(f32)
    velocity_map_out[...] = left_terms(finish_ref[:, :1] * modes_t)
    extent_x = len(planes_at)
    whole = extent_x * CELLS
    here = lax.axis_index("space")
    if vectors_ref.shape[1] == share:
        vectors = vectors_ref[...]
    else:
        vectors = vectors_ref[:, pl.ds(pl.multiple_of(here * share, CELLS), share)]
    cell = lax.broadcasted_iota(jnp.int32, (CELLS, share), 0)
    along = vectors[1:2] * ((cell // NZ) * (extent_x * NZ)) + vectors[2:3] * ((cell % NZ) * (extent_x * NY))
    across = jnp.concatenate([vectors[0:1] * ((here ^ at) * CELLS) for at in planes_at])
    for numerator, out in ((across, planes_out), (along, cells_out)):
        angle = TWO_PI * (numerator & (whole - 1)).astype(f32) / whole
        out[0] = jnp.cos(angle)
        out[1] = jnp.sin(angle)


def finish_kernel(half_ref, velocity_ref, map_ref, kept_ref, came_ref, velocity_out, kick_out):
    sums = kept_ref[...] + came_ref[...]
    velocity_out[...] = (velocity_ref[...] - close_dot(map_ref[...], sums)).astype(bf16)
    kick_out[...] = half_ref[0:1, :] * sums


def projected(velocity_ref, planes_ref, cells_ref, first, part):
    cos_cell, sin_cell = cells_ref[0], cells_ref[1]

    def trig(i):
        cos_plane, sin_plane = (planes_ref[t, first + i : first + i + 1, :] for t in range(2))
        if part == 0:
            return (cos_plane * cos_cell - sin_plane * sin_cell).astype(bf16)
        return (sin_plane * cos_cell + cos_plane * sin_cell).astype(bf16)

    total = 0.0
    for i in range(0, velocity_ref.shape[0] - 1, 2):
        block = jnp.concatenate([velocity_ref[i], velocity_ref[i + 1]], axis=1)
        total += dot(block, jnp.concatenate([trig(i), trig(i + 1)]))
    if velocity_ref.shape[0] % 2:
        total += dot(velocity_ref[velocity_ref.shape[0] - 1], trig(velocity_ref.shape[0] - 1))
    return total


def near_project_kernel(velocity_ref, planes_ref, cells_ref, out_ref):
    fields = velocity_ref.shape[1]
    for part in range(2):
        out_ref[part * fields : (part + 1) * fields, :] = projected(velocity_ref, planes_ref, cells_ref, 0, part)


def project_kernel(scale, near_ref, velocity_ref, planes_ref, cells_ref, out_hbm, result, semaphores):
    count, fields, _ = velocity_ref.shape
    copies = []
    for part in range(2):
        rows = slice(part * fields, (part + 1) * fields)
        result[rows, :] = (near_ref[rows, :] + projected(velocity_ref, planes_ref, cells_ref, count, part)) * scale
        copies.append(pltpu.make_async_copy(result.at[rows, :], out_hbm.at[rows, :], semaphores.at[part]))
        copies[-1].start()
    for copy in copies:
        copy.wait()


def mode_blocks(coords, beads):
    j = np.arange(beads)[:, None]
    k = np.arange(beads)[None, :]
    angles = 2.0 * np.pi * ((j * k) % beads) / beads
    edge = np.cos(angles) / math.sqrt(beads)
    inside = np.where(k < beads // 2, np.cos(angles), np.sin(angles)) * math.sqrt(2.0 / beads)
    matrix = np.where((k == 0) | (k == beads // 2), edge, inside).astype(np.float32)
    high = matrix.astype(jnp.bfloat16).astype(np.float32)
    low = (matrix - high).astype(jnp.bfloat16).astype(np.float32)
    blocks = np.concatenate([np.tile(block, (1, coords)) for block in (high, low, high.T, low.T)])
    return np.pad(blocks, ((0, 0), (0, -coords * beads % CELLS)))


def swap(value, distance):
    return lax.ppermute(value, "space", [(i, i ^ distance) for i in range(lax.axis_size("space"))])


def neighbour_planes(plane):
    count = lax.axis_size("space")
    step = [1 if i % 2 else -1 for i in range(count)]
    outer = lax.ppermute(plane, "space", [(i, (i + step[i]) % count) for i in range(count)])
    inner = swap(plane, 1)
    outer2 = lax.ppermute(plane, "space", [(i, (i - 2 * step[i]) % count) for i in range(count)])
    return outer2, outer, inner


def gather_order(count):
    order, distance = [0], count // 2
    while distance:
        if distance == 4:
            order, distance = [i ^ d for d in (0, 2, 4, 6) for i in order], 1
        else:
            order, distance = [i ^ d for d in (0, distance) for i in order], distance // 2
    return order


def gather_planes(velocity):
    held, distance = velocity[None], lax.axis_size("space") // 2
    while distance > 1:
        if distance == 4:
            near, far = swap(held, 2), swap(held, 4)
            held, distance = jnp.concatenate([held, near, far, swap(near, 4)]), 1
        else:
            held, distance = jnp.concatenate([held, swap(held, distance)]), distance // 2
    return held, swap(held, 1)


def on_device(
    positions, momenta, masses, step_size, cycle_frequency,
    layer_one, bias_one, layer_two, bias_two, readout, wavevectors
):
    coords, beads, planes, cells = positions.shape
    devices = lax.axis_size("space")
    assert planes == 1 and cells == CELLS and devices & (devices - 1) == 0 and devices > 1
    total = coords * beads
    hidden = layer_one.shape[0]
    width = 27 * PAD
    field, narrow = shape((total, CELLS), f32), shape((total, CELLS), bf16)
    square = shape((total, 3 * (total + -total % CELLS)), bf16)

    share = wavevectors.shape[1] // devices
    if share % CELLS:
        wavevectors = lax.dynamic_slice_in_dim(wavevectors, lax.axis_index("space") * share, share, 1)
    inputs = (
        positions.reshape(total, CELLS), layer_one.T, bias_one.reshape(1, hidden), bias_two.reshape(1, hidden),
        readout.reshape(1, hidden), layer_two,
    )
    rounded, *brought = call(
        round_kernel, out_shape=(narrow,) + tuple(shape(x.shape, x.dtype) for x in inputs),
        in_specs=[HBM] * 6, out_specs=(VMEM,) * 7, scratch_shapes=[pltpu.SemaphoreType.DMA((6,))],
    )(*map(in_hbm, inputs))
    two = brought[-1]

    inputs = (momenta.reshape(total, CELLS), jnp.asarray(mode_blocks(coords, beads)), wavevectors)
    (
        forward, outer_forward, backward, two_t, wide, q_base, q_map, p_base, pushed, cosine, finish, half,
        modes, modes_t, wavevectors
    ) = call(
        functools.partial(setup_kernel, coords, beads),
        out_shape=(
            shape((hidden, width), bf16), shape((hidden, width), bf16), shape((width, hidden), bf16),
            shape((hidden, hidden), bf16), shape((2, hidden, CELLS), f32),
            field, square, field, field, field, shape((total, 2 * CELLS), f32), shape((8, CELLS), f32),
            square, square, shape(wavevectors.shape, wavevectors.dtype),
        ),
        in_specs=[HBM] * 6 + [VMEM] * 6, out_specs=(VMEM,) * 15,
        scratch_shapes=[
            pltpu.VMEM((width, hidden), f32), pltpu.SMEM((coords,), f32), pltpu.SMEM((1,), f32),
            pltpu.SMEM((1,), f32), pltpu.VMEM((total, CELLS), f32), pltpu.VMEM(inputs[1].shape, f32),
            pltpu.SemaphoreType.DMA((6,)),
        ],
    )(in_hbm(masses), step_size, cycle_frequency, *map(in_hbm, inputs), *brought)
    layers = (backward, two, two_t, wide)
    stage = pltpu.VMEM((total, CELLS), f32)

    def forces(plane, *tied):
        outer2, outer, inner = neighbour_planes(plane)
        sent, sums, features = call(
            functools.partial(own_kernel, coords, beads, len(tied)),
            out_shape=(field, shape((BLOCK, beads * CELLS), f32), shape((width, beads * CELLS), bf16)),
            in_specs=[VMEM] * (8 + len(tied)), out_specs=(VMEM,) * 3, scratch_shapes=[pltpu.VMEM((3, total, CELLS), f32)],
        )(outer, plane, inner, forward, *layers, *tied)
        came = swap(sent, 1)
        kept = call(
            functools.partial(outer_kernel, coords, beads),
            out_shape=field, in_specs=[VMEM] * 8, out_specs=VMEM,
            scratch_shapes=[pltpu.VMEM((width - DEPTH, beads * CELLS), bf16), stage],
        )(outer2, features, sums, outer_forward, *layers)
        return kept, came

    q_moved, rounded, sums = call(
        move_kernel, out_shape=(field, narrow, field), in_specs=[VMEM] * 4, out_specs=(VMEM,) * 3,
    )(q_base, q_map, *forces(rounded))
    order = gather_order(devices)
    q_new, p_mid, velocity_base, velocity_map, across, along = call(
        functools.partial(push_kernel, share, order),
        out_shape=(
            field, field, field, square, shape((2, devices, share), f32), shape((2, CELLS, share), f32),
        ),
        in_specs=[VMEM] * 10, out_specs=(VMEM,) * 6,
    )(half, q_moved, sums, p_base, pushed, cosine, finish, modes, modes_t, wavevectors)
    velocity, kick = call(
        finish_kernel, out_shape=(narrow, field), in_specs=[VMEM] * 5, out_specs=(VMEM,) * 2,
    )(half, velocity_base, velocity_map, *forces(rounded))
    p_new = p_mid - kick
    held, last = gather_planes(velocity)
    spectrum = shape((2 * total, share), f32)
    near = call(near_project_kernel, out_shape=spectrum, in_specs=[VMEM] * 3, out_specs=VMEM)(held, across, along)
    spectrum = call(
        functools.partial(project_kernel, 1.0 / math.sqrt(devices * CELLS)),
        out_shape=spectrum, in_specs=[VMEM] * 4, out_specs=HBM,
        scratch_shapes=[pltpu.VMEM((2 * total, share), f32), pltpu.SemaphoreType.DMA((2,))],
    )(near, last, across, along)
    return q_new.reshape(positions.shape), p_new.reshape(momenta.shape), spectrum.T


def solution(mesh):
    field = P(None, None, ("rep", "space"), None)

    return jax.shard_map(
        on_device,
        mesh=mesh,
        in_specs=(field, field) + (P(),) * 9,
        out_specs=(field, field, P(("rep", "space"), None)),
        check_vma=False,
    )
```

```python
import functools
import math

import jax
import jax.numpy as jnp
import numpy as np
from jax import lax
from jax.experimental import pallas as pl
from jax.experimental.pallas import tpu as pltpu
from jax.sharding import PartitionSpec as P


NY = 8
NZ = 16
CELLS = NY * NZ
PAD = 16
BLOCK = 9 * PAD
DEPTH = 256
SIZES = (8,8,)
SKEW = 1
SHIFTS = [(b, d) for b in (-1, 0, 1) for d in (-1, 0, 1)]
TWO_PI = 6.283185307179586
VMEM = pl.BlockSpec(memory_space=pltpu.VMEM)
SMEM = pl.BlockSpec(memory_space=pltpu.SMEM)
HBM = pl.BlockSpec(memory_space=pltpu.MemorySpace.HBM)
shape = jax.ShapeDtypeStruct
f32, bf16 = jnp.float32, jnp.bfloat16

call = functools.partial(pl.pallas_call, compiler_params=pltpu.CompilerParams(vmem_limit_bytes=16 << 20))
dot = functools.partial(jnp.dot, preferred_element_type=jnp.float32)


def split(values):
    high = values.astype(bf16)
    return high, (values - high.astype(f32)).astype(bf16)


def left_terms(values):
    high, low = split(values)
    return jnp.concatenate([high, high, low], axis=1)


def close_dot(left, values):
    high, low = split(values)
    rest = jnp.zeros((left.shape[1] // 3 - values.shape[0], values.shape[1]), bf16)
    return dot(left, jnp.concatenate([high, rest, low, rest, high, rest]))


def in_hbm(value):
    return pltpu.with_memory_space_constraint(value, pltpu.MemorySpace.HBM)


def roll(values, amount):
    amount = amount % CELLS
    return values if amount == 0 else pltpu.roll(values, amount, 1)


def shift_y(values, step):
    return roll(values, -step * NZ)


def shift_z(values, step, inner):
    if step == 0:
        return values
    edge = NZ - 1 if step == 1 else 0
    return jnp.where(inner == edge, roll(values, step * (NZ - 1)), roll(values, -step))


def z_index(rows):
    return lax.broadcasted_iota(jnp.int32, (rows, CELLS), 1) % NZ


def round_kernel(*refs):
    count = (len(refs) - 2) // 2
    sources, rounded_ref, targets, semaphores = refs[:count], refs[count], refs[count + 1 : -1], refs[-1]
    copies = [pltpu.make_async_copy(a, b, semaphores.at[i]) for i, (a, b) in enumerate(zip(sources, targets))]
    for copy in copies:
        copy.start()
    copies[0].wait()
    rounded_ref[...] = targets[0][...].astype(bf16)
    for copy in copies[1:]:
        copy.wait()


def setup_kernel(
    coords, beads, step_ref, cycle_ref, vectors_hbm, q_ref, one_ref, bias_one_ref, bias_two_ref, readout_ref,
    p_ref, masses_ref, blocks_ref, two_ref,
    forward_ref, outer_forward_ref, backward_ref, two_t_ref, wide_ref,
    q_base_ref, q_map_ref, p_base_ref, pushed_ref, cosine_ref, finish_ref, half_ref,
    modes_ref, modes_t_ref, vectors_ref, rows, semaphore
):
    copy = pltpu.make_async_copy(vectors_hbm, vectors_ref, semaphore)
    copy.start()
    is_odd = lax.axis_index("space") % 2 == 1
    hidden = one_ref.shape[1]
    rows[: one_ref.shape[0], :] = one_ref[...].astype(f32)
    rows[one_ref.shape[0] :, :] = jnp.zeros((rows.shape[0] - one_ref.shape[0], hidden), f32)
    at = lax.broadcasted_iota(jnp.int32, (PAD, hidden), 0)
    real = at < coords
    rest = bias_one_ref[...]
    turned = []
    for along_x in range(3):
        for o in range(9):
            even, odd = ((a * 9 + o) * coords for a in (along_x, 2 - along_x))
            taken = rows[even : even + PAD, :]
            if odd != even:
                taken = jnp.where(is_odd, rows[odd : odd + PAD, :], taken)
            taken = jnp.where(real, taken, 0.0)
            top = (along_x * 9 + o) * PAD
            backward_ref[top : top + PAD, :] = taken.astype(bf16)
            if along_x == 0 and o < 3:
                term = rest.astype(bf16).astype(f32)
                rest = rest - term
                taken = jnp.where(real, taken, jnp.broadcast_to(term, taken.shape))
                taken = jnp.where(at <= coords, taken, 0.0)
            turned.append(taken)
    forward = jnp.concatenate(turned).T.astype(bf16)
    forward_ref[...] = forward
    outer_forward_ref[...] = jnp.concatenate([forward[:, BLOCK:], forward[:, :BLOCK]], axis=1)
    two_t_ref[...] = two_ref[...].astype(f32).T.astype(bf16)
    columns = jnp.concatenate([bias_two_ref[...], readout_ref[...], jnp.zeros((6, hidden), f32)]).T
    for i in range(2):
        wide_ref[i] = jnp.broadcast_to(columns[:, i : i + 1], (hidden, CELLS))

    depth = blocks_ref.shape[1]
    column = lax.broadcasted_iota(jnp.int32, (beads, depth), 1) // beads
    for matrix_ref, first in ((modes_ref, 0), (modes_t_ref, 2 * beads)):
        high, low = blocks_ref[first : first + beads, :], blocks_ref[first + beads : first + 2 * beads, :]
        for c in range(coords):
            rows_at = slice(c * beads, (c + 1) * beads)
            mine = jnp.where(column == c, high, 0.0).astype(bf16)
            rest = jnp.where(column == c, low, 0.0).astype(bf16)
            matrix_ref[rows_at, :] = jnp.concatenate([mine, mine, rest], axis=1)
    order = lax.broadcasted_iota(jnp.int32, (beads, CELLS), 0).astype(f32)
    mass = jnp.concatenate([jnp.broadcast_to(masses_ref[:, c : c + 1], (beads, CELLS)) for c in range(coords)])
    step = step_ref[0]
    half = 0.5 * step
    frequency = 2.0 * cycle_ref[0] * jnp.sin(order * (0.5 * TWO_PI / beads))
    phase = frequency * step
    sine = jnp.sin(phase)
    ratio = jnp.where(order == 0, 1.0, sine / jnp.where(order == 0, 1.0, phase))
    cosine, drift, spring = (
        jnp.concatenate([term] * coords) for term in (jnp.cos(phase), step * ratio, frequency * sine)
    )
    drift, spring = drift / mass, mass * spring
    mode = close_dot(modes_t_ref[...], jnp.concatenate([q_ref[...], p_ref[...]], axis=1))
    mode_q, mode_p = mode[:, :CELLS], mode[:, CELLS:]
    moved = cosine * mode_q + drift * mode_p
    pushed = cosine * mode_p - spring * mode_q
    base = close_dot(modes_ref[...], jnp.concatenate([moved, pushed], axis=1))
    q_base_ref[...] = base[:, :CELLS]
    p_base_ref[...] = base[:, CELLS:]
    pushed_ref[...] = pushed
    cosine_ref[...] = cosine
    modes_t = modes_t_ref[:, :depth].astype(f32) + modes_t_ref[:, 2 * depth :].astype(f32)
    q_map_ref[...] = left_terms(close_dot(modes_ref[...], (half * drift[:, :1]) * modes_t))
    finish_ref[...] = jnp.concatenate([half / mass, 1.0 / mass], axis=1)
    half_ref[...] = jnp.full(half_ref.shape, half, f32)
    copy.wait()


def put_features(coords, beads, chosen, stage, features, top):
    filler = jnp.ones((PAD - coords, CELLS), f32)
    inner_z = z_index(PAD)
    for j in chosen:
        plane = jnp.concatenate([stage[pl.ds(j, coords, stride=beads), :], filler]).astype(bf16)
        along = {d: shift_z(plane, d, inner_z) for d in (-1, 0, 1)}
        for o, (b, d) in enumerate(SHIFTS):
            first = top + o * PAD
            features[first : first + PAD, j * CELLS : (j + 1) * CELLS] = shift_y(along[d], b)


def groups_of(beads):
    sizes = SIZES if sum(SIZES) == beads else (beads,)
    starts = np.cumsum((0,) + sizes)
    return [range(int(first), int(first) + size) for first, size in zip(starts, sizes)]


def columns_of(chosen):
    return slice(chosen[0] * CELLS, (chosen[-1] + 1) * CELLS)


def run_skewed(groups, stages):
    state = [() for _ in groups]
    order = sorted((SKEW * g + s, -s, g) for g in range(len(groups)) for s in range(len(stages)))
    for _, s, g in order:
        state[g] = stages[-s](groups[g], *state[g])


def back_stages(two_ref, two_t_ref, wide_ref):
    def second(chosen, first):
        bias, readout = (jnp.concatenate([wide_ref[i]] * len(chosen), axis=1) for i in range(2))
        hidden = jnp.tanh(first).astype(bf16)
        second = jnp.tanh(dot(two_ref[...], hidden) + bias)
        return hidden, (readout * (1.0 - second * second)).astype(bf16)

    def third(chosen, hidden, back):
        widened = hidden.astype(f32)
        return ((dot(two_t_ref[...], back) * (1.0 - widened * widened)).astype(bf16),)

    return second, third


def shifted_sum(sums, at):
    inner_z = z_index(PAD)
    total = None
    for d in (-1, 0, 1):
        part = None
        for b in (-1, 0, 1):
            o = (b + 1) * 3 + d + 1
            moved = shift_y(sums[o * PAD : (o + 1) * PAD, at * CELLS : (at + 1) * CELLS], -b)
            part = moved if part is None else part + moved
        part = shift_z(part, -d, inner_z)
        total = part if total is None else total + part
    return total


def own_kernel(
    coords, beads, tied, outer_ref, own_ref, inner_ref, forward_ref, backward_ref, two_ref, two_t_ref, wide_ref, *refs
):
    sent_ref, sums_ref, features, stage = refs[tied:]
    for place, ref in enumerate((outer_ref, own_ref, inner_ref)):
        stage[place] = ref[...].astype(f32)

    def put(chosen):
        for place in range(3):
            put_features(coords, beads, chosen, stage.at[place], features, place * BLOCK)
        return ()

    def first(chosen):
        return (dot(forward_ref[...], features[:, columns_of(chosen)]),)

    def last(chosen, back):
        sums = dot(backward_ref[BLOCK:], back)
        sums_ref[:, columns_of(chosen)] = sums[:BLOCK]
        return (sums,)

    def store(chosen, sums):
        for at, j in enumerate(chosen):
            rows = pl.ds(j, coords, stride=beads)
            sent_ref[rows, :] = shifted_sum(sums[BLOCK:], at)[:coords]

    run_skewed(groups_of(beads), (put, first, *back_stages(two_ref, two_t_ref, wide_ref), last, store))


def outer_kernel(
    coords, beads, outer2_ref, features_ref, sums_ref, forward_ref, backward_ref, two_ref, two_t_ref, wide_ref,
    kept_ref, features, stage
):
    extra = 2 * BLOCK - DEPTH
    stage[...] = outer2_ref[...].astype(f32)

    def put(chosen):
        put_features(coords, beads, chosen, stage, features, extra)
        features[:extra, columns_of(chosen)] = features_ref[DEPTH : 2 * BLOCK, columns_of(chosen)]
        return ()

    def first(chosen):
        near = dot(forward_ref[:, :DEPTH], features_ref[:DEPTH, columns_of(chosen)])
        return (near + dot(forward_ref[:, DEPTH:], features[:, columns_of(chosen)]),)

    def last(chosen, back):
        return (dot(backward_ref[2 * BLOCK :], back) + sums_ref[:, columns_of(chosen)],)

    def store(chosen, sums):
        for at, j in enumerate(chosen):
            rows = pl.ds(j, coords, stride=beads)
            kept_ref[rows, :] = shifted_sum(sums, at)[:coords]

    run_skewed(groups_of(beads), (put, first, *back_stages(two_ref, two_t_ref, wide_ref), last, store))


def move_kernel(q_base_ref, q_map_ref, kept_ref, came_ref, q_out, rounded_out, sum_out):
    sums = kept_ref[...] + came_ref[...]
    q = q_base_ref[...] - close_dot(q_map_ref[...], sums)
    rounded_out[...] = q.astype(bf16)
    q_out[...] = q
    sum_out[...] = sums


def push_kernel(
    share, planes_at, half_ref, q_ref, sum_ref, p_base_ref, pushed_ref, cosine_ref, finish_ref, modes_ref,
    modes_t_ref, vectors_ref, q_out, p_out, velocity_out, velocity_map_out, planes_out, cells_out
):
    depth = modes_ref.shape[1] // 3
    q_out[...] = q_ref[...]
    kick = cosine_ref[...] * close_dot(modes_t_ref[...], half_ref[0:1, :] * sum_ref[...])
    p_out[...] = p_base_ref[...] - close_dot(modes_ref[...], kick)
    velocity_out[...] = (pushed_ref[...] - kick) * finish_ref[:, CELLS:]
    modes_t = modes_t_ref[:, :depth].astype(f32) + modes_t_ref[:, 2 * depth :].astype(f32)
    velocity_map_out[...] = left_terms(finish_ref[:, :1] * modes_t)
    extent_x = len(planes_at)
    whole = extent_x * CELLS
    here = lax.axis_index("space")
    if vectors_ref.shape[1] == share:
        vectors = vectors_ref[...]
    else:
        vectors = vectors_ref[:, pl.ds(pl.multiple_of(here * share, CELLS), share)]
    cell = lax.broadcasted_iota(jnp.int32, (CELLS, share), 0)
    along = vectors[1:2] * ((cell // NZ) * (extent_x * NZ)) + vectors[2:3] * ((cell % NZ) * (extent_x * NY))
    across = jnp.concatenate([vectors[0:1] * ((here ^ at) * CELLS) for at in planes_at])
    for numerator, out in ((across, planes_out), (along, cells_out)):
        angle = TWO_PI * (numerator & (whole - 1)).astype(f32) / whole
        out[0] = jnp.cos(angle)
        out[1] = jnp.sin(angle)


def finish_kernel(half_ref, velocity_ref, map_ref, kept_ref, came_ref, velocity_out, kick_out):
    sums = kept_ref[...] + came_ref[...]
    velocity_out[...] = (velocity_ref[...] - close_dot(map_ref[...], sums)).astype(bf16)
    kick_out[...] = half_ref[0:1, :] * sums


def projected(velocity_ref, planes_ref, cells_ref, first, part):
    cos_cell, sin_cell = cells_ref[0], cells_ref[1]

    def trig(i):
        cos_plane, sin_plane = (planes_ref[t, first + i : first + i + 1, :] for t in range(2))
        if part == 0:
            return (cos_plane * cos_cell - sin_plane * sin_cell).astype(bf16)
        return (sin_plane * cos_cell + cos_plane * sin_cell).astype(bf16)

    total = 0.0
    for i in range(0, velocity_ref.shape[0] - 1, 2):
        block = jnp.concatenate([velocity_ref[i], velocity_ref[i + 1]], axis=1)
        total += dot(block, jnp.concatenate([trig(i), trig(i + 1)]))
    if velocity_ref.shape[0] % 2:
        total += dot(velocity_ref[velocity_ref.shape[0] - 1], trig(velocity_ref.shape[0] - 1))
    return total


def near_project_kernel(velocity_ref, planes_ref, cells_ref, out_ref):
    fields = velocity_ref.shape[1]
    for part in range(2):
        out_ref[part * fields : (part + 1) * fields, :] = projected(velocity_ref, planes_ref, cells_ref, 0, part)


def project_kernel(scale, near_ref, velocity_ref, planes_ref, cells_ref, out_hbm, result, semaphores):
    count, fields, _ = velocity_ref.shape
    copies = []
    for part in range(2):
        rows = slice(part * fields, (part + 1) * fields)
        result[rows, :] = (near_ref[rows, :] + projected(velocity_ref, planes_ref, cells_ref, count, part)) * scale
        copies.append(pltpu.make_async_copy(result.at[rows, :], out_hbm.at[rows, :], semaphores.at[part]))
        copies[-1].start()
    for copy in copies:
        copy.wait()


def mode_blocks(coords, beads):
    j = np.arange(beads)[:, None]
    k = np.arange(beads)[None, :]
    angles = 2.0 * np.pi * ((j * k) % beads) / beads
    edge = np.cos(angles) / math.sqrt(beads)
    inside = np.where(k < beads // 2, np.cos(angles), np.sin(angles)) * math.sqrt(2.0 / beads)
    matrix = np.where((k == 0) | (k == beads // 2), edge, inside).astype(np.float32)
    high = matrix.astype(jnp.bfloat16).astype(np.float32)
    low = (matrix - high).astype(jnp.bfloat16).astype(np.float32)
    blocks = np.concatenate([np.tile(block, (1, coords)) for block in (high, low, high.T, low.T)])
    return np.pad(blocks, ((0, 0), (0, -coords * beads % CELLS)))


def swap(value, distance):
    return lax.ppermute(value, "space", [(i, i ^ distance) for i in range(lax.axis_size("space"))])


def neighbour_planes(plane):
    count = lax.axis_size("space")
    step = [1 if i % 2 else -1 for i in range(count)]
    outer = lax.ppermute(plane, "space", [(i, (i + step[i]) % count) for i in range(count)])
    inner = swap(plane, 1)
    outer2 = lax.ppermute(plane, "space", [(i, (i - 2 * step[i]) % count) for i in range(count)])
    return outer2, outer, inner


def gather_order(count):
    order, distance = [0], count // 2
    while distance:
        if distance == 4:
            order, distance = [i ^ d for d in (0, 2, 4, 6) for i in order], 1
        else:
            order, distance = [i ^ d for d in (0, distance) for i in order], distance // 2
    return order


def gather_planes(velocity):
    held, distance = velocity[None], lax.axis_size("space") // 2
    while distance > 1:
        if distance == 4:
            near, far = swap(held, 2), swap(held, 4)
            held, distance = jnp.concatenate([held, near, far, swap(near, 4)]), 1
        else:
            held, distance = jnp.concatenate([held, swap(held, distance)]), distance // 2
    return held, swap(held, 1)


def on_device(
    positions, momenta, masses, step_size, cycle_frequency,
    layer_one, bias_one, layer_two, bias_two, readout, wavevectors
):
    coords, beads, planes, cells = positions.shape
    devices = lax.axis_size("space")
    assert planes == 1 and cells == CELLS and devices & (devices - 1) == 0 and devices > 1
    total = coords * beads
    hidden = layer_one.shape[0]
    width = 27 * PAD
    field, narrow = shape((total, CELLS), f32), shape((total, CELLS), bf16)
    square = shape((total, 3 * (total + -total % CELLS)), bf16)

    share = wavevectors.shape[1] // devices
    if share % CELLS:
        wavevectors = lax.dynamic_slice_in_dim(wavevectors, lax.axis_index("space") * share, share, 1)
    inputs = (
        positions.reshape(total, CELLS), layer_one.T, bias_one.reshape(1, hidden), bias_two.reshape(1, hidden),
        readout.reshape(1, hidden), momenta.reshape(total, CELLS), masses.reshape(1, coords),
        jnp.asarray(mode_blocks(coords, beads)), layer_two,
    )
    rounded, *brought = call(
        round_kernel, out_shape=(narrow,) + tuple(shape(x.shape, x.dtype) for x in inputs),
        in_specs=[HBM] * len(inputs), out_specs=(VMEM,) * (len(inputs) + 1),
        scratch_shapes=[pltpu.SemaphoreType.DMA((len(inputs),))],
    )(*map(in_hbm, inputs))
    two = brought[-1]

    (
        forward, outer_forward, backward, two_t, wide, q_base, q_map, p_base, pushed, cosine, finish, half,
        modes, modes_t, wavevectors
    ) = call(
        functools.partial(setup_kernel, coords, beads),
        out_shape=(
            shape((hidden, width), bf16), shape((hidden, width), bf16), shape((width, hidden), bf16),
            shape((hidden, hidden), bf16), shape((2, hidden, CELLS), f32),
            field, square, field, field, field, shape((total, 2 * CELLS), f32), shape((8, CELLS), f32),
            square, square, shape(wavevectors.shape, wavevectors.dtype),
        ),
        in_specs=[SMEM, SMEM, HBM] + [VMEM] * len(brought), out_specs=(VMEM,) * 15,
        scratch_shapes=[pltpu.VMEM((width, hidden), f32), pltpu.SemaphoreType.DMA],
    )(step_size, cycle_frequency, in_hbm(wavevectors), *brought)
    layers = (backward, two, two_t, wide)
    stage = pltpu.VMEM((total, CELLS), f32)

    def forces(plane, *tied):
        outer2, outer, inner = neighbour_planes(plane)
        sent, sums, features = call(
            functools.partial(own_kernel, coords, beads, len(tied)),
            out_shape=(field, shape((BLOCK, beads * CELLS), f32), shape((width, beads * CELLS), bf16)),
            in_specs=[VMEM] * (8 + len(tied)), out_specs=(VMEM,) * 3, scratch_shapes=[pltpu.VMEM((3, total, CELLS), f32)],
        )(outer, plane, inner, forward, *layers, *tied)
        came = swap(sent, 1)
        kept = call(
            functools.partial(outer_kernel, coords, beads),
            out_shape=field, in_specs=[VMEM] * 8, out_specs=VMEM,
            scratch_shapes=[pltpu.VMEM((width - DEPTH, beads * CELLS), bf16), stage],
        )(outer2, features, sums, outer_forward, *layers)
        return kept, came

    q_moved, rounded, sums = call(
        move_kernel, out_shape=(field, narrow, field), in_specs=[VMEM] * 4, out_specs=(VMEM,) * 3,
    )(q_base, q_map, *forces(rounded))
    order = gather_order(devices)
    q_new, p_mid, velocity_base, velocity_map, across, along = call(
        functools.partial(push_kernel, share, order),
        out_shape=(
            field, field, field, square, shape((2, devices, share), f32), shape((2, CELLS, share), f32),
        ),
        in_specs=[VMEM] * 10, out_specs=(VMEM,) * 6,
    )(half, q_moved, sums, p_base, pushed, cosine, finish, modes, modes_t, wavevectors)
    velocity, kick = call(
        finish_kernel, out_shape=(narrow, field), in_specs=[VMEM] * 5, out_specs=(VMEM,) * 2,
    )(half, velocity_base, velocity_map, *forces(rounded))
    p_new = p_mid - kick
    held, last = gather_planes(velocity)
    spectrum = shape((2 * total, share), f32)
    near = call(near_project_kernel, out_shape=spectrum, in_specs=[VMEM] * 3, out_specs=VMEM)(held, across, along)
    spectrum = call(
        functools.partial(project_kernel, 1.0 / math.sqrt(devices * CELLS)),
        out_shape=spectrum, in_specs=[VMEM] * 4, out_specs=HBM,
        scratch_shapes=[pltpu.VMEM((2 * total, share), f32), pltpu.SemaphoreType.DMA((2,))],
    )(near, last, across, along)
    return q_new.reshape(positions.shape), p_new.reshape(momenta.shape), spectrum.T


def solution(mesh):
    field = P(None, None, ("rep", "space"), None)

    return jax.shard_map(
        on_device,
        mesh=mesh,
        in_specs=(field, field) + (P(),) * 9,
        out_specs=(field, field, P(("rep", "space"), None)),
        check_vma=False,
    )
```

```python
import functools
import math

import jax
import jax.numpy as jnp
import numpy as np
from jax import lax
from jax.experimental import pallas as pl
from jax.experimental.pallas import tpu as pltpu
from jax.sharding import PartitionSpec as P


NY = 8
NZ = 16
CELLS = NY * NZ
PAD = 16
BLOCK = 9 * PAD
DEPTH = 256
SIZES = (8,8,)
SKEW = 1
SHIFTS = [(b, d) for b in (-1, 0, 1) for d in (-1, 0, 1)]
TWO_PI = 6.283185307179586
VMEM = pl.BlockSpec(memory_space=pltpu.VMEM)
SMEM = pl.BlockSpec(memory_space=pltpu.SMEM)
HBM = pl.BlockSpec(memory_space=pltpu.MemorySpace.HBM)
shape = jax.ShapeDtypeStruct
f32, bf16 = jnp.float32, jnp.bfloat16

call = functools.partial(pl.pallas_call, compiler_params=pltpu.CompilerParams(vmem_limit_bytes=16 << 20))
dot = functools.partial(jnp.dot, preferred_element_type=jnp.float32)


def split(values):
    high = values.astype(bf16)
    return high, (values - high.astype(f32)).astype(bf16)


def left_terms(values):
    high, low = split(values)
    return jnp.concatenate([high, high, low], axis=1)


def close_dot(left, values):
    high, low = split(values)
    rest = jnp.zeros((left.shape[1] // 3 - values.shape[0], values.shape[1]), bf16)
    return dot(left, jnp.concatenate([high, rest, low, rest, high, rest]))


def in_hbm(value):
    return pltpu.with_memory_space_constraint(value, pltpu.MemorySpace.HBM)


def roll(values, amount):
    amount = amount % CELLS
    return values if amount == 0 else pltpu.roll(values, amount, 1)


def shift_y(values, step):
    return roll(values, -step * NZ)


def shift_z(values, step, inner):
    if step == 0:
        return values
    edge = NZ - 1 if step == 1 else 0
    return jnp.where(inner == edge, roll(values, step * (NZ - 1)), roll(values, -step))


def z_index(rows):
    return lax.broadcasted_iota(jnp.int32, (rows, CELLS), 1) % NZ


def round_kernel(*refs):
    count = (len(refs) - 2) // 2
    sources, rounded_ref, targets, semaphores = refs[:count], refs[count], refs[count + 1 : -1], refs[-1]
    copies = [pltpu.make_async_copy(a, b, semaphores.at[i]) for i, (a, b) in enumerate(zip(sources, targets))]
    for copy in copies:
        copy.start()
    copies[0].wait()
    rounded_ref[...] = targets[0][...].astype(bf16)
    for copy in copies[1:]:
        copy.wait()


def setup_kernel(
    coords, beads, step_ref, cycle_ref, vectors_hbm, q_ref, one_ref, bias_one_ref, bias_two_ref, readout_ref,
    p_ref, masses_ref, blocks_ref, two_ref,
    forward_ref, outer_forward_ref, backward_ref, two_t_ref, wide_ref,
    q_base_ref, q_map_ref, p_base_ref, pushed_ref, cosine_ref, finish_ref, half_ref,
    modes_ref, modes_t_ref, vectors_ref, rows, semaphore
):
    copy = pltpu.make_async_copy(vectors_hbm, vectors_ref, semaphore)
    copy.start()
    is_odd = lax.axis_index("space") % 2 == 1
    hidden = one_ref.shape[1]
    rows[: one_ref.shape[0], :] = one_ref[...].astype(f32)
    rows[one_ref.shape[0] :, :] = jnp.zeros((rows.shape[0] - one_ref.shape[0], hidden), f32)
    at = lax.broadcasted_iota(jnp.int32, (PAD, hidden), 0)
    real = at < coords
    rest = bias_one_ref[...]
    turned = []
    for along_x in range(3):
        for o in range(9):
            even, odd = ((a * 9 + o) * coords for a in (along_x, 2 - along_x))
            taken = rows[even : even + PAD, :]
            if odd != even:
                taken = jnp.where(is_odd, rows[odd : odd + PAD, :], taken)
            taken = jnp.where(real, taken, 0.0)
            top = (along_x * 9 + o) * PAD
            backward_ref[top : top + PAD, :] = taken.astype(bf16)
            if along_x == 0 and o < 3:
                term = rest.astype(bf16).astype(f32)
                rest = rest - term
                taken = jnp.where(real, taken, jnp.broadcast_to(term, taken.shape))
                taken = jnp.where(at <= coords, taken, 0.0)
            turned.append(taken)
    forward = jnp.concatenate(turned).T.astype(bf16)
    forward_ref[...] = forward
    outer_forward_ref[...] = jnp.concatenate([forward[:, BLOCK:], forward[:, :BLOCK]], axis=1)
    two_t_ref[...] = two_ref[...].astype(f32).T.astype(bf16)
    columns = jnp.concatenate([bias_two_ref[...], readout_ref[...], jnp.zeros((6, hidden), f32)]).T
    for i in range(2):
        wide_ref[i] = jnp.broadcast_to(columns[:, i : i + 1], (hidden, CELLS))

    depth = blocks_ref.shape[1]
    column = lax.broadcasted_iota(jnp.int32, (beads, depth), 1) // beads
    for matrix_ref, first in ((modes_ref, 0), (modes_t_ref, 2 * beads)):
        high, low = blocks_ref[first : first + beads, :], blocks_ref[first + beads : first + 2 * beads, :]
        for c in range(coords):
            rows_at = slice(c * beads, (c + 1) * beads)
            mine = jnp.where(column == c, high, 0.0).astype(bf16)
            rest = jnp.where(column == c, low, 0.0).astype(bf16)
            matrix_ref[rows_at, :] = jnp.concatenate([mine, mine, rest], axis=1)
    order = lax.broadcasted_iota(jnp.int32, (beads, CELLS), 0).astype(f32)
    mass = jnp.concatenate([jnp.broadcast_to(masses_ref[:, c : c + 1], (beads, CELLS)) for c in range(coords)])
    step = step_ref[0]
    half = 0.5 * step
    frequency = 2.0 * cycle_ref[0] * jnp.sin(order * (0.5 * TWO_PI / beads))
    phase = frequency * step
    sine = jnp.sin(phase)
    ratio = jnp.where(order == 0, 1.0, sine / jnp.where(order == 0, 1.0, phase))
    cosine, drift, spring = (
        jnp.concatenate([term] * coords) for term in (jnp.cos(phase), step * ratio, frequency * sine)
    )
    drift, spring = drift / mass, mass * spring
    mode = close_dot(modes_t_ref[...], jnp.concatenate([q_ref[...], p_ref[...]], axis=1))
    mode_q, mode_p = mode[:, :CELLS], mode[:, CELLS:]
    moved = cosine * mode_q + drift * mode_p
    pushed = cosine * mode_p - spring * mode_q
    base = close_dot(modes_ref[...], jnp.concatenate([moved, pushed], axis=1))
    q_base_ref[...] = base[:, :CELLS]
    p_base_ref[...] = base[:, CELLS:]
    pushed_ref[...] = pushed
    cosine_ref[...] = cosine
    modes_t = modes_t_ref[:, :depth].astype(f32) + modes_t_ref[:, 2 * depth :].astype(f32)
    q_map_ref[...] = left_terms(close_dot(modes_ref[...], (half * drift[:, :1]) * modes_t))
    finish_ref[...] = jnp.concatenate([half / mass, 1.0 / mass], axis=1)
    half_ref[...] = jnp.full(half_ref.shape, half, f32)
    copy.wait()


def put_features(coords, beads, chosen, stage, features, top):
    filler = jnp.ones((PAD - coords, CELLS), f32)
    inner_z = z_index(PAD)
    for j in chosen:
        plane = jnp.concatenate([stage[pl.ds(j, coords, stride=beads), :], filler]).astype(bf16)
        along = {d: shift_z(plane, d, inner_z) for d in (-1, 0, 1)}
        for o, (b, d) in enumerate(SHIFTS):
            first = top + o * PAD
            features[first : first + PAD, j * CELLS : (j + 1) * CELLS] = shift_y(along[d], b)


def groups_of(beads):
    sizes = SIZES if sum(SIZES) == beads else (beads,)
    starts = np.cumsum((0,) + sizes)
    return [range(int(first), int(first) + size) for first, size in zip(starts, sizes)]


def columns_of(chosen):
    return slice(chosen[0] * CELLS, (chosen[-1] + 1) * CELLS)


def run_skewed(groups, stages):
    state = [() for _ in groups]
    order = sorted((SKEW * g + s, -s, g) for g in range(len(groups)) for s in range(len(stages)))
    for _, s, g in order:
        state[g] = stages[-s](groups[g], *state[g])


def back_stages(two_ref, two_t_ref, wide_ref):
    def second(chosen, first):
        bias, readout = (jnp.concatenate([wide_ref[i]] * len(chosen), axis=1) for i in range(2))
        hidden = jnp.tanh(first).astype(bf16)
        second = jnp.tanh(dot(two_ref[...], hidden) + bias)
        return hidden, (readout * (1.0 - second * second)).astype(bf16)

    def third(chosen, hidden, back):
        widened = hidden.astype(f32)
        return ((dot(two_t_ref[...], back) * (1.0 - widened * widened)).astype(bf16),)

    return second, third


def shifted_sum(sums, at):
    inner_z = z_index(PAD)
    total = None
    for d in (-1, 0, 1):
        part = None
        for b in (-1, 0, 1):
            o = (b + 1) * 3 + d + 1
            moved = shift_y(sums[o * PAD : (o + 1) * PAD, at * CELLS : (at + 1) * CELLS], -b)
            part = moved if part is None else part + moved
        part = shift_z(part, -d, inner_z)
        total = part if total is None else total + part
    return total


def own_kernel(
    coords, beads, tied, outer_ref, own_ref, inner_ref, forward_ref, backward_ref, two_ref, two_t_ref, wide_ref, *refs
):
    sent_ref, sums_ref, features, stage = refs[tied:]
    for place, ref in enumerate((outer_ref, own_ref, inner_ref)):
        stage[place] = ref[...].astype(f32)

    def put(chosen):
        for place in range(3):
            put_features(coords, beads, chosen, stage.at[place], features, place * BLOCK)
        return ()

    def first(chosen):
        return (dot(forward_ref[...], features[:, columns_of(chosen)]),)

    def last(chosen, back):
        sums = dot(backward_ref[BLOCK:], back)
        sums_ref[:, columns_of(chosen)] = sums[:BLOCK]
        return (sums,)

    def store(chosen, sums):
        for at, j in enumerate(chosen):
            rows = pl.ds(j, coords, stride=beads)
            sent_ref[rows, :] = shifted_sum(sums[BLOCK:], at)[:coords]

    run_skewed(groups_of(beads), (put, first, *back_stages(two_ref, two_t_ref, wide_ref), last, store))


def outer_kernel(
    coords, beads, outer2_ref, features_ref, sums_ref, forward_ref, backward_ref, two_ref, two_t_ref, wide_ref,
    kept_ref, features, stage
):
    extra = 2 * BLOCK - DEPTH
    stage[...] = outer2_ref[...].astype(f32)

    def put(chosen):
        put_features(coords, beads, chosen, stage, features, extra)
        features[:extra, columns_of(chosen)] = features_ref[DEPTH : 2 * BLOCK, columns_of(chosen)]
        return ()

    def first(chosen):
        near = dot(forward_ref[:, :DEPTH], features_ref[:DEPTH, columns_of(chosen)])
        return (near + dot(forward_ref[:, DEPTH:], features[:, columns_of(chosen)]),)

    def last(chosen, back):
        return (dot(backward_ref[2 * BLOCK :], back) + sums_ref[:, columns_of(chosen)],)

    def store(chosen, sums):
        for at, j in enumerate(chosen):
            rows = pl.ds(j, coords, stride=beads)
            kept_ref[rows, :] = shifted_sum(sums, at)[:coords]

    run_skewed(groups_of(beads), (put, first, *back_stages(two_ref, two_t_ref, wide_ref), last, store))


def move_kernel(q_base_ref, q_map_ref, kept_ref, came_ref, q_out, rounded_out, sum_out):
    sums = kept_ref[...] + came_ref[...]
    q = q_base_ref[...] - close_dot(q_map_ref[...], sums)
    rounded_out[...] = q.astype(bf16)
    q_out[...] = q
    sum_out[...] = sums


def push_kernel(
    share, planes_at, half_ref, q_ref, sum_ref, p_base_ref, pushed_ref, cosine_ref, finish_ref, modes_ref,
    modes_t_ref, vectors_ref, q_out, p_out, velocity_out, velocity_map_out, planes_out, cells_out
):
    depth = modes_ref.shape[1] // 3
    q_out[...] = q_ref[...]
    kick = cosine_ref[...] * close_dot(modes_t_ref[...], half_ref[0:1, :] * sum_ref[...])
    p_out[...] = p_base_ref[...] - close_dot(modes_ref[...], kick)
    velocity_out[...] = (pushed_ref[...] - kick) * finish_ref[:, CELLS:]
    modes_t = modes_t_ref[:, :depth].astype(f32) + modes_t_ref[:, 2 * depth :].astype(f32)
    velocity_map_out[...] = left_terms(finish_ref[:, :1] * modes_t)
    extent_x = len(planes_at)
    whole = extent_x * CELLS
    here = lax.axis_index("space")
    if vectors_ref.shape[1] == share:
        vectors = vectors_ref[...]
    else:
        vectors = vectors_ref[:, pl.ds(pl.multiple_of(here * share, CELLS), share)]
    cell = lax.broadcasted_iota(jnp.int32, (CELLS, share), 0)
    along = vectors[1:2] * ((cell // NZ) * (extent_x * NZ)) + vectors[2:3] * ((cell % NZ) * (extent_x * NY))
    across = jnp.concatenate([vectors[0:1] * ((here ^ at) * CELLS) for at in planes_at])
    for numerator, out in ((across, planes_out), (along, cells_out)):
        angle = TWO_PI * (numerator & (whole - 1)).astype(f32) / whole
        out[0] = jnp.cos(angle)
        out[1] = jnp.sin(angle)


def finish_kernel(half_ref, velocity_ref, map_ref, kept_ref, came_ref, velocity_out, kick_out):
    sums = kept_ref[...] + came_ref[...]
    velocity_out[...] = (velocity_ref[...] - close_dot(map_ref[...], sums)).astype(bf16)
    kick_out[...] = half_ref[0:1, :] * sums


def projected(velocity_ref, planes_ref, cells_ref, first, part):
    cos_cell, sin_cell = cells_ref[0], cells_ref[1]

    def trig(i):
        cos_plane, sin_plane = (planes_ref[t, first + i : first + i + 1, :] for t in range(2))
        if part == 0:
            return (cos_plane * cos_cell - sin_plane * sin_cell).astype(bf16)
        return (sin_plane * cos_cell + cos_plane * sin_cell).astype(bf16)

    total = 0.0
    for i in range(0, velocity_ref.shape[0] - 1, 2):
        block = jnp.concatenate([velocity_ref[i], velocity_ref[i + 1]], axis=1)
        total += dot(block, jnp.concatenate([trig(i), trig(i + 1)]))
    if velocity_ref.shape[0] % 2:
        total += dot(velocity_ref[velocity_ref.shape[0] - 1], trig(velocity_ref.shape[0] - 1))
    return total


def near_project_kernel(velocity_ref, planes_ref, cells_ref, out_ref):
    fields = velocity_ref.shape[1]
    for part in range(2):
        out_ref[part * fields : (part + 1) * fields, :] = projected(velocity_ref, planes_ref, cells_ref, 0, part)


def project_kernel(scale, near_ref, velocity_ref, planes_ref, cells_ref, out_hbm, result, semaphores):
    count, fields, _ = velocity_ref.shape
    copies = []
    for part in range(2):
        rows = slice(part * fields, (part + 1) * fields)
        result[rows, :] = (near_ref[rows, :] + projected(velocity_ref, planes_ref, cells_ref, count, part)) * scale
        copies.append(pltpu.make_async_copy(result.at[rows, :], out_hbm.at[rows, :], semaphores.at[part]))
        copies[-1].start()
    for copy in copies:
        copy.wait()


def mode_blocks(coords, beads):
    j = np.arange(beads)[:, None]
    k = np.arange(beads)[None, :]
    angles = 2.0 * np.pi * ((j * k) % beads) / beads
    edge = np.cos(angles) / math.sqrt(beads)
    inside = np.where(k < beads // 2, np.cos(angles), np.sin(angles)) * math.sqrt(2.0 / beads)
    matrix = np.where((k == 0) | (k == beads // 2), edge, inside).astype(np.float32)
    high = matrix.astype(jnp.bfloat16).astype(np.float32)
    low = (matrix - high).astype(jnp.bfloat16).astype(np.float32)
    blocks = np.concatenate([np.tile(block, (1, coords)) for block in (high, low, high.T, low.T)])
    return np.pad(blocks, ((0, 0), (0, -coords * beads % CELLS)))


def swap(value, distance):
    return lax.ppermute(value, "space", [(i, i ^ distance) for i in range(lax.axis_size("space"))])


def neighbour_planes(plane):
    count = lax.axis_size("space")
    step = [1 if i % 2 else -1 for i in range(count)]
    outer = lax.ppermute(plane, "space", [(i, (i + step[i]) % count) for i in range(count)])
    inner = swap(plane, 1)
    outer2 = lax.ppermute(plane, "space", [(i, (i - 2 * step[i]) % count) for i in range(count)])
    return outer2, outer, inner


def gather_order(count):
    if count % 4:
        return [0, 1]
    far = list(range(4, count, 4))
    return [i ^ j for j in (0, 1) for i in [0] + far + [2] + [d ^ 2 for d in far]]


def gather_planes(velocity):
    count = lax.axis_size("space")
    if count % 4:
        held = velocity[None]
    else:
        near = swap(velocity, 2)
        far = [swap(velocity, distance) for distance in range(4, count, 4)]
        held = jnp.stack([velocity] + far + [near] + [swap(x, 2) for x in far])
    return held, swap(held, 1)


def on_device(
    positions, momenta, masses, step_size, cycle_frequency,
    layer_one, bias_one, layer_two, bias_two, readout, wavevectors
):
    coords, beads, planes, cells = positions.shape
    devices = lax.axis_size("space")
    assert planes == 1 and cells == CELLS and devices & (devices - 1) == 0 and devices > 1
    total = coords * beads
    hidden = layer_one.shape[0]
    width = 27 * PAD
    field, narrow = shape((total, CELLS), f32), shape((total, CELLS), bf16)
    square = shape((total, 3 * (total + -total % CELLS)), bf16)

    share = wavevectors.shape[1] // devices
    if share % CELLS:
        wavevectors = lax.dynamic_slice_in_dim(wavevectors, lax.axis_index("space") * share, share, 1)
    inputs = (
        positions.reshape(total, CELLS), layer_one.T, bias_one.reshape(1, hidden), bias_two.reshape(1, hidden),
        readout.reshape(1, hidden), momenta.reshape(total, CELLS), masses.reshape(1, coords),
        jnp.asarray(mode_blocks(coords, beads)), layer_two,
    )
    rounded, *brought = call(
        round_kernel, out_shape=(narrow,) + tuple(shape(x.shape, x.dtype) for x in inputs),
        in_specs=[HBM] * len(inputs), out_specs=(VMEM,) * (len(inputs) + 1),
        scratch_shapes=[pltpu.SemaphoreType.DMA((len(inputs),))],
    )(*map(in_hbm, inputs))
    two = brought[-1]

    (
        forward, outer_forward, backward, two_t, wide, q_base, q_map, p_base, pushed, cosine, finish, half,
        modes, modes_t, wavevectors
    ) = call(
        functools.partial(setup_kernel, coords, beads),
        out_shape=(
            shape((hidden, width), bf16), shape((hidden, width), bf16), shape((width, hidden), bf16),
            shape((hidden, hidden), bf16), shape((2, hidden, CELLS), f32),
            field, square, field, field, field, shape((total, 2 * CELLS), f32), shape((8, CELLS), f32),
            square, square, shape(wavevectors.shape, wavevectors.dtype),
        ),
        in_specs=[SMEM, SMEM, HBM] + [VMEM] * len(brought), out_specs=(VMEM,) * 15,
        scratch_shapes=[pltpu.VMEM((width, hidden), f32), pltpu.SemaphoreType.DMA],
    )(step_size, cycle_frequency, in_hbm(wavevectors), *brought)
    layers = (backward, two, two_t, wide)
    stage = pltpu.VMEM((total, CELLS), f32)

    def forces(plane, *tied):
        outer2, outer, inner = neighbour_planes(plane)
        sent, sums, features = call(
            functools.partial(own_kernel, coords, beads, len(tied)),
            out_shape=(field, shape((BLOCK, beads * CELLS), f32), shape((width, beads * CELLS), bf16)),
            in_specs=[VMEM] * (8 + len(tied)), out_specs=(VMEM,) * 3, scratch_shapes=[pltpu.VMEM((3, total, CELLS), f32)],
        )(outer, plane, inner, forward, *layers, *tied)
        came = swap(sent, 1)
        kept = call(
            functools.partial(outer_kernel, coords, beads),
            out_shape=field, in_specs=[VMEM] * 8, out_specs=VMEM,
            scratch_shapes=[pltpu.VMEM((width - DEPTH, beads * CELLS), bf16), stage],
        )(outer2, features, sums, outer_forward, *layers)
        return kept, came

    q_moved, rounded, sums = call(
        move_kernel, out_shape=(field, narrow, field), in_specs=[VMEM] * 4, out_specs=(VMEM,) * 3,
    )(q_base, q_map, *forces(rounded))
    order = gather_order(devices)
    q_new, p_mid, velocity_base, velocity_map, across, along = call(
        functools.partial(push_kernel, share, order),
        out_shape=(
            field, field, field, square, shape((2, devices, share), f32), shape((2, CELLS, share), f32),
        ),
        in_specs=[VMEM] * 10, out_specs=(VMEM,) * 6,
    )(half, q_moved, sums, p_base, pushed, cosine, finish, modes, modes_t, wavevectors)
    velocity, kick = call(
        finish_kernel, out_shape=(narrow, field), in_specs=[VMEM] * 5, out_specs=(VMEM,) * 2,
    )(half, velocity_base, velocity_map, *forces(rounded))
    p_new = p_mid - kick
    held, last = gather_planes(velocity)
    spectrum = shape((2 * total, share), f32)
    near = call(near_project_kernel, out_shape=spectrum, in_specs=[VMEM] * 3, out_specs=VMEM)(held, across, along)
    spectrum = call(
        functools.partial(project_kernel, 1.0 / math.sqrt(devices * CELLS)),
        out_shape=spectrum, in_specs=[VMEM] * 4, out_specs=HBM,
        scratch_shapes=[pltpu.VMEM((2 * total, share), f32), pltpu.SemaphoreType.DMA((2,))],
    )(near, last, across, along)
    return q_new.reshape(positions.shape), p_new.reshape(momenta.shape), spectrum.T


def solution(mesh):
    field = P(None, None, ("rep", "space"), None)

    return jax.shard_map(
        on_device,
        mesh=mesh,
        in_specs=(field, field) + (P(),) * 9,
        out_specs=(field, field, P(("rep", "space"), None)),
        check_vma=False,
    )
```

```python
import functools
import math

import jax
import jax.numpy as jnp
import numpy as np
from jax import lax
from jax.experimental import pallas as pl
from jax.experimental.pallas import tpu as pltpu
from jax.sharding import PartitionSpec as P


NY = 8
NZ = 16
CELLS = NY * NZ
PAD = 16
BLOCK = 9 * PAD
DEPTH = 256
SIZES = (8,8,)
SKEW = 1
SHIFTS = [(b, d) for b in (-1, 0, 1) for d in (-1, 0, 1)]
TWO_PI = 6.283185307179586
VMEM = pl.BlockSpec(memory_space=pltpu.VMEM)
SMEM = pl.BlockSpec(memory_space=pltpu.SMEM)
HBM = pl.BlockSpec(memory_space=pltpu.MemorySpace.HBM)
shape = jax.ShapeDtypeStruct
f32, bf16 = jnp.float32, jnp.bfloat16

call = functools.partial(pl.pallas_call, compiler_params=pltpu.CompilerParams(vmem_limit_bytes=16 << 20))
dot = functools.partial(jnp.dot, preferred_element_type=jnp.float32)


def split(values):
    high = values.astype(bf16)
    return high, (values - high.astype(f32)).astype(bf16)


def left_terms(values):
    high, low = split(values)
    return jnp.concatenate([high, high, low], axis=1)


def close_dot(left, values):
    high, low = split(values)
    rest = jnp.zeros((left.shape[1] // 3 - values.shape[0], values.shape[1]), bf16)
    return dot(left, jnp.concatenate([high, rest, low, rest, high, rest]))


def in_hbm(value):
    return pltpu.with_memory_space_constraint(value, pltpu.MemorySpace.HBM)


def roll(values, amount):
    amount = amount % CELLS
    return values if amount == 0 else pltpu.roll(values, amount, 1)


def shift_y(values, step):
    return roll(values, -step * NZ)


def shift_z(values, step, inner):
    if step == 0:
        return values
    edge = NZ - 1 if step == 1 else 0
    return jnp.where(inner == edge, roll(values, step * (NZ - 1)), roll(values, -step))


def z_index(rows):
    return lax.broadcasted_iota(jnp.int32, (rows, CELLS), 1) % NZ


def round_kernel(*refs):
    count = (len(refs) - 2) // 2
    sources, rounded_ref, targets, semaphores = refs[:count], refs[count], refs[count + 1 : -1], refs[-1]
    copies = [pltpu.make_async_copy(a, b, semaphores.at[i]) for i, (a, b) in enumerate(zip(sources, targets))]
    for copy in copies:
        copy.start()
    copies[0].wait()
    rounded_ref[...] = targets[0][...].astype(bf16)
    for copy in copies[1:]:
        copy.wait()


def setup_kernel(
    coords, beads, step_ref, cycle_ref, vectors_hbm, q_ref, one_ref, bias_one_ref, bias_two_ref, readout_ref,
    p_ref, masses_ref, blocks_ref, two_ref,
    forward_ref, outer_forward_ref, backward_ref, two_t_ref, wide_ref,
    q_base_ref, q_map_ref, p_base_ref, pushed_ref, cosine_ref, finish_ref, half_ref,
    modes_ref, modes_t_ref, vectors_ref, rows, semaphore
):
    copy = pltpu.make_async_copy(vectors_hbm, vectors_ref, semaphore)
    copy.start()
    is_odd = lax.axis_index("space") % 2 == 1
    hidden = one_ref.shape[1]
    rows[: one_ref.shape[0], :] = one_ref[...].astype(f32)
    rows[one_ref.shape[0] :, :] = jnp.zeros((rows.shape[0] - one_ref.shape[0], hidden), f32)
    at = lax.broadcasted_iota(jnp.int32, (PAD, hidden), 0)
    real = at < coords
    rest = bias_one_ref[...]
    turned = []
    for along_x in range(3):
        for o in range(9):
            even, odd = ((a * 9 + o) * coords for a in (along_x, 2 - along_x))
            taken = rows[even : even + PAD, :]
            if odd != even:
                taken = jnp.where(is_odd, rows[odd : odd + PAD, :], taken)
            taken = jnp.where(real, taken, 0.0)
            top = (along_x * 9 + o) * PAD
            backward_ref[top : top + PAD, :] = taken.astype(bf16)
            if along_x == 0 and o < 3:
                term = rest.astype(bf16).astype(f32)
                rest = rest - term
                taken = jnp.where(real, taken, jnp.broadcast_to(term, taken.shape))
                taken = jnp.where(at <= coords, taken, 0.0)
            turned.append(taken)
    forward = jnp.concatenate(turned).T.astype(bf16)
    forward_ref[...] = forward
    outer_forward_ref[...] = jnp.concatenate([forward[:, BLOCK:], forward[:, :BLOCK]], axis=1)
    two_t_ref[...] = two_ref[...].astype(f32).T.astype(bf16)
    columns = jnp.concatenate([bias_two_ref[...], readout_ref[...], jnp.zeros((6, hidden), f32)]).T
    for i in range(2):
        wide_ref[i] = jnp.broadcast_to(columns[:, i : i + 1], (hidden, CELLS))

    depth = blocks_ref.shape[1]
    column = lax.broadcasted_iota(jnp.int32, (beads, depth), 1) // beads
    for matrix_ref, first in ((modes_ref, 0), (modes_t_ref, 2 * beads)):
        high, low = blocks_ref[first : first + beads, :], blocks_ref[first + beads : first + 2 * beads, :]
        for c in range(coords):
            rows_at = slice(c * beads, (c + 1) * beads)
            mine = jnp.where(column == c, high, 0.0).astype(bf16)
            rest = jnp.where(column == c, low, 0.0).astype(bf16)
            matrix_ref[rows_at, :] = jnp.concatenate([mine, mine, rest], axis=1)
    order = lax.broadcasted_iota(jnp.int32, (beads, CELLS), 0).astype(f32)
    mass = jnp.concatenate([jnp.broadcast_to(masses_ref[:, c : c + 1], (beads, CELLS)) for c in range(coords)])
    step = step_ref[0]
    half = 0.5 * step
    frequency = 2.0 * cycle_ref[0] * jnp.sin(order * (0.5 * TWO_PI / beads))
    phase = frequency * step
    sine = jnp.sin(phase)
    ratio = jnp.where(order == 0, 1.0, sine / jnp.where(order == 0, 1.0, phase))
    cosine, drift, spring = (
        jnp.concatenate([term] * coords) for term in (jnp.cos(phase), step * ratio, frequency * sine)
    )
    drift, spring = drift / mass, mass * spring
    mode = close_dot(modes_t_ref[...], jnp.concatenate([q_ref[...], p_ref[...]], axis=1))
    mode_q, mode_p = mode[:, :CELLS], mode[:, CELLS:]
    moved = cosine * mode_q + drift * mode_p
    pushed = cosine * mode_p - spring * mode_q
    base = close_dot(modes_ref[...], jnp.concatenate([moved, pushed], axis=1))
    q_base_ref[...] = base[:, :CELLS]
    p_base_ref[...] = base[:, CELLS:]
    pushed_ref[...] = pushed
    cosine_ref[...] = cosine
    modes_t = modes_t_ref[:, :depth].astype(f32) + modes_t_ref[:, 2 * depth :].astype(f32)
    q_map_ref[...] = left_terms(close_dot(modes_ref[...], (half * drift[:, :1]) * modes_t))
    finish_ref[...] = jnp.concatenate([half / mass, 1.0 / mass], axis=1)
    half_ref[...] = jnp.full(half_ref.shape, half, f32)
    copy.wait()


def put_features(coords, beads, chosen, stage, features, top):
    filler = jnp.ones((PAD - coords, CELLS), f32)
    inner_z = z_index(PAD)
    for j in chosen:
        plane = jnp.concatenate([stage[pl.ds(j, coords, stride=beads), :], filler]).astype(bf16)
        along = {d: shift_z(plane, d, inner_z) for d in (-1, 0, 1)}
        for o, (b, d) in enumerate(SHIFTS):
            first = top + o * PAD
            features[first : first + PAD, j * CELLS : (j + 1) * CELLS] = shift_y(along[d], b)


def groups_of(beads):
    sizes = SIZES if sum(SIZES) == beads else (beads,)
    starts = np.cumsum((0,) + sizes)
    return [range(int(first), int(first) + size) for first, size in zip(starts, sizes)]


def columns_of(chosen):
    return slice(chosen[0] * CELLS, (chosen[-1] + 1) * CELLS)


def run_skewed(groups, stages):
    state = [() for _ in groups]
    order = sorted((SKEW * g + s, -s, g) for g in range(len(groups)) for s in range(len(stages)))
    for _, s, g in order:
        state[g] = stages[-s](groups[g], *state[g])


def back_stages(two_ref, two_t_ref, wide_ref):
    def second(chosen, first):
        bias, readout = (jnp.concatenate([wide_ref[i]] * len(chosen), axis=1) for i in range(2))
        hidden = jnp.tanh(first).astype(bf16)
        second = jnp.tanh(dot(two_ref[...], hidden) + bias)
        return hidden, (readout * (1.0 - second * second)).astype(bf16)

    def third(chosen, hidden, back):
        widened = hidden.astype(f32)
        return ((dot(two_t_ref[...], back) * (1.0 - widened * widened)).astype(bf16),)

    return second, third


def shifted_sum(sums, at):
    inner_z = z_index(PAD)
    total = None
    for d in (-1, 0, 1):
        part = None
        for b in (-1, 0, 1):
            o = (b + 1) * 3 + d + 1
            moved = shift_y(sums[o * PAD : (o + 1) * PAD, at * CELLS : (at + 1) * CELLS], -b)
            part = moved if part is None else part + moved
        part = shift_z(part, -d, inner_z)
        total = part if total is None else total + part
    return total


def own_kernel(
    coords, beads, tied, outer_ref, own_ref, inner_ref, forward_ref, backward_ref, two_ref, two_t_ref, wide_ref, *refs
):
    sent_ref, sums_ref, features, stage = refs[tied:]
    for place, ref in enumerate((outer_ref, own_ref, inner_ref)):
        stage[place] = ref[...].astype(f32)

    def put(chosen):
        for place in range(3):
            put_features(coords, beads, chosen, stage.at[place], features, place * BLOCK)
        return ()

    def first(chosen):
        return (dot(forward_ref[...], features[:, columns_of(chosen)]),)

    def last(chosen, back):
        sums = dot(backward_ref[BLOCK:], back)
        sums_ref[:, columns_of(chosen)] = sums[:BLOCK]
        return (sums,)

    def store(chosen, sums):
        for at, j in enumerate(chosen):
            rows = pl.ds(j, coords, stride=beads)
            sent_ref[rows, :] = shifted_sum(sums[BLOCK:], at)[:coords]

    run_skewed(groups_of(beads), (put, first, *back_stages(two_ref, two_t_ref, wide_ref), last, store))


def outer_kernel(
    coords, beads, outer2_ref, features_ref, sums_ref, forward_ref, backward_ref, two_ref, two_t_ref, wide_ref,
    kept_ref, features, stage
):
    extra = 2 * BLOCK - DEPTH
    stage[...] = outer2_ref[...].astype(f32)

    def put(chosen):
        put_features(coords, beads, chosen, stage, features, extra)
        features[:extra, columns_of(chosen)] = features_ref[DEPTH : 2 * BLOCK, columns_of(chosen)]
        return ()

    def first(chosen):
        near = dot(forward_ref[:, :DEPTH], features_ref[:DEPTH, columns_of(chosen)])
        return (near + dot(forward_ref[:, DEPTH:], features[:, columns_of(chosen)]),)

    def last(chosen, back):
        return (dot(backward_ref[2 * BLOCK :], back) + sums_ref[:, columns_of(chosen)],)

    def store(chosen, sums):
        for at, j in enumerate(chosen):
            rows = pl.ds(j, coords, stride=beads)
            kept_ref[rows, :] = shifted_sum(sums, at)[:coords]

    run_skewed(groups_of(beads), (put, first, *back_stages(two_ref, two_t_ref, wide_ref), last, store))


def move_kernel(q_base_ref, q_map_ref, kept_ref, came_ref, q_out, rounded_out, sum_out):
    sums = kept_ref[...] + came_ref[...]
    q = q_base_ref[...] - close_dot(q_map_ref[...], sums)
    rounded_out[...] = q.astype(bf16)
    q_out[...] = q
    sum_out[...] = sums


def push_kernel(
    share, planes_at, half_ref, q_ref, sum_ref, p_base_ref, pushed_ref, cosine_ref, finish_ref, modes_ref,
    modes_t_ref, vectors_ref, q_out, p_out, velocity_out, velocity_map_out, planes_out, cells_out, trig_out
):
    depth = modes_ref.shape[1] // 3
    q_out[...] = q_ref[...]
    kick = cosine_ref[...] * close_dot(modes_t_ref[...], half_ref[0:1, :] * sum_ref[...])
    p_out[...] = p_base_ref[...] - close_dot(modes_ref[...], kick)
    velocity_out[...] = (pushed_ref[...] - kick) * finish_ref[:, CELLS:]
    modes_t = modes_t_ref[:, :depth].astype(f32) + modes_t_ref[:, 2 * depth :].astype(f32)
    velocity_map_out[...] = left_terms(finish_ref[:, :1] * modes_t)
    extent_x = len(planes_at)
    whole = extent_x * CELLS
    here = lax.axis_index("space")
    if vectors_ref.shape[1] == share:
        vectors = vectors_ref[...]
    else:
        vectors = vectors_ref[:, pl.ds(pl.multiple_of(here * share, CELLS), share)]
    cell = lax.broadcasted_iota(jnp.int32, (CELLS, share), 0)
    along = vectors[1:2] * ((cell // NZ) * (extent_x * NZ)) + vectors[2:3] * ((cell % NZ) * (extent_x * NY))
    across = jnp.concatenate([vectors[0:1] * ((here ^ at) * CELLS) for at in planes_at])
    for numerator, out in ((across, planes_out), (along, cells_out)):
        angle = TWO_PI * (numerator & (whole - 1)).astype(f32) / whole
        out[0] = jnp.cos(angle)
        out[1] = jnp.sin(angle)
    half = extent_x // 2
    for i in range(half):
        for part in range(2):
            trig_out[part, i * CELLS : (i + 1) * CELLS, :] = plane_trig(planes_out, cells_out, part, half + i)


def finish_kernel(half_ref, velocity_ref, map_ref, kept_ref, came_ref, velocity_out, kick_out):
    sums = kept_ref[...] + came_ref[...]
    velocity_out[...] = (velocity_ref[...] - close_dot(map_ref[...], sums)).astype(bf16)
    kick_out[...] = half_ref[0:1, :] * sums


def projected(velocity_ref, trig):
    count = velocity_ref.shape[0]
    total = 0.0
    for i in range(0, count - 1, 2):
        block = jnp.concatenate([velocity_ref[i], velocity_ref[i + 1]], axis=1)
        total += dot(block, jnp.concatenate([trig(i), trig(i + 1)]))
    return total + dot(velocity_ref[count - 1], trig(count - 1)) if count % 2 else total


def plane_trig(planes_ref, cells_ref, part, i):
    cos_plane, sin_plane = (planes_ref[t, i : i + 1, :] for t in range(2))
    if part == 0:
        return (cos_plane * cells_ref[0] - sin_plane * cells_ref[1]).astype(bf16)
    return (sin_plane * cells_ref[0] + cos_plane * cells_ref[1]).astype(bf16)


def near_project_kernel(own_ref, other_ref, planes_ref, cells_ref, trig_ref, out_ref):
    fields = own_ref.shape[1]
    for part in range(2):
        own = projected(own_ref, functools.partial(plane_trig, planes_ref, cells_ref, part))
        other = projected(other_ref, lambda i: trig_ref[part, i * CELLS : (i + 1) * CELLS, :])
        out_ref[part * fields : (part + 1) * fields, :] = own + other


def project_kernel(scale, first, near_ref, velocity_ref, trig_ref, out_hbm, result, semaphores):
    fields = velocity_ref.shape[1]
    copies = []
    for part in range(2):
        rows = slice(part * fields, (part + 1) * fields)
        last = projected(velocity_ref, lambda i: trig_ref[part, (first + i) * CELLS : (first + i + 1) * CELLS, :])
        result[rows, :] = (near_ref[rows, :] + last) * scale
        copies.append(pltpu.make_async_copy(result.at[rows, :], out_hbm.at[rows, :], semaphores.at[part]))
        copies[-1].start()
    for copy in copies:
        copy.wait()


def mode_blocks(coords, beads):
    j = np.arange(beads)[:, None]
    k = np.arange(beads)[None, :]
    angles = 2.0 * np.pi * ((j * k) % beads) / beads
    edge = np.cos(angles) / math.sqrt(beads)
    inside = np.where(k < beads // 2, np.cos(angles), np.sin(angles)) * math.sqrt(2.0 / beads)
    matrix = np.where((k == 0) | (k == beads // 2), edge, inside).astype(np.float32)
    high = matrix.astype(jnp.bfloat16).astype(np.float32)
    low = (matrix - high).astype(jnp.bfloat16).astype(np.float32)
    blocks = np.concatenate([np.tile(block, (1, coords)) for block in (high, low, high.T, low.T)])
    return np.pad(blocks, ((0, 0), (0, -coords * beads % CELLS)))


def swap(value, distance):
    return lax.ppermute(value, "space", [(i, i ^ distance) for i in range(lax.axis_size("space"))])


def neighbour_planes(plane):
    count = lax.axis_size("space")
    step = [1 if i % 2 else -1 for i in range(count)]
    outer = lax.ppermute(plane, "space", [(i, (i + step[i]) % count) for i in range(count)])
    inner = swap(plane, 1)
    outer2 = lax.ppermute(plane, "space", [(i, (i - 2 * step[i]) % count) for i in range(count)])
    return outer2, outer, inner


def gather_order(count):
    if count % 4:
        return [0, 1]
    far = list(range(4, count, 4))
    return [i ^ j for j in (0, 1) for i in [0] + far + [2] + [d ^ 2 for d in far]]


def gather_planes(velocity):
    count = lax.axis_size("space")
    first, second = [velocity], []
    if count % 4 == 0:
        near = swap(velocity, 2)
        far = [swap(velocity, distance) for distance in range(4, count, 4)]
        first = first + far + [near]
        second = [swap(x, 2) for x in far]
    if not second:
        first, second = first[:-1], first[-1:]
    others = swap(jnp.stack(first), 1) if first else None
    return jnp.stack(first + second), others, swap(jnp.stack(second), 1)


def on_device(
    positions, momenta, masses, step_size, cycle_frequency,
    layer_one, bias_one, layer_two, bias_two, readout, wavevectors
):
    coords, beads, planes, cells = positions.shape
    devices = lax.axis_size("space")
    assert planes == 1 and cells == CELLS and devices & (devices - 1) == 0 and devices > 2
    total = coords * beads
    hidden = layer_one.shape[0]
    width = 27 * PAD
    field, narrow = shape((total, CELLS), f32), shape((total, CELLS), bf16)
    square = shape((total, 3 * (total + -total % CELLS)), bf16)

    share = wavevectors.shape[1] // devices
    if share % CELLS:
        wavevectors = lax.dynamic_slice_in_dim(wavevectors, lax.axis_index("space") * share, share, 1)
    inputs = (
        positions.reshape(total, CELLS), layer_one.T, bias_one.reshape(1, hidden), bias_two.reshape(1, hidden),
        readout.reshape(1, hidden), momenta.reshape(total, CELLS), masses.reshape(1, coords),
        jnp.asarray(mode_blocks(coords, beads)), layer_two,
    )
    rounded, q = call(
        round_kernel, out_shape=(narrow, field), in_specs=[HBM], out_specs=(VMEM,) * 2,
        scratch_shapes=[pltpu.SemaphoreType.DMA((1,))],
        cost_estimate=pl.CostEstimate(flops=10**10, bytes_accessed=10**8, transcendentals=0),
    )(in_hbm(inputs[0]))
    brought = (q, *inputs[1:])
    two = brought[-1]

    (
        forward, outer_forward, backward, two_t, wide, q_base, q_map, p_base, pushed, cosine, finish, half,
        modes, modes_t, wavevectors
    ) = call(
        functools.partial(setup_kernel, coords, beads),
        out_shape=(
            shape((hidden, width), bf16), shape((hidden, width), bf16), shape((width, hidden), bf16),
            shape((hidden, hidden), bf16), shape((2, hidden, CELLS), f32),
            field, square, field, field, field, shape((total, 2 * CELLS), f32), shape((8, CELLS), f32),
            square, square, shape(wavevectors.shape, wavevectors.dtype),
        ),
        in_specs=[SMEM, SMEM, HBM] + [VMEM] * len(brought), out_specs=(VMEM,) * 15,
        scratch_shapes=[pltpu.VMEM((width, hidden), f32), pltpu.SemaphoreType.DMA],
    )(step_size, cycle_frequency, in_hbm(wavevectors), *brought)
    layers = (backward, two, two_t, wide)
    stage = pltpu.VMEM((total, CELLS), f32)

    def forces(plane, *tied):
        outer2, outer, inner = neighbour_planes(plane)
        sent, sums, features = call(
            functools.partial(own_kernel, coords, beads, len(tied)),
            out_shape=(field, shape((BLOCK, beads * CELLS), f32), shape((width, beads * CELLS), bf16)),
            in_specs=[VMEM] * (8 + len(tied)), out_specs=(VMEM,) * 3, scratch_shapes=[pltpu.VMEM((3, total, CELLS), f32)],
        )(outer, plane, inner, forward, *layers, *tied)
        came = swap(sent, 1)
        kept = call(
            functools.partial(outer_kernel, coords, beads),
            out_shape=field, in_specs=[VMEM] * 8, out_specs=VMEM,
            scratch_shapes=[pltpu.VMEM((width - DEPTH, beads * CELLS), bf16), stage],
        )(outer2, features, sums, outer_forward, *layers)
        return kept, came

    q_moved, rounded, sums = call(
        move_kernel, out_shape=(field, narrow, field), in_specs=[VMEM] * 4, out_specs=(VMEM,) * 3,
    )(q_base, q_map, *forces(rounded))
    order = gather_order(devices)
    q_new, p_mid, velocity_base, velocity_map, across, along, trig = call(
        functools.partial(push_kernel, share, order),
        out_shape=(
            field, field, field, square, shape((2, devices, share), f32), shape((2, CELLS, share), f32),
            shape((2, devices // 2 * CELLS, share), bf16),
        ),
        in_specs=[VMEM] * 10, out_specs=(VMEM,) * 7,
    )(half, q_moved, sums, p_base, pushed, cosine, finish, modes, modes_t, wavevectors)
    velocity, kick = call(
        finish_kernel, out_shape=(narrow, field), in_specs=[VMEM] * 5, out_specs=(VMEM,) * 2,
    )(half, velocity_base, velocity_map, *forces(rounded))
    p_new = p_mid - kick
    held, others, last = gather_planes(velocity)
    spectrum = shape((2 * total, share), f32)
    near = call(near_project_kernel, out_shape=spectrum, in_specs=[VMEM] * 5, out_specs=VMEM)(
        held, others, across, along, trig
    )
    spectrum = call(
        functools.partial(project_kernel, 1.0 / math.sqrt(devices * CELLS), others.shape[0]),
        out_shape=spectrum, in_specs=[VMEM] * 3, out_specs=HBM,
        scratch_shapes=[pltpu.VMEM((2 * total, share), f32), pltpu.SemaphoreType.DMA((2,))],
    )(near, last, trig)
    return q_new.reshape(positions.shape), p_new.reshape(momenta.shape), spectrum.T


def solution(mesh):
    field = P(None, None, ("rep", "space"), None)

    return jax.shard_map(
        on_device,
        mesh=mesh,
        in_specs=(field, field) + (P(),) * 9,
        out_specs=(field, field, P(("rep", "space"), None)),
        check_vma=False,
    )
```

```python
import functools
import math

import jax
import jax.numpy as jnp
import numpy as np
from jax import lax
from jax.experimental import pallas as pl
from jax.experimental.pallas import tpu as pltpu
from jax.sharding import PartitionSpec as P


NY = 8
NZ = 16
CELLS = NY * NZ
PAD = 16
BLOCK = 9 * PAD
DEPTH = 256
SIZES = (8,8,)
SKEW = 1
SHIFTS = [(b, d) for b in (-1, 0, 1) for d in (-1, 0, 1)]
TWO_PI = 6.283185307179586
VMEM = pl.BlockSpec(memory_space=pltpu.VMEM)
SMEM = pl.BlockSpec(memory_space=pltpu.SMEM)
HBM = pl.BlockSpec(memory_space=pltpu.MemorySpace.HBM)
shape = jax.ShapeDtypeStruct
f32, bf16 = jnp.float32, jnp.bfloat16

call = functools.partial(pl.pallas_call, compiler_params=pltpu.CompilerParams(vmem_limit_bytes=16 << 20))
dot = functools.partial(jnp.dot, preferred_element_type=jnp.float32)


def split(values):
    high = values.astype(bf16)
    return high, (values - high.astype(f32)).astype(bf16)


def left_terms(values):
    high, low = split(values)
    return jnp.concatenate([high, high, low], axis=1)


def close_dot(left, values):
    high, low = split(values)
    rest = jnp.zeros((left.shape[1] // 3 - values.shape[0], values.shape[1]), bf16)
    return dot(left, jnp.concatenate([high, rest, low, rest, high, rest]))


def in_hbm(value):
    return pltpu.with_memory_space_constraint(value, pltpu.MemorySpace.HBM)


def roll(values, amount):
    amount = amount % CELLS
    return values if amount == 0 else pltpu.roll(values, amount, 1)


def shift_y(values, step):
    return roll(values, -step * NZ)


def shift_z(values, step, inner):
    if step == 0:
        return values
    edge = NZ - 1 if step == 1 else 0
    return jnp.where(inner == edge, roll(values, step * (NZ - 1)), roll(values, -step))


def z_index(rows):
    return lax.broadcasted_iota(jnp.int32, (rows, CELLS), 1) % NZ


def round_kernel(*refs):
    count = (len(refs) - 2) // 2
    sources, rounded_ref, targets, semaphores = refs[:count], refs[count], refs[count + 1 : -1], refs[-1]
    copies = [pltpu.make_async_copy(a, b, semaphores.at[i]) for i, (a, b) in enumerate(zip(sources, targets))]
    for copy in copies:
        copy.start()
    copies[0].wait()
    rounded_ref[...] = targets[0][...].astype(bf16)
    for copy in copies[1:]:
        copy.wait()


def setup_kernel(
    coords, beads, step_ref, cycle_ref, q_ref, one_ref, bias_one_ref, bias_two_ref, readout_ref,
    p_ref, masses_ref, blocks_ref, two_ref,
    forward_ref, outer_forward_ref, backward_ref, two_t_ref, wide_ref,
    q_base_ref, q_map_ref, p_base_ref, pushed_ref, cosine_ref, finish_ref, half_ref,
    modes_ref, modes_t_ref, rows
):
    is_odd = lax.axis_index("space") % 2 == 1
    hidden = one_ref.shape[1]
    rows[: one_ref.shape[0], :] = one_ref[...].astype(f32)
    rows[one_ref.shape[0] :, :] = jnp.zeros((rows.shape[0] - one_ref.shape[0], hidden), f32)
    at = lax.broadcasted_iota(jnp.int32, (PAD, hidden), 0)
    real = at < coords
    rest = bias_one_ref[...]
    turned = []
    for along_x in range(3):
        for o in range(9):
            even, odd = ((a * 9 + o) * coords for a in (along_x, 2 - along_x))
            taken = rows[even : even + PAD, :]
            if odd != even:
                taken = jnp.where(is_odd, rows[odd : odd + PAD, :], taken)
            taken = jnp.where(real, taken, 0.0)
            top = (along_x * 9 + o) * PAD
            backward_ref[top : top + PAD, :] = taken.astype(bf16)
            if along_x == 0 and o < 3:
                term = rest.astype(bf16).astype(f32)
                rest = rest - term
                taken = jnp.where(real, taken, jnp.broadcast_to(term, taken.shape))
                taken = jnp.where(at <= coords, taken, 0.0)
            turned.append(taken)
    forward = jnp.concatenate(turned).T.astype(bf16)
    forward_ref[...] = forward
    outer_forward_ref[...] = jnp.concatenate([forward[:, BLOCK:], forward[:, :BLOCK]], axis=1)
    two_t_ref[...] = two_ref[...].astype(f32).T.astype(bf16)
    columns = jnp.concatenate([bias_two_ref[...], readout_ref[...], jnp.zeros((6, hidden), f32)]).T
    for i in range(2):
        wide_ref[i] = jnp.broadcast_to(columns[:, i : i + 1], (hidden, CELLS))

    depth = blocks_ref.shape[1]
    column = lax.broadcasted_iota(jnp.int32, (beads, depth), 1) // beads
    for matrix_ref, first in ((modes_ref, 0), (modes_t_ref, 2 * beads)):
        high, low = blocks_ref[first : first + beads, :], blocks_ref[first + beads : first + 2 * beads, :]
        for c in range(coords):
            rows_at = slice(c * beads, (c + 1) * beads)
            mine = jnp.where(column == c, high, 0.0).astype(bf16)
            rest = jnp.where(column == c, low, 0.0).astype(bf16)
            matrix_ref[rows_at, :] = jnp.concatenate([mine, mine, rest], axis=1)
    order = lax.broadcasted_iota(jnp.int32, (beads, CELLS), 0).astype(f32)
    mass = jnp.concatenate([jnp.broadcast_to(masses_ref[:, c : c + 1], (beads, CELLS)) for c in range(coords)])
    step = step_ref[0]
    half = 0.5 * step
    frequency = 2.0 * cycle_ref[0] * jnp.sin(order * (0.5 * TWO_PI / beads))
    phase = frequency * step
    sine = jnp.sin(phase)
    ratio = jnp.where(order == 0, 1.0, sine / jnp.where(order == 0, 1.0, phase))
    cosine, drift, spring = (
        jnp.concatenate([term] * coords) for term in (jnp.cos(phase), step * ratio, frequency * sine)
    )
    drift, spring = drift / mass, mass * spring
    mode = close_dot(modes_t_ref[...], jnp.concatenate([q_ref[...], p_ref[...]], axis=1))
    mode_q, mode_p = mode[:, :CELLS], mode[:, CELLS:]
    moved = cosine * mode_q + drift * mode_p
    pushed = cosine * mode_p - spring * mode_q
    base = close_dot(modes_ref[...], jnp.concatenate([moved, pushed], axis=1))
    q_base_ref[...] = base[:, :CELLS]
    p_base_ref[...] = base[:, CELLS:]
    pushed_ref[...] = pushed
    cosine_ref[...] = cosine
    modes_t = modes_t_ref[:, :depth].astype(f32) + modes_t_ref[:, 2 * depth :].astype(f32)
    q_map_ref[...] = left_terms(close_dot(modes_ref[...], (half * drift[:, :1]) * modes_t))
    finish_ref[...] = jnp.concatenate([half / mass, 1.0 / mass], axis=1)
    half_ref[...] = jnp.full(half_ref.shape, half, f32)


def put_features(coords, beads, chosen, stage, features, top):
    filler = jnp.ones((PAD - coords, CELLS), f32)
    inner_z = z_index(PAD)
    for j in chosen:
        plane = jnp.concatenate([stage[pl.ds(j, coords, stride=beads), :], filler]).astype(bf16)
        along = {d: shift_z(plane, d, inner_z) for d in (-1, 0, 1)}
        for o, (b, d) in enumerate(SHIFTS):
            first = top + o * PAD
            features[first : first + PAD, j * CELLS : (j + 1) * CELLS] = shift_y(along[d], b)


def groups_of(beads):
    sizes = SIZES if sum(SIZES) == beads else (beads,)
    starts = np.cumsum((0,) + sizes)
    return [range(int(first), int(first) + size) for first, size in zip(starts, sizes)]


def columns_of(chosen):
    return slice(chosen[0] * CELLS, (chosen[-1] + 1) * CELLS)


def run_skewed(groups, stages):
    state = [() for _ in groups]
    order = sorted((SKEW * g + s, -s, g) for g in range(len(groups)) for s in range(len(stages)))
    for _, s, g in order:
        state[g] = stages[-s](groups[g], *state[g])


def back_stages(two_ref, two_t_ref, wide_ref):
    def second(chosen, first):
        bias, readout = (jnp.concatenate([wide_ref[i]] * len(chosen), axis=1) for i in range(2))
        hidden = jnp.tanh(first).astype(bf16)
        second = jnp.tanh(dot(two_ref[...], hidden) + bias)
        return hidden, (readout * (1.0 - second * second)).astype(bf16)

    def third(chosen, hidden, back):
        widened = hidden.astype(f32)
        return ((dot(two_t_ref[...], back) * (1.0 - widened * widened)).astype(bf16),)

    return second, third


def shifted_sum(sums, at):
    inner_z = z_index(PAD)
    total = None
    for d in (-1, 0, 1):
        part = None
        for b in (-1, 0, 1):
            o = (b + 1) * 3 + d + 1
            moved = shift_y(sums[o * PAD : (o + 1) * PAD, at * CELLS : (at + 1) * CELLS], -b)
            part = moved if part is None else part + moved
        part = shift_z(part, -d, inner_z)
        total = part if total is None else total + part
    return total


def own_kernel(
    coords, beads, tied, outer_ref, own_ref, inner_ref, forward_ref, backward_ref, two_ref, two_t_ref, wide_ref, *refs
):
    sent_ref, sums_ref, features, stage = refs[tied:]
    for place, ref in enumerate((outer_ref, own_ref, inner_ref)):
        stage[place] = ref[...].astype(f32)

    def put(chosen):
        for place in range(3):
            put_features(coords, beads, chosen, stage.at[place], features, place * BLOCK)
        return ()

    def first(chosen):
        return (dot(forward_ref[...], features[:, columns_of(chosen)]),)

    def last(chosen, back):
        sums = dot(backward_ref[BLOCK:], back)
        sums_ref[:, columns_of(chosen)] = sums[:BLOCK]
        return (sums,)

    def store(chosen, sums):
        for at, j in enumerate(chosen):
            rows = pl.ds(j, coords, stride=beads)
            sent_ref[rows, :] = shifted_sum(sums[BLOCK:], at)[:coords]

    run_skewed(groups_of(beads), (put, first, *back_stages(two_ref, two_t_ref, wide_ref), last, store))


def outer_kernel(
    coords, beads, outer2_ref, features_ref, sums_ref, forward_ref, backward_ref, two_ref, two_t_ref, wide_ref,
    kept_ref, features, stage
):
    extra = 2 * BLOCK - DEPTH
    stage[...] = outer2_ref[...].astype(f32)

    def put(chosen):
        put_features(coords, beads, chosen, stage, features, extra)
        features[:extra, columns_of(chosen)] = features_ref[DEPTH : 2 * BLOCK, columns_of(chosen)]
        return ()

    def first(chosen):
        near = dot(forward_ref[:, :DEPTH], features_ref[:DEPTH, columns_of(chosen)])
        return (near + dot(forward_ref[:, DEPTH:], features[:, columns_of(chosen)]),)

    def last(chosen, back):
        return (dot(backward_ref[2 * BLOCK :], back) + sums_ref[:, columns_of(chosen)],)

    def store(chosen, sums):
        for at, j in enumerate(chosen):
            rows = pl.ds(j, coords, stride=beads)
            kept_ref[rows, :] = shifted_sum(sums, at)[:coords]

    run_skewed(groups_of(beads), (put, first, *back_stages(two_ref, two_t_ref, wide_ref), last, store))


def move_kernel(q_base_ref, q_map_ref, kept_ref, came_ref, q_out, rounded_out, sum_out):
    sums = kept_ref[...] + came_ref[...]
    q = q_base_ref[...] - close_dot(q_map_ref[...], sums)
    rounded_out[...] = q.astype(bf16)
    q_out[...] = q
    sum_out[...] = sums


def push_kernel(
    share, planes_at, half_ref, q_ref, sum_ref, p_base_ref, pushed_ref, cosine_ref, finish_ref, modes_ref,
    modes_t_ref, vectors_ref, q_out, p_out, velocity_out, velocity_map_out, planes_out, cells_out, trig_out
):
    depth = modes_ref.shape[1] // 3
    q_out[...] = q_ref[...]
    kick = cosine_ref[...] * close_dot(modes_t_ref[...], half_ref[0:1, :] * sum_ref[...])
    p_out[...] = p_base_ref[...] - close_dot(modes_ref[...], kick)
    velocity_out[...] = (pushed_ref[...] - kick) * finish_ref[:, CELLS:]
    modes_t = modes_t_ref[:, :depth].astype(f32) + modes_t_ref[:, 2 * depth :].astype(f32)
    velocity_map_out[...] = left_terms(finish_ref[:, :1] * modes_t)
    extent_x = len(planes_at)
    whole = extent_x * CELLS
    here = lax.axis_index("space")
    if vectors_ref.shape[1] == share:
        vectors = vectors_ref[...]
    else:
        vectors = vectors_ref[:, pl.ds(pl.multiple_of(here * share, CELLS), share)]
    cell = lax.broadcasted_iota(jnp.int32, (CELLS, share), 0)
    along = vectors[1:2] * ((cell // NZ) * (extent_x * NZ)) + vectors[2:3] * ((cell % NZ) * (extent_x * NY))
    across = jnp.concatenate([vectors[0:1] * ((here ^ at) * CELLS) for at in planes_at])
    for numerator, out in ((across, planes_out), (along, cells_out)):
        angle = TWO_PI * (numerator & (whole - 1)).astype(f32) / whole
        out[0] = jnp.cos(angle)
        out[1] = jnp.sin(angle)
    half = extent_x // 2
    for i in range(half):
        for part in range(2):
            trig_out[part, i * CELLS : (i + 1) * CELLS, :] = plane_trig(planes_out, cells_out, part, half + i)


def finish_kernel(half_ref, velocity_ref, map_ref, kept_ref, came_ref, velocity_out, kick_out):
    sums = kept_ref[...] + came_ref[...]
    velocity_out[...] = (velocity_ref[...] - close_dot(map_ref[...], sums)).astype(bf16)
    kick_out[...] = half_ref[0:1, :] * sums


def projected(velocity_ref, trig):
    count = velocity_ref.shape[0]
    total = 0.0
    for i in range(0, count - 1, 2):
        block = jnp.concatenate([velocity_ref[i], velocity_ref[i + 1]], axis=1)
        total += dot(block, jnp.concatenate([trig(i), trig(i + 1)]))
    return total + dot(velocity_ref[count - 1], trig(count - 1)) if count % 2 else total


def plane_trig(planes_ref, cells_ref, part, i):
    cos_plane, sin_plane = (planes_ref[t, i : i + 1, :] for t in range(2))
    if part == 0:
        return (cos_plane * cells_ref[0] - sin_plane * cells_ref[1]).astype(bf16)
    return (sin_plane * cells_ref[0] + cos_plane * cells_ref[1]).astype(bf16)


def near_project_kernel(own_ref, other_ref, planes_ref, cells_ref, trig_ref, out_ref):
    fields = own_ref.shape[1]
    for part in range(2):
        own = projected(own_ref, functools.partial(plane_trig, planes_ref, cells_ref, part))
        other = projected(other_ref, lambda i: trig_ref[part, i * CELLS : (i + 1) * CELLS, :])
        out_ref[part * fields : (part + 1) * fields, :] = own + other


def project_kernel(scale, first, near_ref, velocity_ref, trig_ref, out_hbm, result, semaphores):
    fields = velocity_ref.shape[1]
    copies = []
    for part in range(2):
        rows = slice(part * fields, (part + 1) * fields)
        last = projected(velocity_ref, lambda i: trig_ref[part, (first + i) * CELLS : (first + i + 1) * CELLS, :])
        result[rows, :] = (near_ref[rows, :] + last) * scale
        copies.append(pltpu.make_async_copy(result.at[rows, :], out_hbm.at[rows, :], semaphores.at[part]))
        copies[-1].start()
    for copy in copies:
        copy.wait()


def mode_blocks(coords, beads):
    j = np.arange(beads)[:, None]
    k = np.arange(beads)[None, :]
    angles = 2.0 * np.pi * ((j * k) % beads) / beads
    edge = np.cos(angles) / math.sqrt(beads)
    inside = np.where(k < beads // 2, np.cos(angles), np.sin(angles)) * math.sqrt(2.0 / beads)
    matrix = np.where((k == 0) | (k == beads // 2), edge, inside).astype(np.float32)
    high = matrix.astype(jnp.bfloat16).astype(np.float32)
    low = (matrix - high).astype(jnp.bfloat16).astype(np.float32)
    blocks = np.concatenate([np.tile(block, (1, coords)) for block in (high, low, high.T, low.T)])
    return np.pad(blocks, ((0, 0), (0, -coords * beads % CELLS)))


def swap(value, distance):
    return lax.ppermute(value, "space", [(i, i ^ distance) for i in range(lax.axis_size("space"))])


def neighbour_planes(plane):
    count = lax.axis_size("space")
    step = [1 if i % 2 else -1 for i in range(count)]
    outer = lax.ppermute(plane, "space", [(i, (i + step[i]) % count) for i in range(count)])
    inner = swap(plane, 1)
    outer2 = lax.ppermute(plane, "space", [(i, (i - 2 * step[i]) % count) for i in range(count)])
    return outer2, outer, inner


def gather_order(count):
    if count % 4:
        return [0, 1]
    far = list(range(4, count, 4))
    return [i ^ j for j in (0, 1) for i in [0] + far + [2] + [d ^ 2 for d in far]]


def gather_planes(velocity):
    count = lax.axis_size("space")
    first, second = [velocity], []
    if count % 4 == 0:
        near = swap(velocity, 2)
        far = [swap(velocity, distance) for distance in range(4, count, 4)]
        first = first + far + [near]
        second = [swap(x, 2) for x in far]
    if not second:
        first, second = first[:-1], first[-1:]
    others = swap(jnp.stack(first), 1) if first else None
    return jnp.stack(first + second), others, swap(jnp.stack(second), 1)


def on_device(
    positions, momenta, masses, step_size, cycle_frequency,
    layer_one, bias_one, layer_two, bias_two, readout, wavevectors
):
    coords, beads, planes, cells = positions.shape
    devices = lax.axis_size("space")
    assert planes == 1 and cells == CELLS and devices & (devices - 1) == 0 and devices > 2
    total = coords * beads
    hidden = layer_one.shape[0]
    width = 27 * PAD
    field, narrow = shape((total, CELLS), f32), shape((total, CELLS), bf16)
    square = shape((total, 3 * (total + -total % CELLS)), bf16)

    share = wavevectors.shape[1] // devices
    if share % CELLS:
        wavevectors = lax.dynamic_slice_in_dim(wavevectors, lax.axis_index("space") * share, share, 1)
    inputs = (
        positions.reshape(total, CELLS), layer_one.T, bias_one.reshape(1, hidden), bias_two.reshape(1, hidden),
        readout.reshape(1, hidden), momenta.reshape(total, CELLS), masses.reshape(1, coords),
        jnp.asarray(mode_blocks(coords, beads)), layer_two,
    )
    rounded, q = call(
        round_kernel, out_shape=(narrow, field), in_specs=[HBM], out_specs=(VMEM,) * 2,
        scratch_shapes=[pltpu.SemaphoreType.DMA((1,))],
        cost_estimate=pl.CostEstimate(flops=10**10, bytes_accessed=10**8, transcendentals=0),
    )(in_hbm(inputs[0]))
    brought = (q, *inputs[1:])
    two = brought[-1]

    (
        forward, outer_forward, backward, two_t, wide, q_base, q_map, p_base, pushed, cosine, finish, half,
        modes, modes_t
    ) = call(
        functools.partial(setup_kernel, coords, beads),
        out_shape=(
            shape((hidden, width), bf16), shape((hidden, width), bf16), shape((width, hidden), bf16),
            shape((hidden, hidden), bf16), shape((2, hidden, CELLS), f32),
            field, square, field, field, field, shape((total, 2 * CELLS), f32), shape((8, CELLS), f32),
            square, square,
        ),
        in_specs=[SMEM, SMEM] + [VMEM] * len(brought), out_specs=(VMEM,) * 14,
        scratch_shapes=[pltpu.VMEM((width, hidden), f32)],
    )(step_size, cycle_frequency, *brought)
    layers = (backward, two, two_t, wide)
    stage = pltpu.VMEM((total, CELLS), f32)

    def forces(plane, *tied):
        outer2, outer, inner = neighbour_planes(plane)
        sent, sums, features = call(
            functools.partial(own_kernel, coords, beads, len(tied)),
            out_shape=(field, shape((BLOCK, beads * CELLS), f32), shape((width, beads * CELLS), bf16)),
            in_specs=[VMEM] * (8 + len(tied)), out_specs=(VMEM,) * 3, scratch_shapes=[pltpu.VMEM((3, total, CELLS), f32)],
        )(outer, plane, inner, forward, *layers, *tied)
        came = swap(sent, 1)
        kept = call(
            functools.partial(outer_kernel, coords, beads),
            out_shape=field, in_specs=[VMEM] * 8, out_specs=VMEM,
            scratch_shapes=[pltpu.VMEM((width - DEPTH, beads * CELLS), bf16), stage],
        )(outer2, features, sums, outer_forward, *layers)
        return kept, came

    q_moved, rounded, sums = call(
        move_kernel, out_shape=(field, narrow, field), in_specs=[VMEM] * 4, out_specs=(VMEM,) * 3,
    )(q_base, q_map, *forces(rounded))
    order = gather_order(devices)
    q_new, p_mid, velocity_base, velocity_map, across, along, trig = call(
        functools.partial(push_kernel, share, order),
        out_shape=(
            field, field, field, square, shape((2, devices, share), f32), shape((2, CELLS, share), f32),
            shape((2, devices // 2 * CELLS, share), bf16),
        ),
        in_specs=[VMEM] * 10, out_specs=(VMEM,) * 7,
    )(half, q_moved, sums, p_base, pushed, cosine, finish, modes, modes_t, wavevectors)
    velocity, kick = call(
        finish_kernel, out_shape=(narrow, field), in_specs=[VMEM] * 5, out_specs=(VMEM,) * 2,
    )(half, velocity_base, velocity_map, *forces(rounded))
    p_new = p_mid - kick
    held, others, last = gather_planes(velocity)
    spectrum = shape((2 * total, share), f32)
    near = call(near_project_kernel, out_shape=spectrum, in_specs=[VMEM] * 5, out_specs=VMEM)(
        held, others, across, along, trig
    )
    spectrum = call(
        functools.partial(project_kernel, 1.0 / math.sqrt(devices * CELLS), others.shape[0]),
        out_shape=spectrum, in_specs=[VMEM] * 3, out_specs=HBM,
        scratch_shapes=[pltpu.VMEM((2 * total, share), f32), pltpu.SemaphoreType.DMA((2,))],
    )(near, last, trig)
    return q_new.reshape(positions.shape), p_new.reshape(momenta.shape), spectrum.T


def solution(mesh):
    field = P(None, None, ("rep", "space"), None)

    return jax.shard_map(
        on_device,
        mesh=mesh,
        in_specs=(field, field) + (P(),) * 9,
        out_specs=(field, field, P(("rep", "space"), None)),
        check_vma=False,
    )
```
